32 devices in a mesh: dp: 16 (over z, x, core), seq: 2 (over y).
Axes of the slice: x: 2, y: 2, z: 4, core: 2. Of those that a mesh axis runs over, the one named last changes fastest.
Arguments:
- dec_input: bfloat16 [64, 128, 768], P('dp', 'seq'), may hold values from -6 to 6
- memory: bfloat16 [64, 256, 768], P('dp', 'seq'), may hold values from -6 to 6
- src_len: int32 [64], P('dp'), may hold values from 128 to 256, as said below
- out_grad: bfloat16 [64, 128, 768], P('dp', 'seq'), may hold values from -6 to 6
- self_qkv: bfloat16 [768, 2304], replicated, may hold values from -0.21875 to 0.21875
- self_out: bfloat16 [768, 768], replicated, may hold values from -1.75 to 1.75
- cross_query: bfloat16 [768, 768], replicated, may hold values from -0.21875 to 0.21875
- cross_kv: bfloat16 [768, 1536], replicated, may hold values from -0.21875 to 0.21875
- cross_out: bfloat16 [768, 768], replicated, may hold values from -3.5 to 3.5
- ffn_in: bfloat16 [768, 3072], replicated, may hold values from -0.21875 to 0.21875
- ffn_out: bfloat16 [3072, 768], replicated, may hold values from -0.109375 to 0.109375
- norm_gain: float32 [3, 768], replicated, may hold values from 0.5 to 1.5
- norm_bias: float32 [3, 768], replicated, may hold values from -3 to 3
Outputs:
- layer_out: bfloat16 [64, 128, 768], P('dp', 'seq')
- input_grad: float32 [64, 128, 768], P('dp', 'seq')
- memory_grad: float32 [64, 256, 768], P('dp', 'seq')
- self_qkv_grad: float32 [768, 2304], P('dp', 'seq')
- self_out_grad: float32 [768, 768], P('dp', 'seq')
- cross_query_grad: float32 [768, 768], P('dp', 'seq')
- cross_kv_grad: float32 [768, 1536], P('dp', 'seq')
- cross_out_grad: float32 [768, 768], P('dp', 'seq')
- ffn_in_grad: float32 [768, 3072], P('dp', 'seq')
- ffn_out_grad: float32 [3072, 768], P('dp', 'seq')
- norm_gain_grad: float32 [3, 768], replicated
- norm_bias_grad: float32 [3, 768], replicated
The draws below stay inside these ranges and needn't reach their ends.
Inputs may be any that keep to these rules, and one draw needn't show every extreme that they name: `src_len`: each source length is 256 or 128; every block of 4 consecutive examples holds at least one of each.
All inputs are finite; a program needn't handle non-finite values.
Results may differ from the reference program's by a relative error of at most 0.023.
Values may be sent and summed in bfloat16 or wider, within the bound.
A program may use at most 192 MiB of HBM per device.

```python
import math
import jax
import jax.numpy as jnp
from jax import lax

D = 768
HEADS = 12
HEAD_DIM = 64
FF = 3072
EX_DEV = 4
BATCH = 64
TGT = 128
MEM = 256


def draw_src_len(key, part):
    blocks = BATCH // EX_DEV
    key_bits, key_full, key_half = jax.random.split(key, 3)
    choose_long = jax.random.randint(key_bits, (blocks, EX_DEV), 0, 2)
    full_slot = jax.random.randint(key_full, (blocks, 1), 0, EX_DEV)
    offset = jax.random.randint(key_half, (blocks, 1), 1, EX_DEV)
    half_slot = (full_slot + offset) % EX_DEV
    slot_index = jnp.arange(EX_DEV)[None, :]
    choose_long = jnp.where(slot_index == full_slot, 1, choose_long)
    choose_long = jnp.where(slot_index == half_slot, 0, choose_long)
    return (MEM // 2 + choose_long * (MEM // 2)).reshape(BATCH).astype(jnp.int32)


def level_of(stream_key, extent, shards, low, largest):
    factor_of, own = 1.0, jax.random.fold_in(stream_key, 6)
    for axis_at, shards_of in shards:
        draws = jnp.exp(jax.random.uniform(jax.random.fold_in(own, axis_at), (shards_of,), jnp.float32, low / len(shards), largest / len(shards)))
        factor_of = factor_of * jnp.repeat(draws, extent[axis_at] // shards_of).reshape([-1 if axis == axis_at else 1 for axis in range(len(extent))])
    return factor_of


def normal_values(key, dims, deviation, reach, cuts=(), held_as=jnp.bfloat16):
    result = deviation * jax.random.normal(key, dims, jnp.float32)
    if cuts:
        result = result * level_of(key, dims, cuts, -0.22, 0.18)
    return jnp.clip(result, -reach, reach).astype(held_as)


def setup_inputs(seed: int = 0) -> dict:
    splits = jax.random.split(jax.random.key(seed), 14)
    return {
        "dec_input": normal_values(splits[0], (BATCH, TGT, D), 1.0, 6.0, ((0, 16), (1, 2))),
        "memory": normal_values(splits[1], (BATCH, MEM, D), 1.0, 6.0, ((0, 16), (1, 2))),
        "src_len": draw_src_len(jax.random.fold_in(splits[13], 71), 0),
        "out_grad": normal_values(splits[3], (BATCH, TGT, D), 1.0, 6.0, ((0, 16), (1, 2))),
        "self_qkv": normal_values(splits[4], (D, 3 * D), D ** -0.5, 0.21875),
        "self_out": normal_values(splits[5], (D, D), (max(D // 64, 1)) ** -0.5, 1.75),
        "cross_query": normal_values(splits[6], (D, D), D ** -0.5, 0.21875),
        "cross_kv": normal_values(splits[7], (D, 2 * D), D ** -0.5, 0.21875),
        "cross_out": normal_values(splits[8], (D, D), (max(D // 256, 1)) ** -0.5, 3.5),
        "ffn_in": normal_values(splits[9], (D, FF), D ** -0.5, 0.21875),
        "ffn_out": normal_values(splits[10], (FF, D), FF ** -0.5, 0.109375),
        "norm_gain": jnp.clip(1.0 + 0.1 * jax.random.normal(splits[11], (3, D), jnp.float32), 0.5, 1.5),
        "norm_bias": normal_values(splits[12], (3, D), 0.5, 3.0, (), jnp.float32),
    }


@jax.custom_vjp
def low(v):
    return lax.optimization_barrier(v.astype(jnp.bfloat16)).astype(jnp.float32)

@jax.custom_vjp
def low_back(v):
    return v

def low_keep(v):
    return (low(v), None)

def low_pass(kept, grad):
    return (grad,)

def back_keep(v):
    return (v, None)

def back_low(kept, grad):
    return (low(grad),)
low.defvjp(low_keep, low_pass)
low_back.defvjp(back_keep, back_low)

def rounded(v):
    return low_back(low(v))

def product(a, b):
    return jnp.matmul(a, b, precision=lax.Precision.HIGHEST)

def layer_norm(x, gain, shift):
    center = lax.optimization_barrier(jnp.mean(x, axis=-1, keepdims=True))
    centered = x - center
    spread = lax.optimization_barrier(jnp.mean(centered * centered, axis=-1, keepdims=True))
    return centered * lax.rsqrt(spread + 1e-05) * gain + shift

def attend(queries, key_values, allowed):
    rows = queries.shape[0]
    count = key_values.shape[0]
    width = queries.shape[1]
    heads_q = queries.reshape(rows, HEADS, HEAD_DIM)
    heads_k = key_values[:, :width].reshape(count, HEADS, HEAD_DIM)
    heads_v = key_values[:, width:].reshape(count, HEADS, HEAD_DIM)
    scores = low_back(jnp.einsum('qhd,khd->hqk', heads_q, heads_k, precision=lax.Precision.HIGHEST))
    logits = jnp.where(allowed[None], scores * (1.0 / math.sqrt(HEAD_DIM)), -1e+30)
    row_top = lax.optimization_barrier(jnp.max(logits, axis=-1, keepdims=True))
    raised = jnp.where(allowed[None], jnp.exp(logits - row_top), 0.0)
    weights = low(raised / lax.optimization_barrier(jnp.sum(raised, axis=-1, keepdims=True)))
    context = jnp.einsum('hqk,khd->qhd', weights, heads_v, precision=lax.Precision.HIGHEST)
    return context.reshape(rows, width)

def layer(x, sources, length, params):
    self_qkv, self_out, cross_query, cross_kv, cross_out, ffn_in, ffn_out, norm_gain, norm_bias = params
    width = x.shape[1]
    first = low(layer_norm(x, norm_gain[0], norm_bias[0]))
    projected = rounded(product(first, self_qkv))
    causal = jnp.arange(TGT)[:, None] >= jnp.arange(TGT)[None, :]
    context = rounded(attend(projected[:, :width], projected[:, width:], causal))
    hidden1 = x + low_back(product(context, self_out))
    second = low(layer_norm(hidden1, norm_gain[1], norm_bias[1]))
    queries = rounded(product(second, cross_query))
    memory_kv = low(product(sources, cross_kv))
    visible = jnp.broadcast_to(jnp.arange(MEM)[None, :] < length, (TGT, MEM))
    crossed = rounded(attend(queries, memory_kv, visible))
    hidden2 = hidden1 + low_back(product(crossed, cross_out))
    third = low(layer_norm(hidden2, norm_gain[2], norm_bias[2]))
    raised_up = low_back(product(third, ffn_in))
    activated = low(jax.nn.gelu(raised_up, approximate=True))
    return hidden2 + low_back(product(activated, ffn_out))

def reference(dec_input, memory, src_len, out_grad, self_qkv, self_out, cross_query, cross_kv, cross_out, ffn_in, ffn_out, norm_gain, norm_bias):
    params = tuple((w.astype(jnp.float32) for w in (self_qkv, self_out, cross_query, cross_kv, cross_out, ffn_in, ffn_out, norm_gain, norm_bias)))

    def step(totals, items):
        tokens, sources, length, cotangent = items

        def forward(a, b, c):
            return layer(a, b, length, c)
        output, pull = jax.vjp(forward, tokens, sources, params)
        grad_tokens, grad_sources, grad_params = pull(cotangent)
        totals = jax.tree.map(lambda s, g: s + g, totals, grad_params)
        return (totals, (output.astype(jnp.bfloat16), grad_tokens, grad_sources))
    zeros = jax.tree.map(jnp.zeros_like, params)
    totals, outputs = lax.scan(step, zeros, (dec_input.astype(jnp.float32), memory.astype(jnp.float32), src_len, out_grad.astype(jnp.float32)))
    layer_out, input_grad, memory_grad = outputs
    return (layer_out, input_grad, memory_grad, totals[0], totals[1], totals[2], totals[3], totals[4], totals[5], totals[6], totals[7], totals[8])
```

```python
import functools
import math

import jax
import jax.numpy as jnp
from jax import lax
from jax.experimental import pallas as pl
from jax.experimental.pallas import tpu as pltpu
from jax.sharding import PartitionSpec as P

MESH = pl.DeviceIdType.MESH
F32 = jnp.float32
BF16 = jnp.bfloat16
TRIPLES = 16
ORDERS = (("x", "l", "y", "h"), ("y", "x", "l", "h"), ("l", "x", "y", "h"))


def place():
    i = lax.axis_index("dp")
    return {"c": i % 2, "x": (i // 2) % 2, "l": (i // 4) % 2, "h": i // 8, "y": lax.axis_index("seq")}


def partner(axis, at):
    i = lax.axis_index("dp")
    y = at["y"]
    if axis == "y":
        return (i, 1 - y)
    step = {"c": 1, "x": 2, "l": 4, "h": 8}[axis]
    return (i + step - 2 * step * at[axis], y)


def greet(at):
    barrier = pltpu.get_barrier_semaphore()
    for axis in ("c", "x", "l", "h", "y"):
        pl.semaphore_signal(barrier, inc=1, device_id=partner(axis, at), device_id_type=MESH)
    pl.semaphore_wait(barrier, 5)


def left_slot(t):
    return jnp.where(t < 4, t, jnp.where(t < 8, 4, jnp.where(t == 8, 5, jnp.where(t < 11, 6, jnp.where(t == 11, 8, jnp.where(t == 12, 9, 10))))))


def store_left(lt, slot, rows_by_feature):
    for i in range(16):
        lt[slot, i % 2, 48 * (i // 2) : 48 * (i // 2) + 48, :] = rows_by_feature[48 * i : 48 * i + 48, :]


class Reducer:
    SCRATCH = [
        pltpu.VMEM((2, 3, 384, 256), BF16),
        pltpu.VMEM((TRIPLES, 3, 384, 256), BF16),
        pltpu.VMEM((2, 3, 2, 2, 2, 2, 48, 128), BF16),
        pltpu.VMEM((TRIPLES, 3, 2, 2, 2, 48, 128), BF16),
        pltpu.VMEM((2, 3, 2, 2, 2, 48, 128), BF16),
        pltpu.VMEM((TRIPLES, 3, 2, 2, 48, 128), BF16),
        pltpu.VMEM((2, 3, 2, 2, 48, 128), BF16),
        pltpu.VMEM((TRIPLES, 3, 2, 48, 128), BF16),
        pltpu.VMEM((2, 3, 2, 48, 128), BF16),
        pltpu.VMEM((TRIPLES, 3, 48, 128), BF16),
        pltpu.SemaphoreType.DMA((5, 2, 3)),
        pltpu.SemaphoreType.DMA((5, TRIPLES, 3)),
    ]

    def __init__(self, at, lt, rg, out, s0, r0, s1, r1, s2, r2, s3, r3, s4, r4, send_sem, recv_sem):
        self.at, self.lt, self.rg, self.out = at, lt, rg, out
        self.sent, self.got = (s0, s1, s2, s3, s4), (r0, r1, r2, r3, r4)
        self.send_sem, self.recv_sem = send_sem, recv_sem

    def axis(self, stage, g):
        return "c" if stage == 0 else ORDERS[g][stage - 1]

    def copy(self, stage, t, g):
        axis = self.axis(stage, g)
        slot = t % 2
        src = self.sent[stage].at[slot, g]
        if stage:
            src = src.at[1 - self.at[axis]]
        return pltpu.make_async_remote_copy(
            src_ref=src,
            dst_ref=self.got[stage].at[t, g],
            send_sem=self.send_sem.at[stage, slot, g],
            recv_sem=self.recv_sem.at[stage, t, g],
            device_id=partner(axis, self.at),
            device_id_type=MESH,
        )

    def free(self, stage, t):
        @pl.when(t >= 2)
        def _():
            for g in range(3):
                self.copy(stage, t - 2, g).wait_send()

    def product(self, t, half, g):
        cols = slice(256 * g, 256 * g + 256)
        slot = left_slot(t)
        return jnp.dot(self.lt[slot, half], self.rg[t, :, cols], preferred_element_type=F32)

    def first(self, t):
        self.free(0, t)
        half = 1 - self.at["c"]
        memory = (t == 9) | (t == 10)
        for g in range(3):
            cols = slice(256 * g, 256 * g + 256)

            @pl.when(jnp.logical_not(memory))
            def _():
                self.sent[0][t % 2, g] = self.product(t, half, g).astype(BF16)

            @pl.when(memory)
            def _():
                more = jnp.dot(self.lt[7, half], self.rg[t + 7, :, cols], preferred_element_type=F32)
                self.sent[0][t % 2, g] = (self.product(t, half, g) + more).astype(BF16)

            self.copy(0, t, g).start()

    def second(self, t):
        self.free(1, t)
        half = self.at["c"]
        memory = (t == 9) | (t == 10)
        for g in range(3):
            cols = slice(256 * g, 256 * g + 256)
            self.copy(0, t, g).wait_recv()

            def spread(total):
                order = ORDERS[g]
                for b in range(8):
                    bits = {"h": b // 4, "l": (b // 2) % 2, "x": b % 2}
                    for y in range(2):
                        bits["y"] = y
                        where = tuple(bits[a] for a in order)
                        self.sent[1][(t % 2, g) + where] = total[48 * b : 48 * b + 48, 128 * y : 128 * y + 128].astype(BF16)

            @pl.when(jnp.logical_not(memory))
            def _():
                spread(self.product(t, half, g) + self.got[0][t, g].astype(F32))

            @pl.when(memory)
            def _():
                more = jnp.dot(self.lt[7, half], self.rg[t + 7, :, cols], preferred_element_type=F32)
                spread(self.product(t, half, g) + more + self.got[0][t, g].astype(F32))

            self.copy(1, t, g).start()

    def onward(self, stage, t):
        if stage < 5:
            self.free(stage, t)
        for g in range(3):
            self.copy(stage - 1, t, g).wait_recv()
            own = self.sent[stage - 1][t % 2, g, self.at[self.axis(stage - 1, g)]]
            total = own.astype(F32) + self.got[stage - 1][t, g].astype(F32)
            if stage < 5:
                self.sent[stage][t % 2, g] = total.astype(BF16)
                self.copy(stage, t, g).start()
            else:
                self.out[t, g] = total

    def tick(self, n):
        for stage in range(6):
            t = n - stage

            @pl.when((t >= 0) & (t < TRIPLES))
            def _():
                if stage == 0:
                    self.first(t)
                elif stage == 1:
                    self.second(t)
                else:
                    self.onward(stage, t)

    def drain(self):
        for stage in range(5):
            for t in (TRIPLES - 2, TRIPLES - 1):
                for g in range(3):
                    self.copy(stage, t, g).wait_send()


NORM_ORDER = ("c", "x", "y", "l", "h")


def norm_copy(j, at, own, got, send_sem, recv_sem):
    return pltpu.make_async_remote_copy(
        src_ref=own.at[j], dst_ref=got.at[j], send_sem=send_sem.at[j], recv_sem=recv_sem.at[j],
        device_id=partner(NORM_ORDER[j], at), device_id_type=MESH,
    )


def norm_step(j, at, own, got, send_sem, recv_sem):
    if j:
        norm_copy(j - 1, at, own, got, send_sem, recv_sem).wait()
        own[j] = own[j - 1] + got[j - 1]
    if j < 5:
        norm_copy(j, at, own, got, send_sem, recv_sem).start()


def reduce_kernel(*refs):
    (active, third, crossed, memory, second, selfed, first,
     g_out, g_up, g_cross, g_kv, g_q, g_self, g_qkv, part, out, norm_out, lt, rg, n_own, n_got, n_send, n_recv, *rest) = refs
    at = place()
    greet(at)
    red = Reducer(at, lt, rg, out, *rest)
    flipped = active[...].T
    for k in range(4):
        for i in range(16):
            lt[k, i % 2, 48 * (i // 2) : 48 * (i // 2) + 48, :] = flipped[192 * i + 48 * k : 192 * i + 48 * k + 48, :]
    store_left(lt, 4, third[...].T)
    store_left(lt, 5, crossed[...].T)
    store_left(lt, 6, memory[0:256, :].T)
    store_left(lt, 7, memory[256:512, :].T)
    store_left(lt, 8, second[...].T)
    store_left(lt, 9, selfed[...].T)
    store_left(lt, 10, first[...].T)

    def right(slot, grads, rows, j):
        half = grads.shape[1] // 2
        for g in range(3):
            for h in range(2):
                rg[slot, :, 256 * g + 128 * h : 256 * g + 128 * h + 128] = grads[rows, h * half + j * 384 + g * 128 : h * half + j * 384 + g * 128 + 128]

    every = slice(0, 256)
    for k in range(4):
        right(k, g_out, every, 0)
        right(4 + k, g_up, every, k)
    right(8, g_cross, every, 0)
    for j in range(2):
        right(9 + j, g_kv, every, j)
        right(16 + j, g_kv, slice(256, 512), j)
    right(11, g_q, every, 0)
    right(12, g_self, every, 0)
    for j in range(3):
        right(13 + j, g_qkv, every, j)
    n_own[0] = part[...]

    def body(n, carry):
        red.tick(n)
        for j in range(6):
            @pl.when(n == 2 * j)
            def _():
                norm_step(j, at, n_own, n_got, n_send, n_recv)
        return carry

    lax.fori_loop(0, TRIPLES + 5, body, 0)
    norm_out[...] = n_own[5]
    red.drain()


def reduce_call(lefts, rights, part):
    vmem = pl.BlockSpec(memory_space=pltpu.VMEM)
    return pl.pallas_call(
        reduce_kernel,
        out_shape=(jax.ShapeDtypeStruct((TRIPLES, 3, 48, 128), F32), jax.ShapeDtypeStruct((8, 768), F32)),
        in_specs=[vmem] * 15,
        out_specs=(vmem, vmem),
        scratch_shapes=[
            pltpu.VMEM((11, 2, 384, 256), BF16),
            pltpu.VMEM((18, 256, 768), BF16),
            pltpu.VMEM((6, 8, 768), F32),
            pltpu.VMEM((5, 8, 768), F32),
            pltpu.SemaphoreType.DMA((5,)),
            pltpu.SemaphoreType.DMA((5,)),
        ] + Reducer.SCRATCH,
        compiler_params=pltpu.CompilerParams(collective_id=0, has_side_effects=True, vmem_limit_bytes=60 << 20),
    )(*lefts, *rights, part)


def assemble(units, first, count):
    block = units[first : first + count]
    return jnp.transpose(block, (2, 0, 1, 3)).reshape(48, count * 384)


def gather_outputs(units):
    ffn_out = jnp.transpose(units[0:4], (0, 2, 1, 3)).reshape(192, 384)
    return dict(ffn_out=ffn_out, ffn_in=assemble(units, 4, 4), cross_out=assemble(units, 8, 1), cross_kv=assemble(units, 9, 2),
                cross_query=assemble(units, 11, 1), self_out=assemble(units, 12, 1), self_qkv=assemble(units, 13, 3))

HEADS = 12
HEAD_DIM = 64


def layer_norm(x, gain, shift):
    center = jnp.mean(x, axis=-1, keepdims=True)
    centered = x - center
    spread = jnp.mean(centered * centered, axis=-1, keepdims=True)
    return centered * lax.rsqrt(spread + 1e-05) * gain + shift


def smooth(v):
    return jax.nn.gelu(v, approximate=True)


def project(rows, weight):
    return jnp.einsum("etd,df->etf", rows, weight, preferred_element_type=jnp.float32)


def project_back(grads, weight):
    return jnp.einsum("etf,df->etd", grads, weight, preferred_element_type=jnp.float32)


def outer(rows, grads):
    return jnp.einsum("etd,etf->df", rows, grads, preferred_element_type=jnp.float32)


def outer_full(rows, grads):
    return jnp.einsum(
        "etd,etf->df", rows.astype(jnp.float32), grads, precision=lax.Precision.HIGHEST
    )


def back_full(grads, weight):
    return jnp.einsum(
        "etf,df->etd", grads, weight.astype(jnp.float32), precision=lax.Precision.HIGHEST
    )


def split_heads(queries, key_values):
    examples, rows, width = queries.shape
    count = key_values.shape[1]
    heads_q = queries.reshape(examples, rows, HEADS, HEAD_DIM)
    heads_k = key_values[:, :, :width].reshape(examples, count, HEADS, HEAD_DIM)
    heads_v = key_values[:, :, width:].reshape(examples, count, HEADS, HEAD_DIM)
    return (heads_q, heads_k, heads_v)


def masked_logits(heads_q, heads_k, allowed):
    scores = jnp.einsum("eqhd,ekhd->ehqk", heads_q, heads_k, preferred_element_type=jnp.float32)
    return jnp.where(allowed, scores * (1.0 / math.sqrt(HEAD_DIM)), -1e30)


def attend_forward(queries, key_values, allowed):
    examples, rows, width = queries.shape
    heads_q, heads_k, heads_v = split_heads(queries, key_values)
    logits = masked_logits(heads_q, heads_k, allowed)
    row_top = jnp.max(logits, axis=-1, keepdims=True)
    raised = jnp.where(allowed, jnp.exp(logits - row_top), 0.0)
    row_total = jnp.sum(raised, axis=-1, keepdims=True)
    weights = (raised / row_total).astype(jnp.bfloat16)
    context = jnp.einsum("ehqk,ekhd->eqhd", weights, heads_v, preferred_element_type=jnp.float32)
    return (
        context.reshape(examples, rows, width).astype(jnp.bfloat16),
        row_top + jnp.log(row_total),
    )


def attend_backward(queries, key_values, allowed, log_total, grad_context):
    examples, rows, width = queries.shape
    count = key_values.shape[1]
    heads_q, heads_k, heads_v = split_heads(queries, key_values)
    logits = masked_logits(heads_q, heads_k, allowed)
    soft = jnp.where(allowed, jnp.exp(logits - log_total), 0.0)
    grad_heads = grad_context.reshape(examples, rows, HEADS, HEAD_DIM)
    grad_soft = jnp.einsum(
        "eqhd,ekhd->ehqk", grad_heads, heads_v, preferred_element_type=jnp.float32
    )
    grad_values = jnp.einsum(
        "ehqk,eqhd->ekhd", soft.astype(jnp.bfloat16), grad_heads, preferred_element_type=jnp.float32
    )
    inner = jnp.sum(soft * grad_soft, axis=-1, keepdims=True)
    grad_scores = (soft * (grad_soft - inner) * (1.0 / math.sqrt(HEAD_DIM))).astype(jnp.bfloat16)
    grad_queries = jnp.einsum(
        "ehqk,ekhd->eqhd", grad_scores, heads_k, preferred_element_type=jnp.float32
    )
    grad_keys = jnp.einsum(
        "ehqk,eqhd->ekhd", grad_scores, heads_q, preferred_element_type=jnp.float32
    )
    joined = jnp.concatenate(
        [grad_keys.reshape(examples, count, width), grad_values.reshape(examples, count, width)],
        axis=2,
    )
    return (grad_queries.reshape(examples, rows, width), joined)


def per_device_wide(
    dec_input,
    memory,
    src_len,
    out_grad,
    self_qkv,
    self_out,
    cross_query,
    cross_kv,
    cross_out,
    ffn_in,
    ffn_out,
    norm_gain,
    norm_bias,
):
    examples, local_rows, width = dec_input.shape
    local_sources = memory.shape[1]
    seq_count = lax.axis_size("seq")
    all_targets = local_rows * seq_count
    all_sources = local_sources * seq_count
    rank = lax.axis_index("seq")
    x = dec_input.astype(jnp.float32)
    first_f, pull_first = jax.vjp(layer_norm, x, norm_gain[0], norm_bias[0])
    first = first_f.astype(jnp.bfloat16)
    projected = project(first, self_qkv).astype(jnp.bfloat16)
    self_queries = projected[:, :, :width]
    self_kv = lax.all_gather(projected[:, :, width:], "seq", axis=1, tiled=True)
    query_place = rank * local_rows + jnp.arange(local_rows, dtype=jnp.int32)
    key_place = jnp.arange(all_targets, dtype=jnp.int32)
    causal = (query_place[:, None] >= key_place[None, :])[None, None]
    self_context, self_total = attend_forward(self_queries, self_kv, causal)
    hidden1 = x + project(self_context, self_out)
    second_f, pull_second = jax.vjp(layer_norm, hidden1, norm_gain[1], norm_bias[1])
    second = second_f.astype(jnp.bfloat16)
    cross_queries = project(second, cross_query).astype(jnp.bfloat16)
    gathered = lax.all_gather(memory, "seq", axis=1, tiled=True)
    memory_kv = project(gathered, cross_kv).astype(jnp.bfloat16)
    source_place = jnp.arange(all_sources, dtype=jnp.int32)
    visible = (source_place[None, :] < src_len[:, None])[:, None, None, :]
    cross_context, cross_total = attend_forward(cross_queries, memory_kv, visible)
    hidden2 = hidden1 + project(cross_context, cross_out)
    third_f, pull_third = jax.vjp(layer_norm, hidden2, norm_gain[2], norm_bias[2])
    third = third_f.astype(jnp.bfloat16)
    raised_up = project(third, ffn_in)
    active_f, pull_smooth = jax.vjp(smooth, raised_up)
    activated = active_f.astype(jnp.bfloat16)
    layer_out = (hidden2 + project(activated, ffn_out)).astype(jnp.bfloat16)
    grad_out = out_grad.astype(jnp.float32)
    ffn_out_grad = outer(activated, out_grad)
    (grad_up,) = pull_smooth(project_back(out_grad, ffn_out))
    grad_up_low = grad_up.astype(jnp.bfloat16)
    ffn_in_grad = outer(third, grad_up_low)
    back_third, gain_third, bias_third = pull_third(project_back(grad_up_low, ffn_in))
    grad_hidden2 = grad_out + back_third
    cross_branch = grad_hidden2.astype(jnp.bfloat16)
    cross_out_grad = outer(cross_context, cross_branch)
    grad_cross_context = project_back(cross_branch, cross_out).astype(jnp.bfloat16)
    grad_cross_q, grad_memory_kv = attend_backward(
        cross_queries, memory_kv, visible, cross_total, grad_cross_context
    )
    local_kv_grad = lax.psum_scatter(
        grad_memory_kv.astype(jnp.bfloat16), "seq", scatter_dimension=1, tiled=True
    ).astype(jnp.float32)
    cross_kv_grad = outer_full(memory, local_kv_grad)
    memory_grad = back_full(local_kv_grad, cross_kv)
    grad_cross_low = grad_cross_q.astype(jnp.bfloat16)
    cross_query_grad = outer(second, grad_cross_low)
    back_second, gain_second, bias_second = pull_second(project_back(grad_cross_low, cross_query))
    grad_hidden1 = grad_hidden2 + back_second
    self_branch = grad_hidden1.astype(jnp.bfloat16)
    self_out_grad = outer(self_context, self_branch)
    grad_self_context = project_back(self_branch, self_out).astype(jnp.bfloat16)
    grad_self_q, grad_self_kv = attend_backward(
        self_queries, self_kv, causal, self_total, grad_self_context
    )
    local_self_kv = lax.psum_scatter(grad_self_kv, "seq", scatter_dimension=1, tiled=True)
    grad_projected = jnp.concatenate([grad_self_q, local_self_kv], axis=2).astype(jnp.bfloat16)
    self_qkv_grad = outer(first, grad_projected)
    back_first, gain_first, bias_first = pull_first(project_back(grad_projected, self_qkv))
    input_grad = grad_hidden1 + back_first
    gain_terms = jnp.stack([gain_first, gain_second, gain_third])
    bias_terms = jnp.stack([bias_first, bias_second, bias_third])
    gain_total, bias_total = lax.psum((gain_terms, bias_terms), ("dp", "seq"))
    partial_value = (
        lax.psum_scatter(
            self_qkv_grad.astype(jnp.bfloat16), "dp", scatter_dimension=0, tiled=True
        ).astype(jnp.float32),
        lax.psum_scatter(
            self_out_grad.astype(jnp.bfloat16), "dp", scatter_dimension=0, tiled=True
        ).astype(jnp.float32),
        lax.psum_scatter(
            cross_query_grad.astype(jnp.bfloat16), "dp", scatter_dimension=0, tiled=True
        ).astype(jnp.float32),
        lax.psum_scatter(
            cross_kv_grad.astype(jnp.bfloat16), "dp", scatter_dimension=0, tiled=True
        ).astype(jnp.float32),
        lax.psum_scatter(
            cross_out_grad.astype(jnp.bfloat16), "dp", scatter_dimension=0, tiled=True
        ).astype(jnp.float32),
        lax.psum_scatter(
            ffn_in_grad.astype(jnp.bfloat16), "dp", scatter_dimension=0, tiled=True
        ).astype(jnp.float32),
        lax.psum_scatter(
            ffn_out_grad.astype(jnp.bfloat16), "dp", scatter_dimension=0, tiled=True
        ).astype(jnp.float32),
    )
    finished = (
        lax.psum_scatter(
            partial_value[0].astype(jnp.bfloat16), "seq", scatter_dimension=1, tiled=True
        ).astype(jnp.float32),
        lax.psum_scatter(
            partial_value[1].astype(jnp.bfloat16), "seq", scatter_dimension=1, tiled=True
        ).astype(jnp.float32),
        lax.psum_scatter(
            partial_value[2].astype(jnp.bfloat16), "seq", scatter_dimension=1, tiled=True
        ).astype(jnp.float32),
        lax.psum_scatter(
            partial_value[3].astype(jnp.bfloat16), "seq", scatter_dimension=1, tiled=True
        ).astype(jnp.float32),
        lax.psum_scatter(
            partial_value[4].astype(jnp.bfloat16), "seq", scatter_dimension=1, tiled=True
        ).astype(jnp.float32),
        lax.psum_scatter(
            partial_value[5].astype(jnp.bfloat16), "seq", scatter_dimension=1, tiled=True
        ).astype(jnp.float32),
        lax.psum_scatter(
            partial_value[6].astype(jnp.bfloat16), "seq", scatter_dimension=1, tiled=True
        ).astype(jnp.float32),
    )
    return (
        layer_out,
        input_grad,
        memory_grad,
        finished[0],
        finished[1],
        finished[2],
        finished[3],
        finished[4],
        finished[5],
        finished[6],
        gain_total,
        bias_total,
    )


def swap_in(v, y, half):
    mine = lax.dynamic_slice_in_dim(v, y * half, half, 0)
    theirs = lax.dynamic_slice_in_dim(v, (1 - y) * half, half, 0)
    other = lax.ppermute(theirs, "seq", [(0, 1), (1, 0)])
    low = jnp.where(y == 0, mine, other)
    high = jnp.where(y == 0, other, mine)
    return jnp.concatenate([low, high], axis=1)


def swap_out(v, y, rows):
    mine = lax.dynamic_slice_in_dim(v, y * rows, rows, 1)
    theirs = lax.dynamic_slice_in_dim(v, (1 - y) * rows, rows, 1)
    other = lax.ppermute(theirs, "seq", [(0, 1), (1, 0)])
    low = jnp.where(y == 0, mine, other)
    high = jnp.where(y == 0, other, mine)
    return jnp.concatenate([low, high], axis=0)


def per_device_paired(
    dec_input,
    memory,
    src_len,
    out_grad,
    self_qkv,
    self_out,
    cross_query,
    cross_kv,
    cross_out,
    ffn_in,
    ffn_out,
    norm_gain,
    norm_bias,
):
    examples, local_rows, width = dec_input.shape
    local_sources = memory.shape[1]
    half = examples // 2
    y = lax.axis_index("seq")
    dec_input = swap_in(dec_input, y, half)
    memory = swap_in(memory, y, half)
    out_grad = swap_in(out_grad, y, half)
    src_len = lax.dynamic_slice_in_dim(src_len, y * half, half, 0)
    all_targets, all_sources = 2 * local_rows, 2 * local_sources
    x = dec_input.astype(jnp.float32)
    first_f, pull_first = jax.vjp(layer_norm, x, norm_gain[0], norm_bias[0])
    first = first_f.astype(jnp.bfloat16)
    projected = project(first, self_qkv).astype(jnp.bfloat16)
    self_queries = projected[:, :, :width]
    self_kv = projected[:, :, width:]
    key_place = jnp.arange(all_targets, dtype=jnp.int32)
    causal = (key_place[:, None] >= key_place[None, :])[None, None]
    self_context, self_total = attend_forward(self_queries, self_kv, causal)
    hidden1 = x + project(self_context, self_out)
    second_f, pull_second = jax.vjp(layer_norm, hidden1, norm_gain[1], norm_bias[1])
    second = second_f.astype(jnp.bfloat16)
    cross_queries = project(second, cross_query).astype(jnp.bfloat16)
    memory_kv = project(memory, cross_kv).astype(jnp.bfloat16)
    source_place = jnp.arange(all_sources, dtype=jnp.int32)
    visible = (source_place[None, :] < src_len[:, None])[:, None, None, :]
    cross_context, cross_total = attend_forward(cross_queries, memory_kv, visible)
    hidden2 = hidden1 + project(cross_context, cross_out)
    third_f, pull_third = jax.vjp(layer_norm, hidden2, norm_gain[2], norm_bias[2])
    third = third_f.astype(jnp.bfloat16)
    raised_up = project(third, ffn_in)
    active_f, pull_smooth = jax.vjp(smooth, raised_up)
    activated = active_f.astype(jnp.bfloat16)
    layer_out = (hidden2 + project(activated, ffn_out)).astype(jnp.bfloat16)
    grad_out = out_grad.astype(jnp.float32)
    (grad_up,) = pull_smooth(project_back(out_grad, ffn_out))
    grad_up_low = grad_up.astype(jnp.bfloat16)
    back_third, gain_third, bias_third = pull_third(project_back(grad_up_low, ffn_in))
    grad_hidden2 = grad_out + back_third
    cross_branch = grad_hidden2.astype(jnp.bfloat16)
    grad_cross_context = project_back(cross_branch, cross_out).astype(jnp.bfloat16)
    grad_cross_q, grad_memory_kv = attend_backward(
        cross_queries, memory_kv, visible, cross_total, grad_cross_context
    )
    grad_kv_low = grad_memory_kv.astype(jnp.bfloat16)
    memory_grad = project_back(grad_kv_low, cross_kv).astype(jnp.bfloat16)
    grad_cross_low = grad_cross_q.astype(jnp.bfloat16)
    back_second, gain_second, bias_second = pull_second(project_back(grad_cross_low, cross_query))
    grad_hidden1 = grad_hidden2 + back_second
    self_branch = grad_hidden1.astype(jnp.bfloat16)
    grad_self_context = project_back(self_branch, self_out).astype(jnp.bfloat16)
    grad_self_q, grad_self_kv = attend_backward(
        self_queries, self_kv, causal, self_total, grad_self_context
    )
    grad_projected = jnp.concatenate([grad_self_q, grad_self_kv], axis=2).astype(jnp.bfloat16)
    back_first, gain_first, bias_first = pull_first(project_back(grad_projected, self_qkv))
    input_grad = grad_hidden1 + back_first
    zero = jnp.zeros_like(gain_first)
    part = jnp.stack([gain_first, gain_second, gain_third, bias_first, bias_second, bias_third, zero, zero])
    flat = lambda v: v.reshape(-1, v.shape[-1])
    lefts = [flat(v) for v in (activated, third, cross_context, memory, second, self_context, first)]
    rights = [flat(v) for v in (out_grad, grad_up_low, cross_branch, grad_kv_low, grad_cross_low, self_branch, grad_projected)]
    units, norms = reduce_call(lefts, rights, part)
    grads = gather_outputs(units)
    return (
        swap_out(layer_out, y, local_rows),
        swap_out(input_grad.astype(jnp.bfloat16), y, local_rows).astype(jnp.float32),
        swap_out(memory_grad, y, local_sources).astype(jnp.float32),
        grads["self_qkv"],
        grads["self_out"],
        grads["cross_query"],
        grads["cross_kv"],
        grads["cross_out"],
        grads["ffn_in"],
        grads["ffn_out"],
        norms[0:3],
        norms[3:6],
    )


def solution(mesh):
    paired = mesh.shape["dp"] == 16 and mesh.shape["seq"] == 2
    per_device = per_device_paired if paired else per_device_wide
    in_specs = (
        P("dp", "seq", None),
        P("dp", "seq", None),
        P("dp"),
        P("dp", "seq", None),
        P(),
        P(),
        P(),
        P(),
        P(),
        P(),
        P(),
        P(),
        P(),
    )
    out_specs = (
        P("dp", "seq", None),
        P("dp", "seq", None),
        P("dp", "seq", None),
        P("dp", "seq"),
        P("dp", "seq"),
        P("dp", "seq"),
        P("dp", "seq"),
        P("dp", "seq"),
        P("dp", "seq"),
        P("dp", "seq"),
        P(),
        P(),
    )
    return jax.shard_map(
        per_device, mesh=mesh, in_specs=in_specs, out_specs=out_specs, check_vma=False
    )
```

```python
import functools
import math

import jax
import jax.numpy as jnp
from jax import lax
from jax.experimental import pallas as pl
from jax.experimental.pallas import tpu as pltpu
from jax.sharding import PartitionSpec as P

HEADS = 12
HEAD_DIM = 64
MESH = pl.DeviceIdType.MESH
F32 = jnp.float32
BF16 = jnp.bfloat16
TRIPLES = 16
ORDERS = (("x", "l", "y", "h"), ("y", "x", "l", "h"), ("l", "x", "y", "h"))


def place():
    i = lax.axis_index("dp")
    return {"c": i % 2, "x": (i // 2) % 2, "l": (i // 4) % 2, "h": i // 8, "y": lax.axis_index("seq")}


def partner(axis, at):
    i = lax.axis_index("dp")
    y = at["y"]
    if axis == "y":
        return (i, 1 - y)
    step = {"c": 1, "x": 2, "l": 4, "h": 8}[axis]
    return (i + step - 2 * step * at[axis], y)


def greet(at):
    barrier = pltpu.get_barrier_semaphore()
    for axis in ("c", "x", "l", "h", "y"):
        pl.semaphore_signal(barrier, inc=1, device_id=partner(axis, at), device_id_type=MESH)
    pl.semaphore_wait(barrier, 5)


def left_slot(t):
    return jnp.where(t < 4, t, jnp.where(t < 8, 4, jnp.where(t == 8, 5, jnp.where(t < 11, 6, jnp.where(t == 11, 8, jnp.where(t == 12, 9, 10))))))


def store_left(lt, slot, rows_by_feature):
    for i in range(16):
        lt[slot, i % 2, 48 * (i // 2) : 48 * (i // 2) + 48, :] = rows_by_feature[48 * i : 48 * i + 48, :]


class Reducer:
    SCRATCH = [
        pltpu.VMEM((2, 3, 384, 256), BF16),
        pltpu.VMEM((TRIPLES, 3, 384, 256), BF16),
        pltpu.VMEM((2, 3, 2, 2, 2, 2, 48, 128), BF16),
        pltpu.VMEM((TRIPLES, 3, 2, 2, 2, 48, 128), BF16),
        pltpu.VMEM((2, 3, 2, 2, 2, 48, 128), BF16),
        pltpu.VMEM((TRIPLES, 3, 2, 2, 48, 128), BF16),
        pltpu.VMEM((2, 3, 2, 2, 48, 128), BF16),
        pltpu.VMEM((TRIPLES, 3, 2, 48, 128), BF16),
        pltpu.VMEM((2, 3, 2, 48, 128), BF16),
        pltpu.VMEM((TRIPLES, 3, 48, 128), BF16),
        pltpu.SemaphoreType.DMA((5, 2, 3)),
        pltpu.SemaphoreType.DMA((5, TRIPLES, 3)),
    ]

    def __init__(self, at, lt, rg, out, s0, r0, s1, r1, s2, r2, s3, r3, s4, r4, send_sem, recv_sem):
        self.at, self.lt, self.rg, self.out = at, lt, rg, out
        self.sent, self.got = (s0, s1, s2, s3, s4), (r0, r1, r2, r3, r4)
        self.send_sem, self.recv_sem = send_sem, recv_sem

    def axis(self, stage, g):
        return "c" if stage == 0 else ORDERS[g][stage - 1]

    def copy(self, stage, t, g):
        axis = self.axis(stage, g)
        slot = t % 2
        src = self.sent[stage].at[slot, g]
        if stage:
            src = src.at[1 - self.at[axis]]
        return pltpu.make_async_remote_copy(
            src_ref=src,
            dst_ref=self.got[stage].at[t, g],
            send_sem=self.send_sem.at[stage, slot, g],
            recv_sem=self.recv_sem.at[stage, t, g],
            device_id=partner(axis, self.at),
            device_id_type=MESH,
        )

    def free(self, stage, t):
        @pl.when(t >= 2)
        def _():
            for g in range(3):
                self.copy(stage, t - 2, g).wait_send()

    def product(self, t, half, g):
        cols = slice(256 * g, 256 * g + 256)
        slot = left_slot(t)
        return jnp.dot(self.lt[slot, half], self.rg[t, :, cols], preferred_element_type=F32)

    def first(self, t):
        self.free(0, t)
        half = 1 - self.at["c"]
        memory = (t == 9) | (t == 10)
        for g in range(3):
            cols = slice(256 * g, 256 * g + 256)

            @pl.when(jnp.logical_not(memory))
            def _():
                self.sent[0][t % 2, g] = self.product(t, half, g).astype(BF16)

            @pl.when(memory)
            def _():
                more = jnp.dot(self.lt[7, half], self.rg[t + 7, :, cols], preferred_element_type=F32)
                self.sent[0][t % 2, g] = (self.product(t, half, g) + more).astype(BF16)

            self.copy(0, t, g).start()

    def second(self, t):
        self.free(1, t)
        half = self.at["c"]
        memory = (t == 9) | (t == 10)
        for g in range(3):
            cols = slice(256 * g, 256 * g + 256)
            self.copy(0, t, g).wait_recv()

            def spread(total):
                order = ORDERS[g]
                for b in range(8):
                    bits = {"h": b // 4, "l": (b // 2) % 2, "x": b % 2}
                    for y in range(2):
                        bits["y"] = y
                        where = tuple(bits[a] for a in order)
                        self.sent[1][(t % 2, g) + where] = total[48 * b : 48 * b + 48, 128 * y : 128 * y + 128].astype(BF16)

            @pl.when(jnp.logical_not(memory))
            def _():
                spread(self.product(t, half, g) + self.got[0][t, g].astype(F32))

            @pl.when(memory)
            def _():
                more = jnp.dot(self.lt[7, half], self.rg[t + 7, :, cols], preferred_element_type=F32)
                spread(self.product(t, half, g) + more + self.got[0][t, g].astype(F32))

            self.copy(1, t, g).start()

    def onward(self, stage, t):
        if stage < 5:
            self.free(stage, t)
        for g in range(3):
            self.copy(stage - 1, t, g).wait_recv()
            own = self.sent[stage - 1][t % 2, g, self.at[self.axis(stage - 1, g)]]
            total = own.astype(F32) + self.got[stage - 1][t, g].astype(F32)
            if stage < 5:
                self.sent[stage][t % 2, g] = total.astype(BF16)
                self.copy(stage, t, g).start()
            else:
                self.out[t, g] = total

    def tick(self, n):
        for stage in range(6):
            t = n - stage

            @pl.when((t >= 0) & (t < TRIPLES))
            def _():
                if stage == 0:
                    self.first(t)
                elif stage == 1:
                    self.second(t)
                else:
                    self.onward(stage, t)

    def drain(self):
        for stage in range(5):
            for t in (TRIPLES - 2, TRIPLES - 1):
                for g in range(3):
                    self.copy(stage, t, g).wait_send()


NORM_ORDER = ("c", "x", "y", "l", "h")


def norm_copy(j, at, own, got, send_sem, recv_sem):
    return pltpu.make_async_remote_copy(
        src_ref=own.at[j], dst_ref=got.at[j], send_sem=send_sem.at[j], recv_sem=recv_sem.at[j],
        device_id=partner(NORM_ORDER[j], at), device_id_type=MESH,
    )


def norm_step(j, at, own, got, send_sem, recv_sem):
    if j:
        norm_copy(j - 1, at, own, got, send_sem, recv_sem).wait()
        own[j] = own[j - 1] + got[j - 1]
    if j < 5:
        norm_copy(j, at, own, got, send_sem, recv_sem).start()


def assemble(units, first, count):
    block = units[first : first + count]
    return jnp.transpose(block, (2, 0, 1, 3)).reshape(48, count * 384)


def gather_outputs(units):
    ffn_out = jnp.transpose(units[0:4], (0, 2, 1, 3)).reshape(192, 384)
    return dict(ffn_out=ffn_out, ffn_in=assemble(units, 4, 4), cross_out=assemble(units, 8, 1), cross_kv=assemble(units, 9, 2),
                cross_query=assemble(units, 11, 1), self_out=assemble(units, 12, 1), self_qkv=assemble(units, 13, 3))


LANES = 128


def normed(v):
    center = jnp.mean(v, axis=-1, keepdims=True)
    centered = v - center
    spread = jnp.mean(centered * centered, axis=-1, keepdims=True)
    scale = lax.rsqrt(spread + 1e-05)
    return centered * scale, scale


def row_blocks(step, body):
    def run(b, carry):
        body(pl.ds(pl.multiple_of(b * step, step), step))
        return carry

    lax.fori_loop(0, 256 // step, run, 0)


def norm_forward(load, out, norm_gain, norm_bias, k):
    def body(rows):
        hat, _ = normed(load(rows))
        out[rows, :] = (hat * norm_gain[k : k + 1, :] + norm_bias[k : k + 1, :]).astype(BF16)

    row_blocks(64, body)


def norm_backward(load, load_grad, store, norm_gain, sums, k):
    def body(rows):
        hat, scale = normed(load(rows))
        dy = load_grad(rows)
        sums[k : k + 1, :] += jnp.sum(dy * hat, axis=0, keepdims=True)
        sums[k + 3 : k + 4, :] += jnp.sum(dy, axis=0, keepdims=True)
        dhat = dy * norm_gain[k : k + 1, :]
        mean = jnp.mean(dhat, axis=-1, keepdims=True)
        along = jnp.mean(dhat * hat, axis=-1, keepdims=True)
        store(rows, scale * (dhat - mean - hat * along))

    row_blocks(64, body)


def two_heads(tile):
    first = lax.broadcasted_iota(jnp.int32, tile.shape, 1) < HEAD_DIM
    zero = jnp.zeros_like(tile)
    return jnp.concatenate([jnp.where(first, tile, zero), jnp.where(first, zero, tile)], axis=0)


def side_by_side(stacked):
    rows = stacked.shape[0] // 2
    first = lax.broadcasted_iota(jnp.int32, (rows, stacked.shape[1]), 1) < HEAD_DIM
    return jnp.where(first, stacked[:rows], stacked[rows:])


def dot(a, b, over):
    return lax.dot_general(a, b, (over, ((), ())), preferred_element_type=F32)


LAST = ((1,), (1,))
PLAIN = ((1,), (0,))
ROWS = ((0,), (0,))


def attend(q, k, v, allowed):
    scores = jnp.where(allowed, dot(two_heads(q), k, LAST), -1e30)
    raised = jnp.exp(scores - jnp.max(scores, axis=-1, keepdims=True))
    weights = (raised * (1.0 / jnp.sum(raised, axis=-1, keepdims=True))).astype(BF16)
    return weights, side_by_side(dot(weights, v, PLAIN)).astype(BF16)


def attend_back(q, k, v, weights, dc):
    stacked = two_heads(dc)
    dv = dot(weights, stacked, ROWS)
    dweights = dot(stacked, v, LAST)
    probs = weights.astype(F32)
    terms = probs * dweights
    dscores = (terms - probs * jnp.sum(terms, axis=-1, keepdims=True)).astype(BF16)
    dq = side_by_side(dot(dscores, k, PLAIN)) * (1.0 / math.sqrt(HEAD_DIM))
    dk = dot(dscores, two_heads(q), ROWS)
    return dq.astype(BF16), dk.astype(BF16), dv.astype(BF16)


def column(slot, h, g):
    return (slot, slice(None), pl.ds(pl.multiple_of(256 * g + LANES * h, LANES), LANES))


def back(rg, slots, weight, rows=None):
    half = weight.shape[1] // 2
    total = None
    for j, slot in enumerate(slots):
        for g in range(3):
            at = j * 384 + g * LANES
            w = jnp.concatenate([weight[:, at : at + LANES], weight[:, half + at : half + at + LANES]], axis=1)
            term = dot(rg[slot, :, 256 * g : 256 * g + 256], w, LAST)
            total = term if total is None else total + term
    return total


def layer_kernel(
    dec_input, memory, src_len, out_grad, self_qkv, self_out, cross_query, cross_kv, cross_out, ffn_in, ffn_out,
    norm_gain, norm_bias,
    o_layer, o_input, o_memory, units, norm_out,
    x_in, mem, og, w_qkv, w_self, w_query, w_kv, w_cross, w_in, w_out,
    first, qkv, p_self, ctx_self, hidden1, second, qx, kv, p_cross, ctx_cross, hidden2, third,
    active, dup, acc, dthird,
    lt, rg, n_own, n_got, n_send, n_recv, load_sem, swap_send, swap_recv, out_sem, out_send, out_recv, *rest
):
    at = place()
    y = at["y"]
    red = Reducer(at, lt, rg, units, *rest)
    across = partner("y", at)

    loads = [
        pltpu.make_async_copy(src, dst, load_sem.at[n])
        for n, (src, dst) in enumerate(
            ((self_qkv, w_qkv), (self_out, w_self), (cross_kv, w_kv), (cross_query, w_query), (cross_out, w_cross))
        )
    ]
    for load in loads:
        load.start()

    def ffn_load(q):
        slot = q % 2
        cols = pl.ds(pl.multiple_of(q * 768, 768), 768)
        return (
            pltpu.make_async_copy(ffn_in.at[:, cols], w_in.at[slot], load_sem.at[7 + slot]),
            pltpu.make_async_copy(ffn_out.at[cols, :], w_out.at[slot], load_sem.at[9 + slot]),
        )

    for load in ffn_load(0):
        load.start()

    def own_rows(n, src, dst, rows):
        return [
            pltpu.make_async_copy(
                src.at[2 * y + e], dst.at[pl.ds(pl.multiple_of(2 * e * rows + y * rows, rows), rows), :], load_sem.at[11 + 2 * n + e]
            )
            for e in range(2)
        ]

    def swap(n, src, dst, rows):
        return [
            pltpu.make_async_remote_copy(
                src_ref=src.at[2 * (1 - y) + e],
                dst_ref=dst.at[pl.ds(pl.multiple_of(2 * e * rows + y * rows, rows), rows), :],
                send_sem=swap_send.at[n, e], recv_sem=swap_recv.at[n, e], device_id=across, device_id_type=MESH,
            )
            for e in range(2)
        ]

    moved = ((dec_input, x_in, 64), (memory, mem, 128), (out_grad, og, 64))
    owns = [own_rows(n, *m) for n, m in enumerate(moved)]
    swaps = [swap(n, *m) for n, m in enumerate(moved)]
    for own in owns:
        for copy in own:
            copy.start()
    greet(at)
    for n in (0, 1, 2):
        for copy in swaps[n]:
            copy.start()

    def arrived(n):
        for copy in owns[n]:
            copy.wait()
        for copy in swaps[n]:
            copy.wait_recv()

    scale = 1.0 / math.sqrt(HEAD_DIM)

    arrived(0)
    norm_forward(lambda rows: x_in[rows, :].astype(F32), first, norm_gain, norm_bias, 0)
    loads[0].wait()

    def project_qkv(n, carry):
        cols = pl.ds(pl.multiple_of(256 * n, 256), 256)
        out = jnp.dot(first[...], w_qkv[:, cols], preferred_element_type=F32)
        out = (out.astype(BF16) * jnp.where(n < 3, scale, 1.0).astype(BF16)).astype(BF16)
        qkv[2 * n] = out[:, 0:LANES]
        qkv[2 * n + 1] = out[:, LANES:256]
        return carry

    lax.fori_loop(0, 9, project_qkv, 0)

    def pair(it):
        e = it // 6
        p = it % 6
        return e, p, pl.ds(pl.multiple_of(e * 128, 128), 128), pl.ds(pl.multiple_of(p * LANES, LANES), LANES)

    def self_forward(it, carry):
        e, p, rows, lanes = pair(it)
        q_at = lax.broadcasted_iota(jnp.int32, (256, 128), 0) % 128
        k_at = lax.broadcasted_iota(jnp.int32, (256, 128), 1)
        weights, context = attend(qkv[p, rows, :], qkv[6 + p, rows, :], qkv[12 + p, rows, :], q_at >= k_at)
        p_self[it] = weights
        ctx_self[rows, lanes] = context
        return carry

    lax.fori_loop(0, 12, self_forward, 0)

    loads[1].wait()
    for n in range(3):
        cols = slice(256 * n, 256 * n + 256)
        hidden1[:, cols] = x_in[:, cols].astype(F32) + jnp.dot(ctx_self[...], w_self[:, cols], preferred_element_type=F32)
    norm_forward(lambda rows: hidden1[rows, :], second, norm_gain, norm_bias, 1)

    loads[3].wait()
    for n in range(3):
        out = jnp.dot(second[...], w_query[:, 256 * n : 256 * n + 256], preferred_element_type=F32)
        out = (out.astype(BF16) * jnp.asarray(scale, BF16)).astype(BF16)
        qx[2 * n] = out[:, 0:LANES]
        qx[2 * n + 1] = out[:, LANES:256]
    loads[2].wait()
    arrived(1)

    def project_kv(n, carry):
        cols = pl.ds(pl.multiple_of(256 * n, 256), 256)
        for e in range(2):
            out = jnp.dot(mem[256 * e : 256 * e + 256, :], w_kv[:, cols], preferred_element_type=F32).astype(BF16)
            kv[2 * n, 256 * e : 256 * e + 256, :] = out[:, 0:LANES]
            kv[2 * n + 1, 256 * e : 256 * e + 256, :] = out[:, LANES:256]
        return carry

    lax.fori_loop(0, 6, project_kv, 0)

    def cross_rows(e):
        return pl.ds(pl.multiple_of(e * 256, 256), 256)

    def cross_forward(it, carry):
        e, p, rows, lanes = pair(it)
        allowed = lax.broadcasted_iota(jnp.int32, (256, 256), 1) < src_len[2 * y + e]
        weights, context = attend(qx[p, rows, :], kv[p, cross_rows(e), :], kv[6 + p, cross_rows(e), :], allowed)
        p_cross[it] = weights
        ctx_cross[rows, lanes] = context
        return carry

    lax.fori_loop(0, 12, cross_forward, 0)

    loads[4].wait()
    for n in range(3):
        cols = slice(256 * n, 256 * n + 256)
        hidden2[:, cols] = hidden1[:, cols] + jnp.dot(ctx_cross[...], w_cross[:, cols], preferred_element_type=F32)
    norm_forward(lambda rows: hidden2[rows, :], third, norm_gain, norm_bias, 2)

    arrived(2)
    acc[...] = jnp.zeros_like(acc)
    dthird[...] = jnp.zeros_like(dthird)
    root = math.sqrt(2.0 / math.pi)

    def feed(q, carry):
        slot = q % 2

        @pl.when(q < 3)
        def _():
            for load in ffn_load(q + 1):
                load.start()

        for load in ffn_load(q):
            load.wait()
        h = q // 2
        for s in range(3):
            cols = slice(256 * s, 256 * s + 256)
            up = jnp.dot(third[...], w_in[slot, :, cols], preferred_element_type=F32)
            dact = dot(og[...], w_out[slot, cols, :], LAST)
            square = up * up
            bend = jnp.tanh(root * up * (1.0 + 0.044715 * square))
            lift = 0.5 * (1.0 + bend)
            active[:, cols] = (up * lift).astype(BF16)
            slope = lift + 0.5 * up * (1.0 - bend * bend) * (root * (1.0 + 3.0 * 0.044715 * square))
            grad = (dact * slope).astype(BF16)
            dup[:, cols] = grad
            for t in range(2):
                tile = 2 * s + t
                rg[column(4 + (q % 2) * 2 + tile // 3, h, tile % 3)] = grad[:, LANES * t : LANES * t + LANES]
        for s in range(3):
            cols = slice(256 * s, 256 * s + 256)
            acc[:, cols] += jnp.dot(active[...], w_out[slot, :, cols], preferred_element_type=F32)
            dthird[:, cols] += dot(dup[...], w_in[slot, cols, :], LAST)
        flipped = active[...].T
        for i in range(4):
            for k in range(4):
                rows = pl.ds(pl.multiple_of(48 * (2 * q + i // 2), 48), 48)
                lt[k, i % 2, rows, :] = flipped[192 * i + 48 * k : 192 * i + 48 * k + 48, :]
        return carry

    lax.fori_loop(0, 4, feed, 0)

    for k in range(4):
        for g in range(3):
            for h in range(2):
                lane = h * 384 + g * LANES
                rg[k, :, 256 * g + LANES * h : 256 * g + LANES * h + LANES] = og[:, lane : lane + LANES]
    store_left(lt, 4, third[...].T)

    def give(n, buf, out, rows, e):
        def part(which):
            return buf.at[pl.ds(pl.multiple_of(2 * e * rows + which * rows, rows), rows), :]

        stay = pltpu.make_async_copy(part(y), out.at[2 * y + e], out_sem.at[n, e])
        leave = pltpu.make_async_remote_copy(
            src_ref=part(1 - y), dst_ref=out.at[2 * y + e], send_sem=out_send.at[n, e], recv_sem=out_recv.at[n, e],
            device_id=across, device_id_type=MESH,
        )
        return stay, leave

    gives = []

    def send(n, buf, out, rows):
        for e in range(2):
            stay, leave = give(n, buf, out, rows, e)
            stay.start()
            leave.start()
            gives.append((stay, leave))

    third[...] = (hidden2[...] + acc[...]).astype(BF16)
    send(0, third, o_layer, 64)

    sums = n_own.at[0]
    sums[...] = jnp.zeros(sums.shape, F32)

    def store_grad(rows, value):
        acc[rows, :] = value

    def spread(slot):
        for g in range(3):
            for h in range(2):
                lane = h * 384 + g * LANES
                rg[slot, :, 256 * g + LANES * h : 256 * g + LANES * h + LANES] = acc[:, lane : lane + LANES].astype(BF16)

    norm_backward(
        lambda rows: hidden2[rows, :], lambda rows: dthird[rows, :],
        lambda rows, v: store_grad(rows, og[rows, :].astype(F32) + v), norm_gain, sums, 2,
    )
    spread(8)
    store_left(lt, 5, ctx_cross[...].T)

    dc = active

    def context_grad(slot, weight):
        for n in range(3):
            total = None
            for g in range(3):
                lane = g * LANES
                rows = slice(256 * n, 256 * n + 256)
                w = jnp.concatenate([weight[rows, lane : lane + LANES], weight[rows, 384 + lane : 384 + lane + LANES]], axis=1)
                term = dot(rg[slot, :, 256 * g : 256 * g + 256], w, LAST)
                total = term if total is None else total + term
            dc[:, 256 * n : 256 * n + 256] = total.astype(BF16)

    context_grad(8, w_cross)

    def cross_backward(it):
        e, p, rows, lanes = pair(it)
        dq, dk, dv = attend_back(qx[p, rows, :], kv[p, cross_rows(e), :], kv[6 + p, cross_rows(e), :], p_cross[it], dc[rows, lanes])
        h, j, g = p // 3, p // 3, p % 3
        rg[11, rows, pl.ds(pl.multiple_of(256 * g + LANES * h, LANES), LANES)] = dq
        rg[column(9 + 7 * e + j, 0, g)] = dk
        rg[column(9 + 7 * e + j, 1, g)] = dv

    def cross_loop(it, carry):
        cross_backward(it)
        return carry

    lax.fori_loop(0, 12, cross_loop, 0)

    store_left(lt, 6, mem[0:256, :].T)
    store_left(lt, 7, mem[256:512, :].T)
    for e in range(2):
        for n in range(3):
            rows = slice(256 * n, 256 * n + 256)
            mem[256 * e : 256 * e + 256, rows] = back(rg, (9 + 7 * e, 10 + 7 * e), w_kv.at[rows, :]).astype(BF16)
    send(1, mem, o_memory, 128)
    for n in range(3):
        rows = slice(256 * n, 256 * n + 256)
        dthird[:, rows] = back(rg, (11,), w_query.at[rows, :])
    norm_backward(
        lambda rows: hidden1[rows, :], lambda rows: dthird[rows, :],
        lambda rows, v: store_grad(rows, acc[rows, :] + v), norm_gain, sums, 1,
    )
    spread(12)
    context_grad(12, w_self)
    store_left(lt, 8, second[...].T)
    store_left(lt, 9, ctx_self[...].T)
    store_left(lt, 10, first[...].T)

    def self_backward(it):
        e, p, rows, lanes = pair(it)
        dq, dk, dv = attend_back(qkv[p, rows, :], qkv[6 + p, rows, :], qkv[12 + p, rows, :], p_self[it], dc[rows, lanes])
        for n, value in enumerate((dq, dk, dv)):
            tile = 6 * n + p
            h = tile // 9
            j = (tile % 9) // 3
            rg[13 + j, rows, pl.ds(pl.multiple_of(256 * (tile % 3) + LANES * h, LANES), LANES)] = value

    def self_loop(it, carry):
        self_backward(it)
        return carry

    lax.fori_loop(0, 12, self_loop, 0)

    for n in range(3):
        rows = slice(256 * n, 256 * n + 256)
        dthird[:, rows] = back(rg, (13, 14, 15), w_qkv.at[rows, :])

    def store_input(rows, v):
        x_in[rows, :] = (acc[rows, :] + v).astype(BF16)

    norm_backward(
        lambda rows: x_in[rows, :].astype(F32), lambda rows: dthird[rows, :], store_input, norm_gain, sums, 0
    )
    send(2, x_in, o_input, 64)

    def body(n, carry):
        red.tick(n)
        for j in range(6):
            @pl.when(n == 2 * j)
            def _():
                norm_step(j, at, n_own, n_got, n_send, n_recv)
        return carry

    lax.fori_loop(0, TRIPLES + 5, body, 0)
    norm_out[...] = n_own[5]
    red.drain()
    for n in range(3):
        for copy in swaps[n]:
            copy.wait_send()
    for stay, leave in gives:
        stay.wait()
        leave.wait()


def layer_call(args):
    anywhere = pl.BlockSpec(memory_space=pl.ANY)
    vmem = pl.BlockSpec(memory_space=pltpu.VMEM)
    rows = lambda width, kind=BF16: pltpu.VMEM((256, width), kind)
    return pl.pallas_call(
        layer_kernel,
        out_shape=(
            jax.ShapeDtypeStruct((4, 64, 768), BF16),
            jax.ShapeDtypeStruct((4, 64, 768), BF16),
            jax.ShapeDtypeStruct((4, 128, 768), BF16),
            jax.ShapeDtypeStruct((TRIPLES, 3, 48, 128), F32),
            jax.ShapeDtypeStruct((8, 768), F32),
        ),
        in_specs=[anywhere, anywhere, pl.BlockSpec(memory_space=pltpu.SMEM)] + [anywhere] * 8 + [vmem] * 2,
        out_specs=(anywhere, anywhere, anywhere, vmem, vmem),
        scratch_shapes=[
            rows(768), pltpu.VMEM((512, 768), BF16), rows(768),
            pltpu.VMEM((768, 2304), BF16), pltpu.VMEM((768, 768), BF16), pltpu.VMEM((768, 768), BF16),
            pltpu.VMEM((768, 1536), BF16), pltpu.VMEM((768, 768), BF16),
            pltpu.VMEM((2, 768, 768), BF16), pltpu.VMEM((2, 768, 768), BF16),
            rows(768), pltpu.VMEM((18, 256, 128), BF16), pltpu.VMEM((12, 256, 128), BF16), rows(768),
            rows(768, F32), rows(768), pltpu.VMEM((6, 256, 128), BF16), pltpu.VMEM((12, 512, 128), BF16),
            pltpu.VMEM((12, 256, 256), BF16), rows(768), rows(768, F32), rows(768),
            rows(768), rows(768), rows(768, F32), rows(768, F32),
            pltpu.VMEM((11, 2, 384, 256), BF16),
            pltpu.VMEM((18, 256, 768), BF16),
            pltpu.VMEM((6, 8, 768), F32),
            pltpu.VMEM((5, 8, 768), F32),
            pltpu.SemaphoreType.DMA((5,)),
            pltpu.SemaphoreType.DMA((5,)),
            pltpu.SemaphoreType.DMA((17,)),
            pltpu.SemaphoreType.DMA((3, 2)),
            pltpu.SemaphoreType.DMA((3, 2)),
            pltpu.SemaphoreType.DMA((3, 2)),
            pltpu.SemaphoreType.DMA((3, 2)),
            pltpu.SemaphoreType.DMA((3, 2)),
        ] + Reducer.SCRATCH,
        compiler_params=pltpu.CompilerParams(collective_id=0, has_side_effects=True, vmem_limit_bytes=60 << 20),
    )(*args)


def per_device_paired(*args):
    layer_out, input_grad, memory_grad, units, norms = layer_call(args)
    grads = gather_outputs(units)
    return (
        layer_out,
        input_grad.astype(F32),
        memory_grad.astype(F32),
        grads["self_qkv"],
        grads["self_out"],
        grads["cross_query"],
        grads["cross_kv"],
        grads["cross_out"],
        grads["ffn_in"],
        grads["ffn_out"],
        norms[0:3],
        norms[3:6],
    )

def layer_norm(x, gain, shift):
    center = jnp.mean(x, axis=-1, keepdims=True)
    centered = x - center
    spread = jnp.mean(centered * centered, axis=-1, keepdims=True)
    return centered * lax.rsqrt(spread + 1e-05) * gain + shift


def smooth(v):
    return jax.nn.gelu(v, approximate=True)


def project(rows, weight):
    return jnp.einsum("etd,df->etf", rows, weight, preferred_element_type=jnp.float32)


def project_back(grads, weight):
    return jnp.einsum("etf,df->etd", grads, weight, preferred_element_type=jnp.float32)


def outer(rows, grads):
    return jnp.einsum("etd,etf->df", rows, grads, preferred_element_type=jnp.float32)


def outer_full(rows, grads):
    return jnp.einsum(
        "etd,etf->df", rows.astype(jnp.float32), grads, precision=lax.Precision.HIGHEST
    )


def back_full(grads, weight):
    return jnp.einsum(
        "etf,df->etd", grads, weight.astype(jnp.float32), precision=lax.Precision.HIGHEST
    )


def split_heads(queries, key_values):
    examples, rows, width = queries.shape
    count = key_values.shape[1]
    heads_q = queries.reshape(examples, rows, HEADS, HEAD_DIM)
    heads_k = key_values[:, :, :width].reshape(examples, count, HEADS, HEAD_DIM)
    heads_v = key_values[:, :, width:].reshape(examples, count, HEADS, HEAD_DIM)
    return (heads_q, heads_k, heads_v)


def masked_logits(heads_q, heads_k, allowed):
    scores = jnp.einsum("eqhd,ekhd->ehqk", heads_q, heads_k, preferred_element_type=jnp.float32)
    return jnp.where(allowed, scores * (1.0 / math.sqrt(HEAD_DIM)), -1e30)


def attend_forward(queries, key_values, allowed):
    examples, rows, width = queries.shape
    heads_q, heads_k, heads_v = split_heads(queries, key_values)
    logits = masked_logits(heads_q, heads_k, allowed)
    row_top = jnp.max(logits, axis=-1, keepdims=True)
    raised = jnp.where(allowed, jnp.exp(logits - row_top), 0.0)
    row_total = jnp.sum(raised, axis=-1, keepdims=True)
    weights = (raised / row_total).astype(jnp.bfloat16)
    context = jnp.einsum("ehqk,ekhd->eqhd", weights, heads_v, preferred_element_type=jnp.float32)
    return (
        context.reshape(examples, rows, width).astype(jnp.bfloat16),
        row_top + jnp.log(row_total),
    )


def attend_backward(queries, key_values, allowed, log_total, grad_context):
    examples, rows, width = queries.shape
    count = key_values.shape[1]
    heads_q, heads_k, heads_v = split_heads(queries, key_values)
    logits = masked_logits(heads_q, heads_k, allowed)
    soft = jnp.where(allowed, jnp.exp(logits - log_total), 0.0)
    grad_heads = grad_context.reshape(examples, rows, HEADS, HEAD_DIM)
    grad_soft = jnp.einsum(
        "eqhd,ekhd->ehqk", grad_heads, heads_v, preferred_element_type=jnp.float32
    )
    grad_values = jnp.einsum(
        "ehqk,eqhd->ekhd", soft.astype(jnp.bfloat16), grad_heads, preferred_element_type=jnp.float32
    )
    inner = jnp.sum(soft * grad_soft, axis=-1, keepdims=True)
    grad_scores = (soft * (grad_soft - inner) * (1.0 / math.sqrt(HEAD_DIM))).astype(jnp.bfloat16)
    grad_queries = jnp.einsum(
        "ehqk,ekhd->eqhd", grad_scores, heads_k, preferred_element_type=jnp.float32
    )
    grad_keys = jnp.einsum(
        "ehqk,eqhd->ekhd", grad_scores, heads_q, preferred_element_type=jnp.float32
    )
    joined = jnp.concatenate(
        [grad_keys.reshape(examples, count, width), grad_values.reshape(examples, count, width)],
        axis=2,
    )
    return (grad_queries.reshape(examples, rows, width), joined)


def per_device_wide(
    dec_input,
    memory,
    src_len,
    out_grad,
    self_qkv,
    self_out,
    cross_query,
    cross_kv,
    cross_out,
    ffn_in,
    ffn_out,
    norm_gain,
    norm_bias,
):
    examples, local_rows, width = dec_input.shape
    local_sources = memory.shape[1]
    seq_count = lax.axis_size("seq")
    all_targets = local_rows * seq_count
    all_sources = local_sources * seq_count
    rank = lax.axis_index("seq")
    x = dec_input.astype(jnp.float32)
    first_f, pull_first = jax.vjp(layer_norm, x, norm_gain[0], norm_bias[0])
    first = first_f.astype(jnp.bfloat16)
    projected = project(first, self_qkv).astype(jnp.bfloat16)
    self_queries = projected[:, :, :width]
    self_kv = lax.all_gather(projected[:, :, width:], "seq", axis=1, tiled=True)
    query_place = rank * local_rows + jnp.arange(local_rows, dtype=jnp.int32)
    key_place = jnp.arange(all_targets, dtype=jnp.int32)
    causal = (query_place[:, None] >= key_place[None, :])[None, None]
    self_context, self_total = attend_forward(self_queries, self_kv, causal)
    hidden1 = x + project(self_context, self_out)
    second_f, pull_second = jax.vjp(layer_norm, hidden1, norm_gain[1], norm_bias[1])
    second = second_f.astype(jnp.bfloat16)
    cross_queries = project(second, cross_query).astype(jnp.bfloat16)
    gathered = lax.all_gather(memory, "seq", axis=1, tiled=True)
    memory_kv = project(gathered, cross_kv).astype(jnp.bfloat16)
    source_place = jnp.arange(all_sources, dtype=jnp.int32)
    visible = (source_place[None, :] < src_len[:, None])[:, None, None, :]
    cross_context, cross_total = attend_forward(cross_queries, memory_kv, visible)
    hidden2 = hidden1 + project(cross_context, cross_out)
    third_f, pull_third = jax.vjp(layer_norm, hidden2, norm_gain[2], norm_bias[2])
    third = third_f.astype(jnp.bfloat16)
    raised_up = project(third, ffn_in)
    active_f, pull_smooth = jax.vjp(smooth, raised_up)
    activated = active_f.astype(jnp.bfloat16)
    layer_out = (hidden2 + project(activated, ffn_out)).astype(jnp.bfloat16)
    grad_out = out_grad.astype(jnp.float32)
    ffn_out_grad = outer(activated, out_grad)
    (grad_up,) = pull_smooth(project_back(out_grad, ffn_out))
    grad_up_low = grad_up.astype(jnp.bfloat16)
    ffn_in_grad = outer(third, grad_up_low)
    back_third, gain_third, bias_third = pull_third(project_back(grad_up_low, ffn_in))
    grad_hidden2 = grad_out + back_third
    cross_branch = grad_hidden2.astype(jnp.bfloat16)
    cross_out_grad = outer(cross_context, cross_branch)
    grad_cross_context = project_back(cross_branch, cross_out).astype(jnp.bfloat16)
    grad_cross_q, grad_memory_kv = attend_backward(
        cross_queries, memory_kv, visible, cross_total, grad_cross_context
    )
    local_kv_grad = lax.psum_scatter(
        grad_memory_kv.astype(jnp.bfloat16), "seq", scatter_dimension=1, tiled=True
    ).astype(jnp.float32)
    cross_kv_grad = outer_full(memory, local_kv_grad)
    memory_grad = back_full(local_kv_grad, cross_kv)
    grad_cross_low = grad_cross_q.astype(jnp.bfloat16)
    cross_query_grad = outer(second, grad_cross_low)
    back_second, gain_second, bias_second = pull_second(project_back(grad_cross_low, cross_query))
    grad_hidden1 = grad_hidden2 + back_second
    self_branch = grad_hidden1.astype(jnp.bfloat16)
    self_out_grad = outer(self_context, self_branch)
    grad_self_context = project_back(self_branch, self_out).astype(jnp.bfloat16)
    grad_self_q, grad_self_kv = attend_backward(
        self_queries, self_kv, causal, self_total, grad_self_context
    )
    local_self_kv = lax.psum_scatter(grad_self_kv, "seq", scatter_dimension=1, tiled=True)
    grad_projected = jnp.concatenate([grad_self_q, local_self_kv], axis=2).astype(jnp.bfloat16)
    self_qkv_grad = outer(first, grad_projected)
    back_first, gain_first, bias_first = pull_first(project_back(grad_projected, self_qkv))
    input_grad = grad_hidden1 + back_first
    gain_terms = jnp.stack([gain_first, gain_second, gain_third])
    bias_terms = jnp.stack([bias_first, bias_second, bias_third])
    gain_total, bias_total = lax.psum((gain_terms, bias_terms), ("dp", "seq"))
    partial_value = (
        lax.psum_scatter(
            self_qkv_grad.astype(jnp.bfloat16), "dp", scatter_dimension=0, tiled=True
        ).astype(jnp.float32),
        lax.psum_scatter(
            self_out_grad.astype(jnp.bfloat16), "dp", scatter_dimension=0, tiled=True
        ).astype(jnp.float32),
        lax.psum_scatter(
            cross_query_grad.astype(jnp.bfloat16), "dp", scatter_dimension=0, tiled=True
        ).astype(jnp.float32),
        lax.psum_scatter(
            cross_kv_grad.astype(jnp.bfloat16), "dp", scatter_dimension=0, tiled=True
        ).astype(jnp.float32),
        lax.psum_scatter(
            cross_out_grad.astype(jnp.bfloat16), "dp", scatter_dimension=0, tiled=True
        ).astype(jnp.float32),
        lax.psum_scatter(
            ffn_in_grad.astype(jnp.bfloat16), "dp", scatter_dimension=0, tiled=True
        ).astype(jnp.float32),
        lax.psum_scatter(
            ffn_out_grad.astype(jnp.bfloat16), "dp", scatter_dimension=0, tiled=True
        ).astype(jnp.float32),
    )
    finished = (
        lax.psum_scatter(
            partial_value[0].astype(jnp.bfloat16), "seq", scatter_dimension=1, tiled=True
        ).astype(jnp.float32),
        lax.psum_scatter(
            partial_value[1].astype(jnp.bfloat16), "seq", scatter_dimension=1, tiled=True
        ).astype(jnp.float32),
        lax.psum_scatter(
            partial_value[2].astype(jnp.bfloat16), "seq", scatter_dimension=1, tiled=True
        ).astype(jnp.float32),
        lax.psum_scatter(
            partial_value[3].astype(jnp.bfloat16), "seq", scatter_dimension=1, tiled=True
        ).astype(jnp.float32),
        lax.psum_scatter(
            partial_value[4].astype(jnp.bfloat16), "seq", scatter_dimension=1, tiled=True
        ).astype(jnp.float32),
        lax.psum_scatter(
            partial_value[5].astype(jnp.bfloat16), "seq", scatter_dimension=1, tiled=True
        ).astype(jnp.float32),
        lax.psum_scatter(
            partial_value[6].astype(jnp.bfloat16), "seq", scatter_dimension=1, tiled=True
        ).astype(jnp.float32),
    )
    return (
        layer_out,
        input_grad,
        memory_grad,
        finished[0],
        finished[1],
        finished[2],
        finished[3],
        finished[4],
        finished[5],
        finished[6],
        gain_total,
        bias_total,
    )


def solution(mesh):
    paired = mesh.shape["dp"] == 16 and mesh.shape["seq"] == 2
    per_device = per_device_paired if paired else per_device_wide
    in_specs = (
        P("dp", "seq", None),
        P("dp", "seq", None),
        P("dp"),
        P("dp", "seq", None),
        P(),
        P(),
        P(),
        P(),
        P(),
        P(),
        P(),
        P(),
        P(),
    )
    out_specs = (
        P("dp", "seq", None),
        P("dp", "seq", None),
        P("dp", "seq", None),
        P("dp", "seq"),
        P("dp", "seq"),
        P("dp", "seq"),
        P("dp", "seq"),
        P("dp", "seq"),
        P("dp", "seq"),
        P("dp", "seq"),
        P(),
        P(),
    )
    return jax.shard_map(
        per_device, mesh=mesh, in_specs=in_specs, out_specs=out_specs, check_vma=False
    )
```

```python
import functools
import math

import jax
import jax.numpy as jnp
from jax import lax
from jax.experimental import pallas as pl
from jax.experimental.pallas import tpu as pltpu
from jax.sharding import PartitionSpec as P

HEADS = 12
HEAD_DIM = 64
MESH = pl.DeviceIdType.MESH
F32 = jnp.float32
BF16 = jnp.bfloat16
TRIPLES = 16
ORDERS = (("x", "l", "y", "h"), ("y", "x", "l", "h"), ("l", "x", "y", "h"))


def place():
    i = lax.axis_index("dp")
    return {"c": i % 2, "x": (i // 2) % 2, "l": (i // 4) % 2, "h": i // 8, "y": lax.axis_index("seq")}


def partner(axis, at):
    i = lax.axis_index("dp")
    y = at["y"]
    if axis == "y":
        return (i, 1 - y)
    step = {"c": 1, "x": 2, "l": 4, "h": 8}[axis]
    return (i + step - 2 * step * at[axis], y)


def greet(at):
    barrier = pltpu.get_barrier_semaphore()
    for axis in ("c", "x", "l", "h", "y"):
        pl.semaphore_signal(barrier, inc=1, device_id=partner(axis, at), device_id_type=MESH)
    pl.semaphore_wait(barrier, 5)


LEFT = (0, 1, 2, 3, 4, 4, 4, 4, 5, 6, 6, 8, 9, 10, 10, 10)
RIGHT = (0, 0, 0, 0, 1, 2, 3, 4, 5, 6, 7, 8, 9, 10, 11, 12)


def look_up(table, t):
    if isinstance(t, int):
        return table[t]
    value = table[-1]
    for n in range(TRIPLES - 2, -1, -1):
        if table[n] != table[n + 1]:
            value = jnp.where(t <= n, table[n], value)
    return value


def when(condition):
    if isinstance(condition, bool):
        return (lambda body: body()) if condition else (lambda body: None)
    return pl.when(condition)


def negate(condition):
    return not condition if isinstance(condition, bool) else jnp.logical_not(condition)


def store_left(lt, slot, rows_by_feature):
    for i in range(16):
        lt[slot, i % 2, 48 * (i // 2) : 48 * (i // 2) + 48, :] = rows_by_feature[48 * i : 48 * i + 48, :]


class Reducer:
    LAGS = (0, 1, 3, 5, 7, 8)
    SLOTS = (2, 3, 3, 3, 3)
    TICKS = TRIPLES + 8
    SCRATCH = [
        pltpu.VMEM((2, 3, 384, 256), BF16),
        pltpu.VMEM((TRIPLES, 3, 384, 256), BF16),
        pltpu.VMEM((3, 3, 2, 2, 2, 2, 48, 128), BF16),
        pltpu.VMEM((TRIPLES, 3, 2, 2, 2, 48, 128), BF16),
        pltpu.VMEM((3, 3, 2, 2, 2, 48, 128), BF16),
        pltpu.VMEM((TRIPLES, 3, 2, 2, 48, 128), BF16),
        pltpu.VMEM((3, 3, 2, 2, 48, 128), BF16),
        pltpu.VMEM((TRIPLES, 3, 2, 48, 128), BF16),
        pltpu.VMEM((3, 3, 2, 48, 128), BF16),
        pltpu.VMEM((TRIPLES, 3, 48, 128), BF16),
        pltpu.VMEM((3, 3, 48, 128), F32),
        pltpu.SemaphoreType.DMA((3,)),
        pltpu.SemaphoreType.DMA((5, 3, 3)),
        pltpu.SemaphoreType.DMA((5, TRIPLES, 3)),
    ]

    def __init__(self, at, lt, rg, out, s0, r0, s1, r1, s2, r2, s3, r3, s4, r4, done, done_sem, send_sem, recv_sem):
        self.at, self.lt, self.rg, self.out = at, lt, rg, out
        self.sent, self.got = (s0, s1, s2, s3, s4), (r0, r1, r2, r3, r4)
        self.done, self.done_sem = done, done_sem
        self.send_sem, self.recv_sem = send_sem, recv_sem

    def axis(self, stage, g):
        return "c" if stage == 0 else ORDERS[g][stage - 1]

    def copy(self, stage, t, g):
        axis = self.axis(stage, g)
        slot = t % self.SLOTS[stage]
        src = self.sent[stage].at[slot, g]
        if stage:
            src = src.at[1 - self.at[axis]]
        return pltpu.make_async_remote_copy(
            src_ref=src,
            dst_ref=self.got[stage].at[t, g],
            send_sem=self.send_sem.at[stage, slot, g],
            recv_sem=self.recv_sem.at[stage, t, g],
            device_id=partner(axis, self.at),
            device_id_type=MESH,
        )

    def free(self, stage, t):
        slots = self.SLOTS[stage]

        @when(t >= slots)
        def _():
            for g in range(3):
                self.copy(stage, t - slots, g).wait_send()

    def product(self, t, half, g):
        cols = slice(256 * g, 256 * g + 256)
        return jnp.dot(self.lt[look_up(LEFT, t), half], self.rg[look_up(RIGHT, t), :, cols], preferred_element_type=F32)

    def first(self, t):
        self.free(0, t)
        half = 1 - self.at["c"]
        memory = (t == 9) | (t == 10)
        for g in range(3):
            cols = slice(256 * g, 256 * g + 256)

            @when(negate(memory))
            def _():
                self.sent[0][t % 2, g] = self.product(t, half, g).astype(BF16)

            @when(memory)
            def _():
                more = jnp.dot(self.lt[7, half], self.rg[t + 4, :, cols], preferred_element_type=F32)
                self.sent[0][t % 2, g] = (self.product(t, half, g) + more).astype(BF16)

            self.copy(0, t, g).start()

    def second(self, t):
        self.free(1, t)
        half = self.at["c"]
        memory = (t == 9) | (t == 10)
        for g in range(3):
            cols = slice(256 * g, 256 * g + 256)
            self.copy(0, t, g).wait_recv()

            def spread(total):
                order = ORDERS[g]
                for b in range(8):
                    bits = {"h": b // 4, "l": (b // 2) % 2, "x": b % 2}
                    for y in range(2):
                        bits["y"] = y
                        where = tuple(bits[a] for a in order)
                        self.sent[1][(t % self.SLOTS[1], g) + where] = total[48 * b : 48 * b + 48, 128 * y : 128 * y + 128].astype(BF16)

            @when(negate(memory))
            def _():
                spread(self.product(t, half, g) + self.got[0][t, g].astype(F32))

            @when(memory)
            def _():
                more = jnp.dot(self.lt[7, half], self.rg[t + 4, :, cols], preferred_element_type=F32)
                spread(self.product(t, half, g) + more + self.got[0][t, g].astype(F32))

            self.copy(1, t, g).start()

    def write(self, t):
        return pltpu.make_async_copy(self.done.at[t % 3], self.out.at[t], self.done_sem.at[t % 3])

    def onward(self, stage, t):
        if stage < 5:
            self.free(stage, t)
        else:

            @when(t >= 3)
            def _():
                self.write(t - 3).wait()

        for g in range(3):
            self.copy(stage - 1, t, g).wait_recv()
            own = self.sent[stage - 1][t % self.SLOTS[stage - 1], g, self.at[self.axis(stage - 1, g)]]
            total = own.astype(F32) + self.got[stage - 1][t, g].astype(F32)
            if stage < 5:
                self.sent[stage][t % self.SLOTS[stage], g] = total.astype(BF16)
                self.copy(stage, t, g).start()
            else:
                self.done[t % 3, g] = total
        if stage == 5:
            self.write(t).start()

    def tick(self, n):
        for stage in range(6):
            t = n - self.LAGS[stage]

            @when((t >= 0) & (t < TRIPLES))
            def _():
                if stage == 0:
                    self.first(t)
                elif stage == 1:
                    self.second(t)
                else:
                    self.onward(stage, t)

    def drain(self):
        for t in range(TRIPLES - 3, TRIPLES):
            self.write(t).wait()
        for stage in range(5):
            for t in range(TRIPLES - self.SLOTS[stage], TRIPLES):
                for g in range(3):
                    self.copy(stage, t, g).wait_send()


NORM_ORDER = ("c", "x", "y", "l", "h")


def norm_copy(j, at, own, got, send_sem, recv_sem):
    return pltpu.make_async_remote_copy(
        src_ref=own.at[j], dst_ref=got.at[j], send_sem=send_sem.at[j], recv_sem=recv_sem.at[j],
        device_id=partner(NORM_ORDER[j], at), device_id_type=MESH,
    )


def norm_step(j, at, own, got, send_sem, recv_sem):
    if j:
        norm_copy(j - 1, at, own, got, send_sem, recv_sem).wait()
        own[j] = own[j - 1] + got[j - 1]
    if j < 5:
        norm_copy(j, at, own, got, send_sem, recv_sem).start()


LANES = 128


def normed(v):
    center = jnp.mean(v, axis=-1, keepdims=True)
    centered = v - center
    spread = jnp.mean(centered * centered, axis=-1, keepdims=True)
    scale = lax.rsqrt(spread + 1e-05)
    return centered * scale, scale


def row_blocks(step, body):
    for b in range(256 // step):
        body(slice(b * step, b * step + step))


def norm_forward(load, out, norm_gain, norm_bias, k):
    def body(rows):
        hat, _ = normed(load(rows))
        out[rows, :] = (hat * norm_gain[k : k + 1, :] + norm_bias[k : k + 1, :]).astype(BF16)

    row_blocks(64, body)


def norm_backward(load, load_grad, store, norm_gain, sums, k):
    def body(rows):
        hat, scale = normed(load(rows))
        dy = load_grad(rows)
        sums[k : k + 1, :] += jnp.sum(dy * hat, axis=0, keepdims=True)
        sums[k + 3 : k + 4, :] += jnp.sum(dy, axis=0, keepdims=True)
        dhat = dy * norm_gain[k : k + 1, :]
        mean = jnp.mean(dhat, axis=-1, keepdims=True)
        along = jnp.mean(dhat * hat, axis=-1, keepdims=True)
        store(rows, scale * (dhat - mean - hat * along))

    row_blocks(64, body)


def two_heads(tile):
    first = lax.broadcasted_iota(jnp.int32, tile.shape, 1) < HEAD_DIM
    zero = jnp.zeros_like(tile)
    return jnp.concatenate([jnp.where(first, tile, zero), jnp.where(first, zero, tile)], axis=0)


def side_by_side(stacked):
    rows = stacked.shape[0] // 2
    first = lax.broadcasted_iota(jnp.int32, (rows, stacked.shape[1]), 1) < HEAD_DIM
    return jnp.where(first, stacked[:rows], stacked[rows:])


def dot(a, b, over):
    return lax.dot_general(a, b, (over, ((), ())), preferred_element_type=F32)


LAST = ((1,), (1,))
PLAIN = ((1,), (0,))
ROWS = ((0,), (0,))


def attend(q, k, v, allowed):
    scores = jnp.where(allowed, dot(two_heads(q), k, LAST), -1e30)
    raised = jnp.exp(scores - jnp.max(scores, axis=-1, keepdims=True))
    weights = (raised * (1.0 / jnp.sum(raised, axis=-1, keepdims=True))).astype(BF16)
    return weights, side_by_side(dot(weights, v, PLAIN)).astype(BF16)


def attend_back(q, k, v, weights, dc):
    stacked = two_heads(dc)
    dv = dot(weights, stacked, ROWS)
    dweights = dot(stacked, v, LAST)
    probs = weights.astype(F32)
    terms = probs * dweights
    dscores = (terms - probs * jnp.sum(terms, axis=-1, keepdims=True)).astype(BF16)
    dq = side_by_side(dot(dscores, k, PLAIN)) * (1.0 / math.sqrt(HEAD_DIM))
    dk = dot(dscores, two_heads(q), ROWS)
    return dq.astype(BF16), dk.astype(BF16), dv.astype(BF16)


def column(slot, h, g):
    return (slot, slice(None), pl.ds(pl.multiple_of(256 * g + LANES * h, LANES), LANES))


def back(rg, slots, weight, rows=None):
    half = weight.shape[1] // 2
    total = None
    for j, slot in enumerate(slots):
        for g in range(3):
            at = j * 384 + g * LANES
            w = jnp.concatenate([weight[:, at : at + LANES], weight[:, half + at : half + at + LANES]], axis=1)
            term = dot(rg[slot, :, 256 * g : 256 * g + 256], w, LAST)
            total = term if total is None else total + term
    return total


def layer_kernel(
    dec_input, memory, src_len, out_grad, self_qkv, self_out, cross_query, cross_kv, cross_out, ffn_in, ffn_out,
    norm_gain, norm_bias,
    o_layer, o_input, o_memory, units, norm_out,
    x_in, mem, og, w_qkv, w_self, w_query, w_kv, w_cross, w_in, w_out,
    first, qkv, p_self, ctx_self, hidden1, second, qx, kv, p_cross, ctx_cross, hidden2, third,
    active, acc, dthird,
    lt, rg, n_own, n_got, n_send, n_recv, load_sem, swap_send, swap_recv, out_sem, out_send, out_recv, *rest
):
    at = place()
    y = at["y"]
    red = Reducer(at, lt, rg, units, *rest)
    across = partner("y", at)

    loads = [
        pltpu.make_async_copy(src, dst, load_sem.at[n])
        for n, (src, dst) in enumerate(
            ((self_qkv, w_qkv), (self_out, w_self), (cross_kv, w_kv), (cross_query, w_query), (cross_out, w_cross))
        )
    ]
    for load in loads:
        load.start()

    def ffn_load(q):
        slot = q % 2
        cols = pl.ds(pl.multiple_of(q * 768, 768), 768)
        return (
            pltpu.make_async_copy(ffn_in.at[:, cols], w_in.at[slot], load_sem.at[7 + slot]),
            pltpu.make_async_copy(ffn_out.at[cols, :], w_out.at[slot], load_sem.at[9 + slot]),
        )

    for load in ffn_load(0):
        load.start()

    def own_rows(n, src, dst, rows):
        return [
            pltpu.make_async_copy(
                src.at[2 * y + e], dst.at[pl.ds(pl.multiple_of(2 * e * rows + y * rows, rows), rows), :], load_sem.at[11 + 2 * n + e]
            )
            for e in range(2)
        ]

    def swap(n, src, dst, rows):
        return [
            pltpu.make_async_remote_copy(
                src_ref=src.at[2 * (1 - y) + e],
                dst_ref=dst.at[pl.ds(pl.multiple_of(2 * e * rows + y * rows, rows), rows), :],
                send_sem=swap_send.at[n, e], recv_sem=swap_recv.at[n, e], device_id=across, device_id_type=MESH,
            )
            for e in range(2)
        ]

    moved = ((dec_input, x_in, 64), (memory, mem, 128), (out_grad, og, 64))
    owns = [own_rows(n, *m) for n, m in enumerate(moved)]
    swaps = [swap(n, *m) for n, m in enumerate(moved)]
    for own in owns:
        for copy in own:
            copy.start()
    greet(at)
    for copy in swaps[0]:
        copy.start()

    def arrived(n):
        for copy in owns[n]:
            copy.wait()
        for copy in swaps[n]:
            copy.wait()
        if n < 2:
            for copy in swaps[n + 1]:
                copy.start()

    scale = 1.0 / math.sqrt(HEAD_DIM)

    arrived(0)
    norm_forward(lambda rows: x_in[rows, :].astype(F32), first, norm_gain, norm_bias, 0)
    loads[0].wait()

    def project_qkv(n, carry):
        cols = pl.ds(pl.multiple_of(256 * n, 256), 256)
        out = jnp.dot(first[...], w_qkv[:, cols], preferred_element_type=F32)
        out = (out.astype(BF16) * jnp.where(n < 3, scale, 1.0).astype(BF16)).astype(BF16)
        qkv[2 * n] = out[:, 0:LANES]
        qkv[2 * n + 1] = out[:, LANES:256]
        return carry

    lax.fori_loop(0, 9, project_qkv, 0)

    def pair(e, p):
        return slice(e * 128, e * 128 + 128), pl.ds(pl.multiple_of(p * LANES, LANES), LANES)

    def self_forward(p, carry):
        q_at = lax.broadcasted_iota(jnp.int32, (256, 128), 0) % 128
        k_at = lax.broadcasted_iota(jnp.int32, (256, 128), 1)
        for e in range(2):
            rows, lanes = pair(e, p)
            weights, context = attend(qkv[p, rows, :], qkv[6 + p, rows, :], qkv[12 + p, rows, :], q_at >= k_at)
            p_self[6 * e + p] = weights
            ctx_self[rows, lanes] = context
        return carry

    lax.fori_loop(0, 6, self_forward, 0)

    loads[1].wait()
    for n in range(3):
        cols = slice(256 * n, 256 * n + 256)
        hidden1[:, cols] = x_in[:, cols].astype(F32) + jnp.dot(ctx_self[...], w_self[:, cols], preferred_element_type=F32)
    norm_forward(lambda rows: hidden1[rows, :], second, norm_gain, norm_bias, 1)

    loads[3].wait()
    for n in range(3):
        out = jnp.dot(second[...], w_query[:, 256 * n : 256 * n + 256], preferred_element_type=F32)
        out = (out.astype(BF16) * jnp.asarray(scale, BF16)).astype(BF16)
        qx[2 * n] = out[:, 0:LANES]
        qx[2 * n + 1] = out[:, LANES:256]
    loads[2].wait()
    arrived(1)

    def project_kv(n, carry):
        cols = pl.ds(pl.multiple_of(256 * n, 256), 256)
        out = jnp.dot(mem[...], w_kv[:, cols], preferred_element_type=F32).astype(BF16)
        kv[2 * n] = out[:, 0:LANES]
        kv[2 * n + 1] = out[:, LANES:256]
        return carry

    lax.fori_loop(0, 6, project_kv, 0)

    def cross_rows(e):
        return slice(e * 256, e * 256 + 256)

    def cross_forward(p, carry):
        for e in range(2):
            rows, lanes = pair(e, p)
            allowed = lax.broadcasted_iota(jnp.int32, (256, 256), 1) < src_len[2 * y + e]
            weights, context = attend(qx[p, rows, :], kv[p, cross_rows(e), :], kv[6 + p, cross_rows(e), :], allowed)
            p_cross[6 * e + p] = weights
            ctx_cross[rows, lanes] = context
        return carry

    lax.fori_loop(0, 6, cross_forward, 0)

    loads[4].wait()
    for n in range(3):
        cols = slice(256 * n, 256 * n + 256)
        hidden2[:, cols] = hidden1[:, cols] + jnp.dot(ctx_cross[...], w_cross[:, cols], preferred_element_type=F32)
    norm_forward(lambda rows: hidden2[rows, :], third, norm_gain, norm_bias, 2)

    arrived(2)

    def spread(slot, rows_of):
        for g in range(3):
            for h in range(2):
                lane = h * 384 + g * LANES
                rg[slot, :, 256 * g + LANES * h : 256 * g + LANES * h + LANES] = rows_of[:, lane : lane + LANES].astype(BF16)

    spread(0, og)
    acc[...] = jnp.zeros_like(acc)
    dthird[...] = jnp.zeros_like(dthird)
    root = math.sqrt(2.0 / math.pi)

    def feed(q, carry):
        slot = q % 2

        @pl.when(q < 3)
        def _():
            for load in ffn_load(q + 1):
                load.start()

        for load in ffn_load(q):
            load.wait()

        def up_tile(tile):
            return column(1 + (q % 2) * 2 + tile // 3, q // 2, tile % 3)

        for s in range(3):
            cols = slice(256 * s, 256 * s + 256)
            up = jnp.dot(third[...], w_in[slot, :, cols], preferred_element_type=F32)
            dact = dot(og[...], w_out[slot, cols, :], LAST)
            square = up * up
            bend = jnp.tanh(root * up * (1.0 + 0.044715 * square))
            lift = 0.5 * (1.0 + bend)
            active[:, cols] = (up * lift).astype(BF16)
            slope = lift + 0.5 * up * (1.0 - bend * bend) * (root * (1.0 + 3.0 * 0.044715 * square))
            grad = (dact * slope).astype(BF16)
            for t in range(2):
                tile = 2 * s + t
                rg[up_tile(tile)] = grad[:, LANES * t : LANES * t + LANES]
        dup = jnp.concatenate([rg[up_tile(tile)] for tile in range(6)], axis=1)
        for s in range(3):
            cols = slice(256 * s, 256 * s + 256)
            acc[:, cols] += jnp.dot(active[...], w_out[slot, :, cols], preferred_element_type=F32)
            dthird[:, cols] += dot(dup, w_in[slot, cols, :], LAST)
        flipped = active[...].T
        for i in range(4):
            for k in range(4):
                rows = pl.ds(pl.multiple_of(48 * (2 * q + i // 2), 48), 48)
                lt[k, i % 2, rows, :] = flipped[192 * i + 48 * k : 192 * i + 48 * k + 48, :]
        return carry

    lax.fori_loop(0, 4, feed, 0)

    PIECES = (
        [(third, o_layer, 64, e, r) for e in range(2) for r in (0, 32)]
        + [(mem, o_memory, 128, e, r) for e in range(2) for r in (0, 32, 64, 96)]
        + [(x_in, o_input, 64, e, r) for e in range(2) for r in (0, 32)]
    )

    def piece(n, leaving):
        buf, out, rows, e, r = PIECES[n]
        which = 1 - y if leaving else y
        src = buf.at[pl.ds(pl.multiple_of(2 * e * rows + which * rows + r, 32), 32), :]
        dst = out.at[2 * y + e, r : r + 32, :]
        if not leaving:
            return pltpu.make_async_copy(src, dst, out_sem.at[n])
        return pltpu.make_async_remote_copy(
            src_ref=src, dst_ref=dst, send_sem=out_send.at[n], recv_sem=out_recv.at[n], device_id=across, device_id_type=MESH
        )

    def send(n):
        piece(n, True).start()
        piece(n, False).start()

    def tick(n):
        red.tick(n)
        if n:
            send(n - 1)

    tick(0)
    store_left(lt, 4, third[...].T)

    third[...] = (hidden2[...] + acc[...]).astype(BF16)

    sums = n_own.at[0]
    sums[...] = jnp.zeros(sums.shape, F32)

    def store_grad(rows, value):
        acc[rows, :] = value

    norm_backward(
        lambda rows: hidden2[rows, :], lambda rows: dthird[rows, :],
        lambda rows, v: store_grad(rows, og[rows, :].astype(F32) + v), norm_gain, sums, 2,
    )
    spread(5, acc)
    tick(1)
    store_left(lt, 5, ctx_cross[...].T)
    dc = active

    def context_grad(slot, weight):
        for n in range(3):
            rows = slice(256 * n, 256 * n + 256)
            dc[:, rows] = back(rg, (slot,), weight.at[rows, :]).astype(BF16)

    context_grad(5, w_cross)

    def cross_backward(p, carry):
        for e in range(2):
            rows, lanes = pair(e, p)
            dq, dk, dv = attend_back(qx[p, rows, :], kv[p, cross_rows(e), :], kv[6 + p, cross_rows(e), :], p_cross[6 * e + p], dc[rows, lanes])
            h, j, g = p // 3, p // 3, p % 3
            rg[8, rows, pl.ds(pl.multiple_of(256 * g + LANES * h, LANES), LANES)] = dq
            rg[column(6 + 7 * e + j, 0, g)] = dk
            rg[column(6 + 7 * e + j, 1, g)] = dv
        return carry

    tick(2)
    lax.fori_loop(0, 3, cross_backward, 0)
    tick(3)
    lax.fori_loop(3, 6, cross_backward, 0)

    store_left(lt, 6, mem[0:256, :].T)
    store_left(lt, 7, mem[256:512, :].T)

    def memory_rows(e):
        for n in range(3):
            rows = slice(256 * n, 256 * n + 256)
            mem[256 * e : 256 * e + 256, rows] = back(rg, (6 + 7 * e, 7 + 7 * e), w_kv.at[rows, :]).astype(BF16)

    memory_rows(0)
    tick(4)
    memory_rows(1)
    for n in range(3):
        rows = slice(256 * n, 256 * n + 256)
        dthird[:, rows] = back(rg, (8,), w_query.at[rows, :])
    tick(5)
    norm_backward(
        lambda rows: hidden1[rows, :], lambda rows: dthird[rows, :],
        lambda rows, v: store_grad(rows, acc[rows, :] + v), norm_gain, sums, 1,
    )
    spread(9, acc)
    context_grad(9, w_self)
    tick(6)
    store_left(lt, 8, second[...].T)
    store_left(lt, 9, ctx_self[...].T)
    store_left(lt, 10, first[...].T)

    def self_backward(p, carry):
        for e in range(2):
            rows, lanes = pair(e, p)
            dq, dk, dv = attend_back(qkv[p, rows, :], qkv[6 + p, rows, :], qkv[12 + p, rows, :], p_self[6 * e + p], dc[rows, lanes])
            for n, value in enumerate((dq, dk, dv)):
                tile = 6 * n + p
                h = tile // 9
                j = (tile % 9) // 3
                rg[10 + j, rows, pl.ds(pl.multiple_of(256 * (tile % 3) + LANES * h, LANES), LANES)] = value
        return carry

    lax.fori_loop(0, 3, self_backward, 0)
    tick(7)
    lax.fori_loop(3, 6, self_backward, 0)
    tick(8)
    for n in range(3):
        rows = slice(256 * n, 256 * n + 256)
        dthird[:, rows] = back(rg, (10, 11, 12), w_qkv.at[rows, :])
    tick(9)

    def store_input(rows, v):
        x_in[rows, :] = (acc[rows, :] + v).astype(BF16)

    norm_backward(
        lambda rows: x_in[rows, :].astype(F32), lambda rows: dthird[rows, :], store_input, norm_gain, sums, 0
    )

    def body(n, carry):
        red.tick(n)
        for j in range(6):
            @pl.when(n == 10 + j)
            def _():
                norm_step(j, at, n_own, n_got, n_send, n_recv)

        for k in range(9, 16):
            @pl.when(n == k + 1)
            def _():
                send(k)

        return carry

    lax.fori_loop(10, red.TICKS, body, 0)
    norm_out[...] = n_own[5]
    red.drain()
    for n in range(16):
        piece(n, True).wait()
        piece(n, False).wait()


def layer_call(args):
    anywhere = pl.BlockSpec(memory_space=pl.ANY)
    vmem = pl.BlockSpec(memory_space=pltpu.VMEM)
    rows = lambda width, kind=BF16: pltpu.VMEM((256, width), kind)
    return pl.pallas_call(
        layer_kernel,
        out_shape=(
            jax.ShapeDtypeStruct((4, 64, 768), BF16),
            jax.ShapeDtypeStruct((4, 64, 768), BF16),
            jax.ShapeDtypeStruct((4, 128, 768), BF16),
            jax.ShapeDtypeStruct((TRIPLES, 3, 48, 128), F32),
            jax.ShapeDtypeStruct((8, 768), F32),
        ),
        in_specs=[anywhere, anywhere, pl.BlockSpec(memory_space=pltpu.SMEM)] + [anywhere] * 8 + [vmem] * 2,
        out_specs=(anywhere, anywhere, anywhere, anywhere, vmem),
        scratch_shapes=[
            rows(768), pltpu.VMEM((512, 768), BF16), rows(768),
            pltpu.VMEM((768, 2304), BF16), pltpu.VMEM((768, 768), BF16), pltpu.VMEM((768, 768), BF16),
            pltpu.VMEM((768, 1536), BF16), pltpu.VMEM((768, 768), BF16),
            pltpu.VMEM((2, 768, 768), BF16), pltpu.VMEM((2, 768, 768), BF16),
            rows(768), pltpu.VMEM((18, 256, 128), BF16), pltpu.VMEM((12, 256, 128), BF16), rows(768),
            rows(768, F32), rows(768), pltpu.VMEM((6, 256, 128), BF16), pltpu.VMEM((12, 512, 128), BF16),
            pltpu.VMEM((12, 256, 256), BF16), rows(768), rows(768, F32), rows(768),
            rows(768), rows(768, F32), rows(768, F32),
            pltpu.VMEM((11, 2, 384, 256), BF16),
            pltpu.VMEM((15, 256, 768), BF16),
            pltpu.VMEM((6, 8, 768), F32),
            pltpu.VMEM((5, 8, 768), F32),
            pltpu.SemaphoreType.DMA((5,)),
            pltpu.SemaphoreType.DMA((5,)),
            pltpu.SemaphoreType.DMA((17,)),
            pltpu.SemaphoreType.DMA((3, 2)),
            pltpu.SemaphoreType.DMA((3, 2)),
            pltpu.SemaphoreType.DMA((16,)),
            pltpu.SemaphoreType.DMA((16,)),
            pltpu.SemaphoreType.DMA((16,)),
        ] + Reducer.SCRATCH,
        compiler_params=pltpu.CompilerParams(collective_id=0, has_side_effects=True, vmem_limit_bytes=61 << 20),
    )(*args)


WEIGHTS = ((13, 3), (12, 1), (11, 1), (9, 2), (8, 1), (4, 4))


def finish_kernel(layer, inputs, memories, units, norms, *refs):
    o_layer, o_input, o_memory = refs[0:3]
    o_weights, o_ffn_out, o_gain, o_bias = refs[3:9], refs[9], refs[10], refs[11]
    low_input, low_memory, high_input, high_memory, blocks = refs[12:17]
    w_bufs, ffn_buf, sem, out_sem, low_layer = refs[17:23], refs[23], refs[24], refs[25], refs[26]
    loads = [
        pltpu.make_async_copy(units, blocks, sem.at[0]),
        pltpu.make_async_copy(memories, low_memory, sem.at[1]),
        pltpu.make_async_copy(inputs, low_input, sem.at[2]),
        pltpu.make_async_copy(layer, low_layer, sem.at[3]),
    ]
    for load in loads:
        load.start()
    stores = []

    def store(src, dst):
        copy = pltpu.make_async_copy(src, dst, out_sem.at[len(stores)])
        copy.start()
        stores.append(copy)

    o_gain[...] = norms[0:3, :]
    o_bias[...] = norms[3:6, :]
    loads[0].wait()
    for (t, count), buf, out in zip(WEIGHTS, w_bufs, o_weights):
        for j in range(count):
            for g in range(3):
                buf[:, j * 384 + g * LANES : j * 384 + g * LANES + LANES] = blocks[t + j, g]
        store(buf, out)
    for k in range(4):
        for g in range(3):
            ffn_buf[48 * k : 48 * k + 48, g * LANES : g * LANES + LANES] = blocks[k, g]
    store(ffn_buf, o_ffn_out)
    loads[1].wait()
    for e in range(4):
        high_memory[e] = low_memory[e].astype(F32)
        store(high_memory.at[e], o_memory.at[e])
    loads[2].wait()
    high_input[...] = low_input[...].astype(F32)
    store(high_input, o_input)
    loads[3].wait()
    store(low_layer, o_layer)
    for copy in stores:
        copy.wait()


def finish_call(layer, inputs, memories, units, norms):
    anywhere = pl.BlockSpec(memory_space=pl.ANY)
    vmem = pl.BlockSpec(memory_space=pltpu.VMEM)
    widths = [count * 384 for _, count in WEIGHTS]
    return pl.pallas_call(
        finish_kernel,
        out_shape=(
            jax.ShapeDtypeStruct(layer.shape, BF16),
            jax.ShapeDtypeStruct(inputs.shape, F32),
            jax.ShapeDtypeStruct(memories.shape, F32),
            *[jax.ShapeDtypeStruct((48, w), F32) for w in widths],
            jax.ShapeDtypeStruct((192, 384), F32),
            jax.ShapeDtypeStruct((3, 768), F32),
            jax.ShapeDtypeStruct((3, 768), F32),
        ),
        in_specs=[anywhere] * 4 + [vmem],
        out_specs=(anywhere,) * 10 + (vmem, vmem),
        scratch_shapes=[
            pltpu.VMEM(inputs.shape, BF16), pltpu.VMEM(memories.shape, BF16),
            pltpu.VMEM(inputs.shape, F32), pltpu.VMEM(memories.shape, F32), pltpu.VMEM(units.shape, F32),
            *[pltpu.VMEM((48, w), F32) for w in widths], pltpu.VMEM((192, 384), F32),
            pltpu.SemaphoreType.DMA((4,)), pltpu.SemaphoreType.DMA((13,)), pltpu.VMEM(layer.shape, BF16),
        ],
        compiler_params=pltpu.CompilerParams(vmem_limit_bytes=60 << 20),
    )(layer, inputs, memories, units, norms)


def per_device_paired(*args):
    return finish_call(*layer_call(args))

def layer_norm(x, gain, shift):
    center = jnp.mean(x, axis=-1, keepdims=True)
    centered = x - center
    spread = jnp.mean(centered * centered, axis=-1, keepdims=True)
    return centered * lax.rsqrt(spread + 1e-05) * gain + shift


def smooth(v):
    return jax.nn.gelu(v, approximate=True)


def project(rows, weight):
    return jnp.einsum("etd,df->etf", rows, weight, preferred_element_type=jnp.float32)


def project_back(grads, weight):
    return jnp.einsum("etf,df->etd", grads, weight, preferred_element_type=jnp.float32)


def outer(rows, grads):
    return jnp.einsum("etd,etf->df", rows, grads, preferred_element_type=jnp.float32)


def outer_full(rows, grads):
    return jnp.einsum(
        "etd,etf->df", rows.astype(jnp.float32), grads, precision=lax.Precision.HIGHEST
    )


def back_full(grads, weight):
    return jnp.einsum(
        "etf,df->etd", grads, weight.astype(jnp.float32), precision=lax.Precision.HIGHEST
    )


def split_heads(queries, key_values):
    examples, rows, width = queries.shape
    count = key_values.shape[1]
    heads_q = queries.reshape(examples, rows, HEADS, HEAD_DIM)
    heads_k = key_values[:, :, :width].reshape(examples, count, HEADS, HEAD_DIM)
    heads_v = key_values[:, :, width:].reshape(examples, count, HEADS, HEAD_DIM)
    return (heads_q, heads_k, heads_v)


def masked_logits(heads_q, heads_k, allowed):
    scores = jnp.einsum("eqhd,ekhd->ehqk", heads_q, heads_k, preferred_element_type=jnp.float32)
    return jnp.where(allowed, scores * (1.0 / math.sqrt(HEAD_DIM)), -1e30)


def attend_forward(queries, key_values, allowed):
    examples, rows, width = queries.shape
    heads_q, heads_k, heads_v = split_heads(queries, key_values)
    logits = masked_logits(heads_q, heads_k, allowed)
    row_top = jnp.max(logits, axis=-1, keepdims=True)
    raised = jnp.where(allowed, jnp.exp(logits - row_top), 0.0)
    row_total = jnp.sum(raised, axis=-1, keepdims=True)
    weights = (raised / row_total).astype(jnp.bfloat16)
    context = jnp.einsum("ehqk,ekhd->eqhd", weights, heads_v, preferred_element_type=jnp.float32)
    return (
        context.reshape(examples, rows, width).astype(jnp.bfloat16),
        row_top + jnp.log(row_total),
    )


def attend_backward(queries, key_values, allowed, log_total, grad_context):
    examples, rows, width = queries.shape
    count = key_values.shape[1]
    heads_q, heads_k, heads_v = split_heads(queries, key_values)
    logits = masked_logits(heads_q, heads_k, allowed)
    soft = jnp.where(allowed, jnp.exp(logits - log_total), 0.0)
    grad_heads = grad_context.reshape(examples, rows, HEADS, HEAD_DIM)
    grad_soft = jnp.einsum(
        "eqhd,ekhd->ehqk", grad_heads, heads_v, preferred_element_type=jnp.float32
    )
    grad_values = jnp.einsum(
        "ehqk,eqhd->ekhd", soft.astype(jnp.bfloat16), grad_heads, preferred_element_type=jnp.float32
    )
    inner = jnp.sum(soft * grad_soft, axis=-1, keepdims=True)
    grad_scores = (soft * (grad_soft - inner) * (1.0 / math.sqrt(HEAD_DIM))).astype(jnp.bfloat16)
    grad_queries = jnp.einsum(
        "ehqk,ekhd->eqhd", grad_scores, heads_k, preferred_element_type=jnp.float32
    )
    grad_keys = jnp.einsum(
        "ehqk,eqhd->ekhd", grad_scores, heads_q, preferred_element_type=jnp.float32
    )
    joined = jnp.concatenate(
        [grad_keys.reshape(examples, count, width), grad_values.reshape(examples, count, width)],
        axis=2,
    )
    return (grad_queries.reshape(examples, rows, width), joined)


def per_device_wide(
    dec_input,
    memory,
    src_len,
    out_grad,
    self_qkv,
    self_out,
    cross_query,
    cross_kv,
    cross_out,
    ffn_in,
    ffn_out,
    norm_gain,
    norm_bias,
):
    examples, local_rows, width = dec_input.shape
    local_sources = memory.shape[1]
    seq_count = lax.axis_size("seq")
    all_targets = local_rows * seq_count
    all_sources = local_sources * seq_count
    rank = lax.axis_index("seq")
    x = dec_input.astype(jnp.float32)
    first_f, pull_first = jax.vjp(layer_norm, x, norm_gain[0], norm_bias[0])
    first = first_f.astype(jnp.bfloat16)
    projected = project(first, self_qkv).astype(jnp.bfloat16)
    self_queries = projected[:, :, :width]
    self_kv = lax.all_gather(projected[:, :, width:], "seq", axis=1, tiled=True)
    query_place = rank * local_rows + jnp.arange(local_rows, dtype=jnp.int32)
    key_place = jnp.arange(all_targets, dtype=jnp.int32)
    causal = (query_place[:, None] >= key_place[None, :])[None, None]
    self_context, self_total = attend_forward(self_queries, self_kv, causal)
    hidden1 = x + project(self_context, self_out)
    second_f, pull_second = jax.vjp(layer_norm, hidden1, norm_gain[1], norm_bias[1])
    second = second_f.astype(jnp.bfloat16)
    cross_queries = project(second, cross_query).astype(jnp.bfloat16)
    gathered = lax.all_gather(memory, "seq", axis=1, tiled=True)
    memory_kv = project(gathered, cross_kv).astype(jnp.bfloat16)
    source_place = jnp.arange(all_sources, dtype=jnp.int32)
    visible = (source_place[None, :] < src_len[:, None])[:, None, None, :]
    cross_context, cross_total = attend_forward(cross_queries, memory_kv, visible)
    hidden2 = hidden1 + project(cross_context, cross_out)
    third_f, pull_third = jax.vjp(layer_norm, hidden2, norm_gain[2], norm_bias[2])
    third = third_f.astype(jnp.bfloat16)
    raised_up = project(third, ffn_in)
    active_f, pull_smooth = jax.vjp(smooth, raised_up)
    activated = active_f.astype(jnp.bfloat16)
    layer_out = (hidden2 + project(activated, ffn_out)).astype(jnp.bfloat16)
    grad_out = out_grad.astype(jnp.float32)
    ffn_out_grad = outer(activated, out_grad)
    (grad_up,) = pull_smooth(project_back(out_grad, ffn_out))
    grad_up_low = grad_up.astype(jnp.bfloat16)
    ffn_in_grad = outer(third, grad_up_low)
    back_third, gain_third, bias_third = pull_third(project_back(grad_up_low, ffn_in))
    grad_hidden2 = grad_out + back_third
    cross_branch = grad_hidden2.astype(jnp.bfloat16)
    cross_out_grad = outer(cross_context, cross_branch)
    grad_cross_context = project_back(cross_branch, cross_out).astype(jnp.bfloat16)
    grad_cross_q, grad_memory_kv = attend_backward(
        cross_queries, memory_kv, visible, cross_total, grad_cross_context
    )
    local_kv_grad = lax.psum_scatter(
        grad_memory_kv.astype(jnp.bfloat16), "seq", scatter_dimension=1, tiled=True
    ).astype(jnp.float32)
    cross_kv_grad = outer_full(memory, local_kv_grad)
    memory_grad = back_full(local_kv_grad, cross_kv)
    grad_cross_low = grad_cross_q.astype(jnp.bfloat16)
    cross_query_grad = outer(second, grad_cross_low)
    back_second, gain_second, bias_second = pull_second(project_back(grad_cross_low, cross_query))
    grad_hidden1 = grad_hidden2 + back_second
    self_branch = grad_hidden1.astype(jnp.bfloat16)
    self_out_grad = outer(self_context, self_branch)
    grad_self_context = project_back(self_branch, self_out).astype(jnp.bfloat16)
    grad_self_q, grad_self_kv = attend_backward(
        self_queries, self_kv, causal, self_total, grad_self_context
    )
    local_self_kv = lax.psum_scatter(grad_self_kv, "seq", scatter_dimension=1, tiled=True)
    grad_projected = jnp.concatenate([grad_self_q, local_self_kv], axis=2).astype(jnp.bfloat16)
    self_qkv_grad = outer(first, grad_projected)
    back_first, gain_first, bias_first = pull_first(project_back(grad_projected, self_qkv))
    input_grad = grad_hidden1 + back_first
    gain_terms = jnp.stack([gain_first, gain_second, gain_third])
    bias_terms = jnp.stack([bias_first, bias_second, bias_third])
    gain_total, bias_total = lax.psum((gain_terms, bias_terms), ("dp", "seq"))
    partial_value = (
        lax.psum_scatter(
            self_qkv_grad.astype(jnp.bfloat16), "dp", scatter_dimension=0, tiled=True
        ).astype(jnp.float32),
        lax.psum_scatter(
            self_out_grad.astype(jnp.bfloat16), "dp", scatter_dimension=0, tiled=True
        ).astype(jnp.float32),
        lax.psum_scatter(
            cross_query_grad.astype(jnp.bfloat16), "dp", scatter_dimension=0, tiled=True
        ).astype(jnp.float32),
        lax.psum_scatter(
            cross_kv_grad.astype(jnp.bfloat16), "dp", scatter_dimension=0, tiled=True
        ).astype(jnp.float32),
        lax.psum_scatter(
            cross_out_grad.astype(jnp.bfloat16), "dp", scatter_dimension=0, tiled=True
        ).astype(jnp.float32),
        lax.psum_scatter(
            ffn_in_grad.astype(jnp.bfloat16), "dp", scatter_dimension=0, tiled=True
        ).astype(jnp.float32),
        lax.psum_scatter(
            ffn_out_grad.astype(jnp.bfloat16), "dp", scatter_dimension=0, tiled=True
        ).astype(jnp.float32),
    )
    finished = (
        lax.psum_scatter(
            partial_value[0].astype(jnp.bfloat16), "seq", scatter_dimension=1, tiled=True
        ).astype(jnp.float32),
        lax.psum_scatter(
            partial_value[1].astype(jnp.bfloat16), "seq", scatter_dimension=1, tiled=True
        ).astype(jnp.float32),
        lax.psum_scatter(
            partial_value[2].astype(jnp.bfloat16), "seq", scatter_dimension=1, tiled=True
        ).astype(jnp.float32),
        lax.psum_scatter(
            partial_value[3].astype(jnp.bfloat16), "seq", scatter_dimension=1, tiled=True
        ).astype(jnp.float32),
        lax.psum_scatter(
            partial_value[4].astype(jnp.bfloat16), "seq", scatter_dimension=1, tiled=True
        ).astype(jnp.float32),
        lax.psum_scatter(
            partial_value[5].astype(jnp.bfloat16), "seq", scatter_dimension=1, tiled=True
        ).astype(jnp.float32),
        lax.psum_scatter(
            partial_value[6].astype(jnp.bfloat16), "seq", scatter_dimension=1, tiled=True
        ).astype(jnp.float32),
    )
    return (
        layer_out,
        input_grad,
        memory_grad,
        finished[0],
        finished[1],
        finished[2],
        finished[3],
        finished[4],
        finished[5],
        finished[6],
        gain_total,
        bias_total,
    )


def solution(mesh):
    paired = mesh.shape["dp"] == 16 and mesh.shape["seq"] == 2
    per_device = per_device_paired if paired else per_device_wide
    in_specs = (
        P("dp", "seq", None),
        P("dp", "seq", None),
        P("dp"),
        P("dp", "seq", None),
        P(),
        P(),
        P(),
        P(),
        P(),
        P(),
        P(),
        P(),
        P(),
    )
    out_specs = (
        P("dp", "seq", None),
        P("dp", "seq", None),
        P("dp", "seq", None),
        P("dp", "seq"),
        P("dp", "seq"),
        P("dp", "seq"),
        P("dp", "seq"),
        P("dp", "seq"),
        P("dp", "seq"),
        P("dp", "seq"),
        P(),
        P(),
    )
    return jax.shard_map(
        per_device, mesh=mesh, in_specs=in_specs, out_specs=out_specs, check_vma=False
    )
```

```python
import functools
import math

import jax
import jax.numpy as jnp
from jax import lax
from jax.experimental import pallas as pl
from jax.experimental.pallas import tpu as pltpu
from jax.sharding import PartitionSpec as P

HEADS = 12
HEAD_DIM = 64
MESH = pl.DeviceIdType.MESH
F32 = jnp.float32
BF16 = jnp.bfloat16
TRIPLES = 16
ORDERS = (("x", "l", "y", "h"), ("y", "x", "l", "h"), ("l", "x", "y", "h"))


def place():
    i = lax.axis_index("dp")
    return {"c": i % 2, "x": (i // 2) % 2, "l": (i // 4) % 2, "h": i // 8, "y": lax.axis_index("seq")}


def partner(axis, at):
    i = lax.axis_index("dp")
    y = at["y"]
    if axis == "y":
        return (i, 1 - y)
    step = {"c": 1, "x": 2, "l": 4, "h": 8}[axis]
    return (i + step - 2 * step * at[axis], y)


def greet(at):
    barrier = pltpu.get_barrier_semaphore()
    for axis in ("c", "x", "l", "h", "y"):
        pl.semaphore_signal(barrier, inc=1, device_id=partner(axis, at), device_id_type=MESH)
    pl.semaphore_wait(barrier, 5)


LEFT = (4, 4, 4, 4, 0, 1, 2, 3, 5, 6, 6, 8, 9, 10, 10, 10)
RIGHT = (1, 2, 3, 4, 0, 0, 0, 0, 5, 6, 7, 8, 9, 10, 11, 12)


def look_up(table, t):
    if isinstance(t, int):
        return table[t]
    value = table[-1]
    for n in range(TRIPLES - 2, -1, -1):
        if table[n] != table[n + 1]:
            value = jnp.where(t <= n, table[n], value)
    return value


def when(condition):
    if isinstance(condition, bool):
        return (lambda body: body()) if condition else (lambda body: None)
    return pl.when(condition)


def negate(condition):
    return not condition if isinstance(condition, bool) else jnp.logical_not(condition)


def store_left(lt, slot, rows_by_feature):
    for i in range(16):
        lt[slot, i % 2, 48 * (i // 2) : 48 * (i // 2) + 48, :] = rows_by_feature[48 * i : 48 * i + 48, :]


class Reducer:
    LAGS = (0, 1, 3, 5, 7, 8)
    SLOTS = (2, 3, 3, 3, 3)
    TICKS = TRIPLES + 8
    SCRATCH = [
        pltpu.VMEM((2, 3, 384, 256), BF16),
        pltpu.VMEM((TRIPLES, 3, 384, 256), BF16),
        pltpu.VMEM((3, 3, 2, 2, 2, 2, 48, 128), BF16),
        pltpu.VMEM((TRIPLES, 3, 2, 2, 2, 48, 128), BF16),
        pltpu.VMEM((3, 3, 2, 2, 2, 48, 128), BF16),
        pltpu.VMEM((TRIPLES, 3, 2, 2, 48, 128), BF16),
        pltpu.VMEM((3, 3, 2, 2, 48, 128), BF16),
        pltpu.VMEM((TRIPLES, 3, 2, 48, 128), BF16),
        pltpu.VMEM((3, 3, 2, 48, 128), BF16),
        pltpu.VMEM((TRIPLES, 3, 48, 128), BF16),
        pltpu.VMEM((3, 3, 48, 128), F32),
        pltpu.SemaphoreType.DMA((3,)),
        pltpu.SemaphoreType.DMA((5, 3, 3)),
        pltpu.SemaphoreType.DMA((5, TRIPLES, 3)),
    ]

    def __init__(self, at, lt, rg, out, s0, r0, s1, r1, s2, r2, s3, r3, s4, r4, done, done_sem, send_sem, recv_sem):
        self.at, self.lt, self.rg, self.out = at, lt, rg, out
        self.sent, self.got = (s0, s1, s2, s3, s4), (r0, r1, r2, r3, r4)
        self.done, self.done_sem = done, done_sem
        self.send_sem, self.recv_sem = send_sem, recv_sem

    def axis(self, stage, g):
        return "c" if stage == 0 else ORDERS[g][stage - 1]

    def copy(self, stage, t, g):
        axis = self.axis(stage, g)
        slot = t % self.SLOTS[stage]
        src = self.sent[stage].at[slot, g]
        if stage:
            src = src.at[1 - self.at[axis]]
        return pltpu.make_async_remote_copy(
            src_ref=src,
            dst_ref=self.got[stage].at[t, g],
            send_sem=self.send_sem.at[stage, slot, g],
            recv_sem=self.recv_sem.at[stage, t, g],
            device_id=partner(axis, self.at),
            device_id_type=MESH,
        )

    def free(self, stage, t):
        slots = self.SLOTS[stage]

        @when(t >= slots)
        def _():
            for g in range(3):
                self.copy(stage, t - slots, g).wait_send()

    def product(self, t, half, g):
        cols = slice(256 * g, 256 * g + 256)
        return jnp.dot(self.lt[look_up(LEFT, t), half], self.rg[look_up(RIGHT, t), :, cols], preferred_element_type=F32)

    def first(self, t):
        self.free(0, t)
        half = 1 - self.at["c"]
        memory = (t == 9) | (t == 10)
        for g in range(3):
            cols = slice(256 * g, 256 * g + 256)

            @when(negate(memory))
            def _():
                self.sent[0][t % 2, g] = self.product(t, half, g).astype(BF16)

            @when(memory)
            def _():
                more = jnp.dot(self.lt[7, half], self.rg[t + 4, :, cols], preferred_element_type=F32)
                self.sent[0][t % 2, g] = (self.product(t, half, g) + more).astype(BF16)

            self.copy(0, t, g).start()

    def second(self, t):
        self.free(1, t)
        half = self.at["c"]
        memory = (t == 9) | (t == 10)
        for g in range(3):
            cols = slice(256 * g, 256 * g + 256)
            self.copy(0, t, g).wait_recv()

            def spread(total):
                order = ORDERS[g]
                for b in range(8):
                    bits = {"h": b // 4, "l": (b // 2) % 2, "x": b % 2}
                    for y in range(2):
                        bits["y"] = y
                        where = tuple(bits[a] for a in order)
                        self.sent[1][(t % self.SLOTS[1], g) + where] = total[48 * b : 48 * b + 48, 128 * y : 128 * y + 128].astype(BF16)

            @when(negate(memory))
            def _():
                spread(self.product(t, half, g) + self.got[0][t, g].astype(F32))

            @when(memory)
            def _():
                more = jnp.dot(self.lt[7, half], self.rg[t + 4, :, cols], preferred_element_type=F32)
                spread(self.product(t, half, g) + more + self.got[0][t, g].astype(F32))

            self.copy(1, t, g).start()

    def write(self, t):
        return pltpu.make_async_copy(self.done.at[t % 3], self.out.at[t], self.done_sem.at[t % 3])

    def onward(self, stage, t):
        if stage < 5:
            self.free(stage, t)
        else:

            @when(t >= 3)
            def _():
                self.write(t - 3).wait()

        for g in range(3):
            self.copy(stage - 1, t, g).wait_recv()
            own = self.sent[stage - 1][t % self.SLOTS[stage - 1], g, self.at[self.axis(stage - 1, g)]]
            total = own.astype(F32) + self.got[stage - 1][t, g].astype(F32)
            if stage < 5:
                self.sent[stage][t % self.SLOTS[stage], g] = total.astype(BF16)
                self.copy(stage, t, g).start()
            else:
                self.done[t % 3, g] = total
        if stage == 5:
            self.write(t).start()

    def tick(self, n):
        for stage in range(6):
            t = n - self.LAGS[stage]

            @when((t >= 0) & (t < TRIPLES))
            def _():
                if stage == 0:
                    self.first(t)
                elif stage == 1:
                    self.second(t)
                else:
                    self.onward(stage, t)

    def drain(self):
        for t in range(TRIPLES - 3, TRIPLES):
            self.write(t).wait()
        for stage in range(5):
            for t in range(TRIPLES - self.SLOTS[stage], TRIPLES):
                for g in range(3):
                    self.copy(stage, t, g).wait_send()


NORM_ORDER = ("c", "x", "y", "l", "h")


def norm_copy(j, at, own, got, send_sem, recv_sem):
    return pltpu.make_async_remote_copy(
        src_ref=own.at[j], dst_ref=got.at[j], send_sem=send_sem.at[j], recv_sem=recv_sem.at[j],
        device_id=partner(NORM_ORDER[j], at), device_id_type=MESH,
    )


def norm_step(j, at, own, got, send_sem, recv_sem):
    if j:
        norm_copy(j - 1, at, own, got, send_sem, recv_sem).wait()
        own[j] = own[j - 1] + got[j - 1]
    if j < 5:
        norm_copy(j, at, own, got, send_sem, recv_sem).start()


LANES = 128


def normed(v):
    center = jnp.mean(v, axis=-1, keepdims=True)
    centered = v - center
    spread = jnp.mean(centered * centered, axis=-1, keepdims=True)
    scale = lax.rsqrt(spread + 1e-05)
    return centered * scale, scale


def row_blocks(step, body):
    for b in range(256 // step):
        body(slice(b * step, b * step + step))


def norm_forward(load, out, norm_gain, norm_bias, k):
    def body(rows):
        hat, _ = normed(load(rows))
        out[rows, :] = (hat * norm_gain[k : k + 1, :] + norm_bias[k : k + 1, :]).astype(BF16)

    row_blocks(64, body)


def norm_backward(load, load_grad, store, norm_gain, sums, k):
    def body(rows):
        hat, scale = normed(load(rows))
        dy = load_grad(rows)
        sums[k : k + 1, :] += jnp.sum(dy * hat, axis=0, keepdims=True)
        sums[k + 3 : k + 4, :] += jnp.sum(dy, axis=0, keepdims=True)
        dhat = dy * norm_gain[k : k + 1, :]
        mean = jnp.mean(dhat, axis=-1, keepdims=True)
        along = jnp.mean(dhat * hat, axis=-1, keepdims=True)
        store(rows, scale * (dhat - mean - hat * along))

    row_blocks(64, body)


def two_heads(tile):
    first = lax.broadcasted_iota(jnp.int32, tile.shape, 1) < HEAD_DIM
    zero = jnp.zeros_like(tile)
    return jnp.concatenate([jnp.where(first, tile, zero), jnp.where(first, zero, tile)], axis=0)


def upright(sideways):
    rows = sideways.shape[1] // 2
    own = jnp.concatenate([sideways[:HEAD_DIM, :rows], sideways[HEAD_DIM:, rows:]], axis=0)
    return own.T


def dot(a, b, over):
    return lax.dot_general(a, b, (over, ((), ())), preferred_element_type=F32)


LAST = ((1,), (1,))
PLAIN = ((1,), (0,))
ROWS = ((0,), (0,))


def attend(items):
    scores = [jnp.where(allowed, dot(k, two_heads(q), LAST), -1e30) for q, k, _, allowed in items]
    raised = [jnp.exp(s - jnp.max(s, axis=0, keepdims=True)) for s in scores]
    weights = [(r * (1.0 / jnp.sum(r, axis=0, keepdims=True))).astype(BF16) for r in raised]
    contexts = [upright(dot(item[2], w, ROWS).astype(BF16)) for w, item in zip(weights, items)]
    return list(zip(weights, contexts))


def attend_back(items):
    stacked = [two_heads(item[4]) for item in items]
    dweights = [dot(item[2], s, LAST) for item, s in zip(items, stacked)]
    dvs = [dot(item[3], s, PLAIN).astype(BF16) for item, s in zip(items, stacked)]
    dscores = []
    for item, d in zip(items, dweights):
        probs = item[3].astype(F32)
        terms = probs * d
        dscores.append((terms - probs * jnp.sum(terms, axis=0, keepdims=True)).astype(BF16))
    dqs = [upright((dot(item[1], d, ROWS) * (1.0 / math.sqrt(HEAD_DIM))).astype(BF16)) for item, d in zip(items, dscores)]
    dks = [dot(d, two_heads(item[0]), PLAIN).astype(BF16) for item, d in zip(items, dscores)]
    return list(zip(dqs, dks, dvs))


def in_groups(pairs, size, body):
    for n in range(0, len(pairs), size):
        body(pairs[n : n + size])


def column(slot, h, g):
    return (slot, slice(None), pl.ds(pl.multiple_of(256 * g + LANES * h, LANES), LANES))


def back(rg, slots, weight, rows=None):
    half = weight.shape[1] // 2
    total = None
    for j, slot in enumerate(slots):
        for g in range(3):
            at = j * 384 + g * LANES
            w = jnp.concatenate([weight[:, at : at + LANES], weight[:, half + at : half + at + LANES]], axis=1)
            term = dot(rg[slot, :, 256 * g : 256 * g + 256], w, LAST)
            total = term if total is None else total + term
    return total


def layer_kernel(
    dec_input, memory, src_len, out_grad, self_qkv, self_out, cross_query, cross_kv, cross_out, ffn_in, ffn_out,
    norm_gain, norm_bias,
    o_layer, o_input, o_memory, units, norm_out,
    x_in, mem, og, w_qkv, w_self, w_query, w_kv, w_cross, w_in, w_out,
    first, qkv, p_self, ctx_self, hidden1, second, qx, kv, p_cross, ctx_cross, hidden2, third,
    active, acc, dthird,
    lt, rg, n_own, n_got, n_send, n_recv, load_sem, swap_send, swap_recv, out_sem, out_send, out_recv, *rest
):
    at = place()
    y = at["y"]
    red = Reducer(at, lt, rg, units, *rest)
    across = partner("y", at)

    loads = [
        pltpu.make_async_copy(src, dst, load_sem.at[n])
        for n, (src, dst) in enumerate(
            ((self_qkv, w_qkv), (self_out, w_self), (cross_kv, w_kv), (cross_query, w_query), (cross_out, w_cross))
        )
    ]
    for load in loads:
        load.start()

    def ffn_load(n):
        slot = n % 2
        q = (n % 2) * 2 + n // 2
        cols = pl.ds(pl.multiple_of(q * 768, 768), 768)
        return (
            pltpu.make_async_copy(ffn_in.at[:, cols], w_in.at[slot], load_sem.at[7 + slot]),
            pltpu.make_async_copy(ffn_out.at[cols, :], w_out.at[slot], load_sem.at[9 + slot]),
        )

    for load in ffn_load(0):
        load.start()

    def own_rows(n, src, dst, rows):
        return [
            pltpu.make_async_copy(
                src.at[2 * y + e], dst.at[pl.ds(pl.multiple_of(2 * e * rows + y * rows, rows), rows), :], load_sem.at[11 + 2 * n + e]
            )
            for e in range(2)
        ]

    def swap(n, src, dst, rows):
        return [
            pltpu.make_async_remote_copy(
                src_ref=src.at[2 * (1 - y) + e],
                dst_ref=dst.at[pl.ds(pl.multiple_of(2 * e * rows + y * rows, rows), rows), :],
                send_sem=swap_send.at[n, e], recv_sem=swap_recv.at[n, e], device_id=across, device_id_type=MESH,
            )
            for e in range(2)
        ]

    moved = ((dec_input, x_in, 64), (memory, mem, 128), (out_grad, og, 64))
    owns = [own_rows(n, *m) for n, m in enumerate(moved)]
    swaps = [swap(n, *m) for n, m in enumerate(moved)]
    for own in owns:
        for copy in own:
            copy.start()
    greet(at)
    for copy in swaps[0]:
        copy.start()

    def arrived(n):
        for copy in owns[n]:
            copy.wait()
        for copy in swaps[n]:
            copy.wait()
        if n < 2:
            for copy in swaps[n + 1]:
                copy.start()

    scale = 1.0 / math.sqrt(HEAD_DIM)

    arrived(0)
    norm_forward(lambda rows: x_in[rows, :].astype(F32), first, norm_gain, norm_bias, 0)
    loads[0].wait()

    for n in range(9):
        out = jnp.dot(first[...], w_qkv[:, 256 * n : 256 * n + 256], preferred_element_type=F32)
        out = (out * scale if n < 3 else out).astype(BF16)
        qkv[2 * n] = out[:, 0:LANES]
        qkv[2 * n + 1] = out[:, LANES:256]

    def pair(e, p):
        return slice(e * 128, e * 128 + 128), slice(p * LANES, p * LANES + LANES)

    pairs = [(e, p) for p in range(6) for e in range(2)]

    def self_operands(e, p):
        rows, _ = pair(e, p)
        return qkv[p, rows, :], qkv[6 + p, rows, :], qkv[12 + p, rows, :]

    def self_forward(group):
        k_at = lax.broadcasted_iota(jnp.int32, (128, 256), 0)
        q_at = lax.broadcasted_iota(jnp.int32, (128, 256), 1) % 128
        results = attend([(*self_operands(e, p), q_at >= k_at) for e, p in group])
        for (e, p), (weights, context) in zip(group, results):
            p_self[6 * e + p] = weights
            ctx_self[pair(e, p)] = context

    in_groups(pairs, 4, self_forward)

    loads[1].wait()
    for n in range(3):
        cols = slice(256 * n, 256 * n + 256)
        hidden1[:, cols] = x_in[:, cols].astype(F32) + jnp.dot(ctx_self[...], w_self[:, cols], preferred_element_type=F32)
    norm_forward(lambda rows: hidden1[rows, :], second, norm_gain, norm_bias, 1)

    loads[3].wait()
    for n in range(3):
        out = jnp.dot(second[...], w_query[:, 256 * n : 256 * n + 256], preferred_element_type=F32)
        out = (out * scale).astype(BF16)
        qx[2 * n] = out[:, 0:LANES]
        qx[2 * n + 1] = out[:, LANES:256]
    loads[2].wait()
    arrived(1)

    for n in range(6):
        out = jnp.dot(mem[...], w_kv[:, 256 * n : 256 * n + 256], preferred_element_type=F32).astype(BF16)
        kv[2 * n] = out[:, 0:LANES]
        kv[2 * n + 1] = out[:, LANES:256]

    def cross_operands(e, p):
        rows, keys = pair(e, p)[0], slice(e * 256, e * 256 + 256)
        return qx[p, rows, :], kv[p, keys, :], kv[6 + p, keys, :]

    def cross_forward(group):
        k_at = lax.broadcasted_iota(jnp.int32, (256, 256), 0)
        results = attend([(*cross_operands(e, p), k_at < src_len[2 * y + e]) for e, p in group])
        for (e, p), (weights, context) in zip(group, results):
            p_cross[6 * e + p] = weights
            ctx_cross[pair(e, p)] = context

    in_groups(pairs, 4, cross_forward)

    loads[4].wait()
    for n in range(3):
        cols = slice(256 * n, 256 * n + 256)
        hidden2[:, cols] = hidden1[:, cols] + jnp.dot(ctx_cross[...], w_cross[:, cols], preferred_element_type=F32)
    norm_forward(lambda rows: hidden2[rows, :], third, norm_gain, norm_bias, 2)

    arrived(2)

    def spread(slot, rows_of):
        for g in range(3):
            for h in range(2):
                lane = h * 384 + g * LANES
                rg[slot, :, 256 * g + LANES * h : 256 * g + LANES * h + LANES] = rows_of[:, lane : lane + LANES].astype(BF16)

    spread(0, og)
    acc[...] = jnp.zeros_like(acc)
    dthird[...] = jnp.zeros_like(dthird)
    root = math.sqrt(2.0 / math.pi)

    def feed(n, carry):
        slot = n % 2
        q = (n % 2) * 2 + n // 2

        @pl.when(n < 3)
        def _():
            for load in ffn_load(n + 1):
                load.start()

        for load in ffn_load(n):
            load.wait()

        def up_tile(tile):
            return column(1 + (q % 2) * 2 + tile // 3, q // 2, tile % 3)

        for s in range(3):
            cols = slice(256 * s, 256 * s + 256)
            up = jnp.dot(third[...], w_in[slot, :, cols], preferred_element_type=F32)
            dact = dot(og[...], w_out[slot, cols, :], LAST)
            square = up * up
            bend = jnp.tanh(root * up * (1.0 + 0.044715 * square))
            lift = 0.5 * (1.0 + bend)
            active[:, cols] = (up * lift).astype(BF16)
            slope = lift + 0.5 * up * (1.0 - bend * bend) * (root * (1.0 + 3.0 * 0.044715 * square))
            grad = (dact * slope).astype(BF16)
            for t in range(2):
                tile = 2 * s + t
                rg[up_tile(tile)] = grad[:, LANES * t : LANES * t + LANES]
        dup = jnp.concatenate([rg[up_tile(tile)] for tile in range(6)], axis=1)
        for s in range(3):
            cols = slice(256 * s, 256 * s + 256)
            acc[:, cols] += jnp.dot(active[...], w_out[slot, :, cols], preferred_element_type=F32)
            dthird[:, cols] += dot(dup, w_in[slot, cols, :], LAST)
        flipped = active[...].T
        for i in range(4):
            for k in range(4):
                rows = pl.ds(pl.multiple_of(48 * (2 * q + i // 2), 48), 48)
                lt[k, i % 2, rows, :] = flipped[192 * i + 48 * k : 192 * i + 48 * k + 48, :]
        return carry

    PIECES = (
        [(third, o_layer, 64, e, r) for e in range(2) for r in (0, 32)]
        + [(mem, o_memory, 128, e, r) for e in range(2) for r in (0, 32, 64, 96)]
        + [(x_in, o_input, 64, e, r) for e in range(2) for r in (0, 32)]
    )

    def piece(n, leaving):
        buf, out, rows, e, r = PIECES[n]
        which = 1 - y if leaving else y
        src = buf.at[pl.ds(pl.multiple_of(2 * e * rows + which * rows + r, 32), 32), :]
        dst = out.at[2 * y + e, r : r + 32, :]
        if not leaving:
            return pltpu.make_async_copy(src, dst, out_sem.at[n])
        return pltpu.make_async_remote_copy(
            src_ref=src, dst_ref=dst, send_sem=out_send.at[n], recv_sem=out_recv.at[n], device_id=across, device_id_type=MESH
        )

    def send(n):
        piece(n, True).start()
        piece(n, False).start()

    def tick(n):
        red.tick(n)
        if n >= 3:
            send(n - 3)

    lax.fori_loop(0, 2, feed, 0)
    store_left(lt, 4, third[...].T)
    tick(0)
    tick(1)
    lax.fori_loop(2, 4, feed, 0)
    tick(2)

    third[...] = (hidden2[...] + acc[...]).astype(BF16)

    sums = n_own.at[0]
    sums[...] = jnp.zeros(sums.shape, F32)

    def store_grad(rows, value):
        acc[rows, :] = value

    norm_backward(
        lambda rows: hidden2[rows, :], lambda rows: dthird[rows, :],
        lambda rows, v: store_grad(rows, og[rows, :].astype(F32) + v), norm_gain, sums, 2,
    )
    spread(5, acc)
    tick(3)
    store_left(lt, 5, ctx_cross[...].T)
    dc = active

    def context_grad(slot, weight):
        for n in range(3):
            rows = slice(256 * n, 256 * n + 256)
            dc[:, rows] = back(rg, (slot,), weight.at[rows, :]).astype(BF16)

    context_grad(5, w_cross)

    def cross_backward(group):
        results = attend_back([(*cross_operands(e, p), p_cross[6 * e + p], dc[pair(e, p)]) for e, p in group])
        for (e, p), (dq, dk, dv) in zip(group, results):
            j, g = p // 3, p % 3
            rg[8, pair(e, p)[0], 256 * g + LANES * j : 256 * g + LANES * j + LANES] = dq
            rg[6 + 7 * e + j, :, 256 * g : 256 * g + LANES] = dk
            rg[6 + 7 * e + j, :, 256 * g + LANES : 256 * g + 256] = dv

    tick(4)
    in_groups(pairs[:6], 3, cross_backward)
    tick(5)
    in_groups(pairs[6:], 3, cross_backward)

    store_left(lt, 6, mem[0:256, :].T)
    store_left(lt, 7, mem[256:512, :].T)

    def memory_rows(e):
        for n in range(3):
            rows = slice(256 * n, 256 * n + 256)
            mem[256 * e : 256 * e + 256, rows] = back(rg, (6 + 7 * e, 7 + 7 * e), w_kv.at[rows, :]).astype(BF16)

    memory_rows(0)
    tick(6)
    memory_rows(1)
    for n in range(3):
        rows = slice(256 * n, 256 * n + 256)
        dthird[:, rows] = back(rg, (8,), w_query.at[rows, :])
    tick(7)
    norm_backward(
        lambda rows: hidden1[rows, :], lambda rows: dthird[rows, :],
        lambda rows, v: store_grad(rows, acc[rows, :] + v), norm_gain, sums, 1,
    )
    spread(9, acc)
    context_grad(9, w_self)
    tick(8)
    store_left(lt, 8, second[...].T)
    store_left(lt, 9, ctx_self[...].T)
    store_left(lt, 10, first[...].T)

    def self_backward(group):
        results = attend_back([(*self_operands(e, p), p_self[6 * e + p], dc[pair(e, p)]) for e, p in group])
        for (e, p), values in zip(group, results):
            for n, value in enumerate(values):
                tile = 6 * n + p
                lane = 256 * (tile % 3) + LANES * (tile // 9)
                rg[10 + (tile % 9) // 3, pair(e, p)[0], lane : lane + LANES] = value

    in_groups(pairs[:6], 3, self_backward)
    tick(9)
    in_groups(pairs[6:], 3, self_backward)
    tick(10)
    for n in range(3):
        rows = slice(256 * n, 256 * n + 256)
        dthird[:, rows] = back(rg, (10, 11, 12), w_qkv.at[rows, :])
    tick(11)

    def store_input(rows, v):
        x_in[rows, :] = (acc[rows, :] + v).astype(BF16)

    norm_backward(
        lambda rows: x_in[rows, :].astype(F32), lambda rows: dthird[rows, :], store_input, norm_gain, sums, 0
    )

    def body(n, carry):
        red.tick(n)
        for j in range(6):
            @pl.when(n == 12 + j)
            def _():
                norm_step(j, at, n_own, n_got, n_send, n_recv)

        for k in range(9, 16):
            @pl.when(n == k + 3)
            def _():
                send(k)

        return carry

    lax.fori_loop(12, red.TICKS, body, 0)
    norm_out[...] = n_own[5]
    red.drain()
    for n in range(16):
        piece(n, True).wait()
        piece(n, False).wait()


def layer_call(args):
    anywhere = pl.BlockSpec(memory_space=pl.ANY)
    vmem = pl.BlockSpec(memory_space=pltpu.VMEM)
    rows = lambda width, kind=BF16: pltpu.VMEM((256, width), kind)
    return pl.pallas_call(
        layer_kernel,
        out_shape=(
            jax.ShapeDtypeStruct((4, 64, 768), BF16),
            jax.ShapeDtypeStruct((4, 64, 768), BF16),
            jax.ShapeDtypeStruct((4, 128, 768), BF16),
            jax.ShapeDtypeStruct((TRIPLES, 3, 48, 128), F32),
            jax.ShapeDtypeStruct((8, 768), F32),
        ),
        in_specs=[anywhere, anywhere, pl.BlockSpec(memory_space=pltpu.SMEM)] + [anywhere] * 8 + [vmem] * 2,
        out_specs=(anywhere, anywhere, anywhere, anywhere, vmem),
        scratch_shapes=[
            rows(768), pltpu.VMEM((512, 768), BF16), rows(768),
            pltpu.VMEM((768, 2304), BF16), pltpu.VMEM((768, 768), BF16), pltpu.VMEM((768, 768), BF16),
            pltpu.VMEM((768, 1536), BF16), pltpu.VMEM((768, 768), BF16),
            pltpu.VMEM((2, 768, 768), BF16), pltpu.VMEM((2, 768, 768), BF16),
            rows(768), pltpu.VMEM((18, 256, 128), BF16), pltpu.VMEM((12, 128, 256), BF16), rows(768),
            rows(768, F32), rows(768), pltpu.VMEM((6, 256, 128), BF16), pltpu.VMEM((12, 512, 128), BF16),
            pltpu.VMEM((12, 256, 256), BF16), rows(768), rows(768, F32), rows(768),
            rows(768), rows(768, F32), rows(768, F32),
            pltpu.VMEM((11, 2, 384, 256), BF16),
            pltpu.VMEM((15, 256, 768), BF16),
            pltpu.VMEM((6, 8, 768), F32),
            pltpu.VMEM((5, 8, 768), F32),
            pltpu.SemaphoreType.DMA((5,)),
            pltpu.SemaphoreType.DMA((5,)),
            pltpu.SemaphoreType.DMA((17,)),
            pltpu.SemaphoreType.DMA((3, 2)),
            pltpu.SemaphoreType.DMA((3, 2)),
            pltpu.SemaphoreType.DMA((16,)),
            pltpu.SemaphoreType.DMA((16,)),
            pltpu.SemaphoreType.DMA((16,)),
        ] + Reducer.SCRATCH,
        compiler_params=pltpu.CompilerParams(collective_id=0, has_side_effects=True, vmem_limit_bytes=61 << 20),
    )(*args)


WEIGHTS = ((13, 3), (12, 1), (11, 1), (9, 2), (8, 1), (0, 4))


def finish_kernel(layer, inputs, memories, units, norms, *refs):
    o_layer, o_input, o_memory = refs[0:3]
    o_weights, o_ffn_out, o_gain, o_bias = refs[3:9], refs[9], refs[10], refs[11]
    low_input, low_memory, high_input, high_memory, blocks = refs[12:17]
    w_bufs, ffn_buf, sem, out_sem, low_layer = refs[17:23], refs[23], refs[24], refs[25], refs[26]
    loads = [
        pltpu.make_async_copy(units, blocks, sem.at[0]),
        pltpu.make_async_copy(memories, low_memory, sem.at[1]),
        pltpu.make_async_copy(inputs, low_input, sem.at[2]),
        pltpu.make_async_copy(layer, low_layer, sem.at[3]),
    ]
    for load in loads:
        load.start()
    stores = []

    def store(src, dst):
        copy = pltpu.make_async_copy(src, dst, out_sem.at[len(stores)])
        copy.start()
        stores.append(copy)

    o_gain[...] = norms[0:3, :]
    o_bias[...] = norms[3:6, :]
    loads[0].wait()
    for (t, count), buf, out in zip(WEIGHTS, w_bufs, o_weights):
        for j in range(count):
            for g in range(3):
                buf[:, j * 384 + g * LANES : j * 384 + g * LANES + LANES] = blocks[t + j, g]
        store(buf, out)
    for k in range(4):
        for g in range(3):
            ffn_buf[48 * k : 48 * k + 48, g * LANES : g * LANES + LANES] = blocks[4 + k, g]
    store(ffn_buf, o_ffn_out)
    loads[1].wait()
    for e in range(4):
        high_memory[e] = low_memory[e].astype(F32)
        store(high_memory.at[e], o_memory.at[e])
    loads[2].wait()
    high_input[...] = low_input[...].astype(F32)
    store(high_input, o_input)
    loads[3].wait()
    store(low_layer, o_layer)
    for copy in stores:
        copy.wait()


def finish_call(layer, inputs, memories, units, norms):
    anywhere = pl.BlockSpec(memory_space=pl.ANY)
    vmem = pl.BlockSpec(memory_space=pltpu.VMEM)
    widths = [count * 384 for _, count in WEIGHTS]
    return pl.pallas_call(
        finish_kernel,
        out_shape=(
            jax.ShapeDtypeStruct(layer.shape, BF16),
            jax.ShapeDtypeStruct(inputs.shape, F32),
            jax.ShapeDtypeStruct(memories.shape, F32),
            *[jax.ShapeDtypeStruct((48, w), F32) for w in widths],
            jax.ShapeDtypeStruct((192, 384), F32),
            jax.ShapeDtypeStruct((3, 768), F32),
            jax.ShapeDtypeStruct((3, 768), F32),
        ),
        in_specs=[anywhere] * 4 + [vmem],
        out_specs=(anywhere,) * 10 + (vmem, vmem),
        scratch_shapes=[
            pltpu.VMEM(inputs.shape, BF16), pltpu.VMEM(memories.shape, BF16),
            pltpu.VMEM(inputs.shape, F32), pltpu.VMEM(memories.shape, F32), pltpu.VMEM(units.shape, F32),
            *[pltpu.VMEM((48, w), F32) for w in widths], pltpu.VMEM((192, 384), F32),
            pltpu.SemaphoreType.DMA((4,)), pltpu.SemaphoreType.DMA((13,)), pltpu.VMEM(layer.shape, BF16),
        ],
        compiler_params=pltpu.CompilerParams(vmem_limit_bytes=60 << 20),
    )(layer, inputs, memories, units, norms)


def per_device_paired(*args):
    return finish_call(*layer_call(args))

def layer_norm(x, gain, shift):
    center = jnp.mean(x, axis=-1, keepdims=True)
    centered = x - center
    spread = jnp.mean(centered * centered, axis=-1, keepdims=True)
    return centered * lax.rsqrt(spread + 1e-05) * gain + shift


def smooth(v):
    return jax.nn.gelu(v, approximate=True)


def project(rows, weight):
    return jnp.einsum("etd,df->etf", rows, weight, preferred_element_type=jnp.float32)


def project_back(grads, weight):
    return jnp.einsum("etf,df->etd", grads, weight, preferred_element_type=jnp.float32)


def outer(rows, grads):
    return jnp.einsum("etd,etf->df", rows, grads, preferred_element_type=jnp.float32)


def outer_full(rows, grads):
    return jnp.einsum(
        "etd,etf->df", rows.astype(jnp.float32), grads, precision=lax.Precision.HIGHEST
    )


def back_full(grads, weight):
    return jnp.einsum(
        "etf,df->etd", grads, weight.astype(jnp.float32), precision=lax.Precision.HIGHEST
    )


def split_heads(queries, key_values):
    examples, rows, width = queries.shape
    count = key_values.shape[1]
    heads_q = queries.reshape(examples, rows, HEADS, HEAD_DIM)
    heads_k = key_values[:, :, :width].reshape(examples, count, HEADS, HEAD_DIM)
    heads_v = key_values[:, :, width:].reshape(examples, count, HEADS, HEAD_DIM)
    return (heads_q, heads_k, heads_v)


def masked_logits(heads_q, heads_k, allowed):
    scores = jnp.einsum("eqhd,ekhd->ehqk", heads_q, heads_k, preferred_element_type=jnp.float32)
    return jnp.where(allowed, scores * (1.0 / math.sqrt(HEAD_DIM)), -1e30)


def attend_forward(queries, key_values, allowed):
    examples, rows, width = queries.shape
    heads_q, heads_k, heads_v = split_heads(queries, key_values)
    logits = masked_logits(heads_q, heads_k, allowed)
    row_top = jnp.max(logits, axis=-1, keepdims=True)
    raised = jnp.where(allowed, jnp.exp(logits - row_top), 0.0)
    row_total = jnp.sum(raised, axis=-1, keepdims=True)
    weights = (raised / row_total).astype(jnp.bfloat16)
    context = jnp.einsum("ehqk,ekhd->eqhd", weights, heads_v, preferred_element_type=jnp.float32)
    return (
        context.reshape(examples, rows, width).astype(jnp.bfloat16),
        row_top + jnp.log(row_total),
    )


def attend_backward(queries, key_values, allowed, log_total, grad_context):
    examples, rows, width = queries.shape
    count = key_values.shape[1]
    heads_q, heads_k, heads_v = split_heads(queries, key_values)
    logits = masked_logits(heads_q, heads_k, allowed)
    soft = jnp.where(allowed, jnp.exp(logits - log_total), 0.0)
    grad_heads = grad_context.reshape(examples, rows, HEADS, HEAD_DIM)
    grad_soft = jnp.einsum(
        "eqhd,ekhd->ehqk", grad_heads, heads_v, preferred_element_type=jnp.float32
    )
    grad_values = jnp.einsum(
        "ehqk,eqhd->ekhd", soft.astype(jnp.bfloat16), grad_heads, preferred_element_type=jnp.float32
    )
    inner = jnp.sum(soft * grad_soft, axis=-1, keepdims=True)
    grad_scores = (soft * (grad_soft - inner) * (1.0 / math.sqrt(HEAD_DIM))).astype(jnp.bfloat16)
    grad_queries = jnp.einsum(
        "ehqk,ekhd->eqhd", grad_scores, heads_k, preferred_element_type=jnp.float32
    )
    grad_keys = jnp.einsum(
        "ehqk,eqhd->ekhd", grad_scores, heads_q, preferred_element_type=jnp.float32
    )
    joined = jnp.concatenate(
        [grad_keys.reshape(examples, count, width), grad_values.reshape(examples, count, width)],
        axis=2,
    )
    return (grad_queries.reshape(examples, rows, width), joined)


def per_device_wide(
    dec_input,
    memory,
    src_len,
    out_grad,
    self_qkv,
    self_out,
    cross_query,
    cross_kv,
    cross_out,
    ffn_in,
    ffn_out,
    norm_gain,
    norm_bias,
):
    examples, local_rows, width = dec_input.shape
    local_sources = memory.shape[1]
    seq_count = lax.axis_size("seq")
    all_targets = local_rows * seq_count
    all_sources = local_sources * seq_count
    rank = lax.axis_index("seq")
    x = dec_input.astype(jnp.float32)
    first_f, pull_first = jax.vjp(layer_norm, x, norm_gain[0], norm_bias[0])
    first = first_f.astype(jnp.bfloat16)
    projected = project(first, self_qkv).astype(jnp.bfloat16)
    self_queries = projected[:, :, :width]
    self_kv = lax.all_gather(projected[:, :, width:], "seq", axis=1, tiled=True)
    query_place = rank * local_rows + jnp.arange(local_rows, dtype=jnp.int32)
    key_place = jnp.arange(all_targets, dtype=jnp.int32)
    causal = (query_place[:, None] >= key_place[None, :])[None, None]
    self_context, self_total = attend_forward(self_queries, self_kv, causal)
    hidden1 = x + project(self_context, self_out)
    second_f, pull_second = jax.vjp(layer_norm, hidden1, norm_gain[1], norm_bias[1])
    second = second_f.astype(jnp.bfloat16)
    cross_queries = project(second, cross_query).astype(jnp.bfloat16)
    gathered = lax.all_gather(memory, "seq", axis=1, tiled=True)
    memory_kv = project(gathered, cross_kv).astype(jnp.bfloat16)
    source_place = jnp.arange(all_sources, dtype=jnp.int32)
    visible = (source_place[None, :] < src_len[:, None])[:, None, None, :]
    cross_context, cross_total = attend_forward(cross_queries, memory_kv, visible)
    hidden2 = hidden1 + project(cross_context, cross_out)
    third_f, pull_third = jax.vjp(layer_norm, hidden2, norm_gain[2], norm_bias[2])
    third = third_f.astype(jnp.bfloat16)
    raised_up = project(third, ffn_in)
    active_f, pull_smooth = jax.vjp(smooth, raised_up)
    activated = active_f.astype(jnp.bfloat16)
    layer_out = (hidden2 + project(activated, ffn_out)).astype(jnp.bfloat16)
    grad_out = out_grad.astype(jnp.float32)
    ffn_out_grad = outer(activated, out_grad)
    (grad_up,) = pull_smooth(project_back(out_grad, ffn_out))
    grad_up_low = grad_up.astype(jnp.bfloat16)
    ffn_in_grad = outer(third, grad_up_low)
    back_third, gain_third, bias_third = pull_third(project_back(grad_up_low, ffn_in))
    grad_hidden2 = grad_out + back_third
    cross_branch = grad_hidden2.astype(jnp.bfloat16)
    cross_out_grad = outer(cross_context, cross_branch)
    grad_cross_context = project_back(cross_branch, cross_out).astype(jnp.bfloat16)
    grad_cross_q, grad_memory_kv = attend_backward(
        cross_queries, memory_kv, visible, cross_total, grad_cross_context
    )
    local_kv_grad = lax.psum_scatter(
        grad_memory_kv.astype(jnp.bfloat16), "seq", scatter_dimension=1, tiled=True
    ).astype(jnp.float32)
    cross_kv_grad = outer_full(memory, local_kv_grad)
    memory_grad = back_full(local_kv_grad, cross_kv)
    grad_cross_low = grad_cross_q.astype(jnp.bfloat16)
    cross_query_grad = outer(second, grad_cross_low)
    back_second, gain_second, bias_second = pull_second(project_back(grad_cross_low, cross_query))
    grad_hidden1 = grad_hidden2 + back_second
    self_branch = grad_hidden1.astype(jnp.bfloat16)
    self_out_grad = outer(self_context, self_branch)
    grad_self_context = project_back(self_branch, self_out).astype(jnp.bfloat16)
    grad_self_q, grad_self_kv = attend_backward(
        self_queries, self_kv, causal, self_total, grad_self_context
    )
    local_self_kv = lax.psum_scatter(grad_self_kv, "seq", scatter_dimension=1, tiled=True)
    grad_projected = jnp.concatenate([grad_self_q, local_self_kv], axis=2).astype(jnp.bfloat16)
    self_qkv_grad = outer(first, grad_projected)
    back_first, gain_first, bias_first = pull_first(project_back(grad_projected, self_qkv))
    input_grad = grad_hidden1 + back_first
    gain_terms = jnp.stack([gain_first, gain_second, gain_third])
    bias_terms = jnp.stack([bias_first, bias_second, bias_third])
    gain_total, bias_total = lax.psum((gain_terms, bias_terms), ("dp", "seq"))
    partial_value = (
        lax.psum_scatter(
            self_qkv_grad.astype(jnp.bfloat16), "dp", scatter_dimension=0, tiled=True
        ).astype(jnp.float32),
        lax.psum_scatter(
            self_out_grad.astype(jnp.bfloat16), "dp", scatter_dimension=0, tiled=True
        ).astype(jnp.float32),
        lax.psum_scatter(
            cross_query_grad.astype(jnp.bfloat16), "dp", scatter_dimension=0, tiled=True
        ).astype(jnp.float32),
        lax.psum_scatter(
            cross_kv_grad.astype(jnp.bfloat16), "dp", scatter_dimension=0, tiled=True
        ).astype(jnp.float32),
        lax.psum_scatter(
            cross_out_grad.astype(jnp.bfloat16), "dp", scatter_dimension=0, tiled=True
        ).astype(jnp.float32),
        lax.psum_scatter(
            ffn_in_grad.astype(jnp.bfloat16), "dp", scatter_dimension=0, tiled=True
        ).astype(jnp.float32),
        lax.psum_scatter(
            ffn_out_grad.astype(jnp.bfloat16), "dp", scatter_dimension=0, tiled=True
        ).astype(jnp.float32),
    )
    finished = (
        lax.psum_scatter(
            partial_value[0].astype(jnp.bfloat16), "seq", scatter_dimension=1, tiled=True
        ).astype(jnp.float32),
        lax.psum_scatter(
            partial_value[1].astype(jnp.bfloat16), "seq", scatter_dimension=1, tiled=True
        ).astype(jnp.float32),
        lax.psum_scatter(
            partial_value[2].astype(jnp.bfloat16), "seq", scatter_dimension=1, tiled=True
        ).astype(jnp.float32),
        lax.psum_scatter(
            partial_value[3].astype(jnp.bfloat16), "seq", scatter_dimension=1, tiled=True
        ).astype(jnp.float32),
        lax.psum_scatter(
            partial_value[4].astype(jnp.bfloat16), "seq", scatter_dimension=1, tiled=True
        ).astype(jnp.float32),
        lax.psum_scatter(
            partial_value[5].astype(jnp.bfloat16), "seq", scatter_dimension=1, tiled=True
        ).astype(jnp.float32),
        lax.psum_scatter(
            partial_value[6].astype(jnp.bfloat16), "seq", scatter_dimension=1, tiled=True
        ).astype(jnp.float32),
    )
    return (
        layer_out,
        input_grad,
        memory_grad,
        finished[0],
        finished[1],
        finished[2],
        finished[3],
        finished[4],
        finished[5],
        finished[6],
        gain_total,
        bias_total,
    )


def solution(mesh):
    paired = mesh.shape["dp"] == 16 and mesh.shape["seq"] == 2
    per_device = per_device_paired if paired else per_device_wide
    in_specs = (
        P("dp", "seq", None),
        P("dp", "seq", None),
        P("dp"),
        P("dp", "seq", None),
        P(),
        P(),
        P(),
        P(),
        P(),
        P(),
        P(),
        P(),
        P(),
    )
    out_specs = (
        P("dp", "seq", None),
        P("dp", "seq", None),
        P("dp", "seq", None),
        P("dp", "seq"),
        P("dp", "seq"),
        P("dp", "seq"),
        P("dp", "seq"),
        P("dp", "seq"),
        P("dp", "seq"),
        P("dp", "seq"),
        P(),
        P(),
    )
    return jax.shard_map(
        per_device, mesh=mesh, in_specs=in_specs, out_specs=out_specs, check_vma=False
    )
```

```python
import functools
import math

import jax
import jax.numpy as jnp
from jax import lax
from jax.experimental import pallas as pl
from jax.experimental.pallas import tpu as pltpu
from jax.sharding import PartitionSpec as P

HEADS = 12
HEAD_DIM = 64
MESH = pl.DeviceIdType.MESH
F32 = jnp.float32
BF16 = jnp.bfloat16
TRIPLES = 16
ORDERS = (("x", "l", "y", "h"), ("y", "x", "l", "h"), ("l", "x", "y", "h"))


def place():
    i = lax.axis_index("dp")
    return {"c": i % 2, "x": (i // 2) % 2, "l": (i // 4) % 2, "h": i // 8, "y": lax.axis_index("seq")}


def partner(axis, at):
    i = lax.axis_index("dp")
    y = at["y"]
    if axis == "y":
        return (i, 1 - y)
    step = {"c": 1, "x": 2, "l": 4, "h": 8}[axis]
    return (i + step - 2 * step * at[axis], y)


def greet(at):
    barrier = pltpu.get_barrier_semaphore()
    for axis in ("c", "x", "l", "h", "y"):
        pl.semaphore_signal(barrier, inc=1, device_id=partner(axis, at), device_id_type=MESH)
    pl.semaphore_wait(barrier, 5)


LEFT = (4, 4, 4, 4, 0, 1, 2, 3, 5, 6, 6, 8, 9, 10, 10, 10)
RIGHT = (1, 2, 3, 4, 0, 0, 0, 0, 5, 6, 7, 8, 9, 10, 11, 12)


def look_up(table, t):
    if isinstance(t, int):
        return table[t]
    value = table[-1]
    for n in range(TRIPLES - 2, -1, -1):
        if table[n] != table[n + 1]:
            value = jnp.where(t <= n, table[n], value)
    return value


def when(condition):
    if isinstance(condition, bool):
        return (lambda body: body()) if condition else (lambda body: None)
    return pl.when(condition)


def negate(condition):
    return not condition if isinstance(condition, bool) else jnp.logical_not(condition)


def store_left(lt, slot, rows_by_feature):
    for i in range(16):
        lt[slot, i % 2, 48 * (i // 2) : 48 * (i // 2) + 48, :] = rows_by_feature[48 * i : 48 * i + 48, :]


class Reducer:
    LAGS = (0, 1, 3, 5, 7, 8)
    SLOTS = (2, 3, 3, 3, 3)
    TICKS = TRIPLES + 8
    SCRATCH = [
        pltpu.VMEM((2, 3, 384, 256), BF16),
        pltpu.VMEM((TRIPLES, 3, 384, 256), BF16),
        pltpu.VMEM((3, 3, 2, 2, 2, 2, 48, 128), BF16),
        pltpu.VMEM((TRIPLES, 3, 2, 2, 2, 48, 128), BF16),
        pltpu.VMEM((3, 3, 2, 2, 2, 48, 128), BF16),
        pltpu.VMEM((TRIPLES, 3, 2, 2, 48, 128), BF16),
        pltpu.VMEM((3, 3, 2, 2, 48, 128), BF16),
        pltpu.VMEM((TRIPLES, 3, 2, 48, 128), BF16),
        pltpu.VMEM((3, 3, 2, 48, 128), BF16),
        pltpu.VMEM((TRIPLES, 3, 48, 128), BF16),
        pltpu.VMEM((3, 3, 48, 128), F32),
        pltpu.SemaphoreType.DMA((3,)),
        pltpu.SemaphoreType.DMA((5, 3, 3)),
        pltpu.SemaphoreType.DMA((5, TRIPLES, 3)),
    ]

    def __init__(self, at, lt, rg, out, s0, r0, s1, r1, s2, r2, s3, r3, s4, r4, done, done_sem, send_sem, recv_sem):
        self.at, self.lt, self.rg, self.out = at, lt, rg, out
        self.sent, self.got = (s0, s1, s2, s3, s4), (r0, r1, r2, r3, r4)
        self.done, self.done_sem = done, done_sem
        self.send_sem, self.recv_sem = send_sem, recv_sem

    def axis(self, stage, g):
        return "c" if stage == 0 else ORDERS[g][stage - 1]

    def copy(self, stage, t, g):
        axis = self.axis(stage, g)
        slot = t % self.SLOTS[stage]
        src = self.sent[stage].at[slot, g]
        if stage:
            src = src.at[1 - self.at[axis]]
        return pltpu.make_async_remote_copy(
            src_ref=src,
            dst_ref=self.got[stage].at[t, g],
            send_sem=self.send_sem.at[stage, slot, g],
            recv_sem=self.recv_sem.at[stage, t, g],
            device_id=partner(axis, self.at),
            device_id_type=MESH,
        )

    def free(self, stage, t):
        slots = self.SLOTS[stage]

        @when(t >= slots)
        def _():
            for g in range(3):
                self.copy(stage, t - slots, g).wait_send()

    def product(self, t, half, g):
        cols = slice(256 * g, 256 * g + 256)
        return jnp.dot(self.lt[look_up(LEFT, t), half], self.rg[look_up(RIGHT, t), :, cols], preferred_element_type=F32)

    def first(self, t):
        self.free(0, t)
        half = 1 - self.at["c"]
        memory = (t == 9) | (t == 10)
        for g in range(3):
            cols = slice(256 * g, 256 * g + 256)

            @when(negate(memory))
            def _():
                self.sent[0][t % 2, g] = self.product(t, half, g).astype(BF16)

            @when(memory)
            def _():
                more = jnp.dot(self.lt[7, half], self.rg[t + 4, :, cols], preferred_element_type=F32)
                self.sent[0][t % 2, g] = (self.product(t, half, g) + more).astype(BF16)

            self.copy(0, t, g).start()

    def second(self, t):
        self.free(1, t)
        half = self.at["c"]
        memory = (t == 9) | (t == 10)
        for g in range(3):
            cols = slice(256 * g, 256 * g + 256)
            self.copy(0, t, g).wait_recv()

            def spread(total):
                order = ORDERS[g]
                for b in range(8):
                    bits = {"h": b // 4, "l": (b // 2) % 2, "x": b % 2}
                    for y in range(2):
                        bits["y"] = y
                        where = tuple(bits[a] for a in order)
                        self.sent[1][(t % self.SLOTS[1], g) + where] = total[48 * b : 48 * b + 48, 128 * y : 128 * y + 128].astype(BF16)

            @when(negate(memory))
            def _():
                spread(self.product(t, half, g) + self.got[0][t, g].astype(F32))

            @when(memory)
            def _():
                more = jnp.dot(self.lt[7, half], self.rg[t + 4, :, cols], preferred_element_type=F32)
                spread(self.product(t, half, g) + more + self.got[0][t, g].astype(F32))

            self.copy(1, t, g).start()

    def write(self, t):
        return pltpu.make_async_copy(self.done.at[t % 3], self.out.at[t], self.done_sem.at[t % 3])

    def onward(self, stage, t):
        if stage < 5:
            self.free(stage, t)
        else:

            @when(t >= 3)
            def _():
                self.write(t - 3).wait()

        for g in range(3):
            self.copy(stage - 1, t, g).wait_recv()
            own = self.sent[stage - 1][t % self.SLOTS[stage - 1], g, self.at[self.axis(stage - 1, g)]]
            total = own.astype(F32) + self.got[stage - 1][t, g].astype(F32)
            if stage < 5:
                self.sent[stage][t % self.SLOTS[stage], g] = total.astype(BF16)
                self.copy(stage, t, g).start()
            else:
                self.done[t % 3, g] = total
        if stage == 5:
            self.write(t).start()

    def tick(self, n, but=()):
        for stage in range(6):
            if stage in but:
                continue
            t = n - self.LAGS[stage]

            @when((t >= 0) & (t < TRIPLES))
            def _():
                if stage == 0:
                    self.first(t)
                elif stage == 1:
                    self.second(t)
                else:
                    self.onward(stage, t)

    def drain(self):
        for t in range(TRIPLES - 3, TRIPLES):
            self.write(t).wait()
        for stage in range(5):
            for t in range(TRIPLES - self.SLOTS[stage], TRIPLES):
                for g in range(3):
                    self.copy(stage, t, g).wait_send()


NORM_ORDER = ("c", "x", "y", "l", "h")


def norm_copy(j, at, own, got, send_sem, recv_sem):
    return pltpu.make_async_remote_copy(
        src_ref=own.at[j], dst_ref=got.at[j], send_sem=send_sem.at[j], recv_sem=recv_sem.at[j],
        device_id=partner(NORM_ORDER[j], at), device_id_type=MESH,
    )


def norm_step(j, at, own, got, send_sem, recv_sem):
    if j:
        norm_copy(j - 1, at, own, got, send_sem, recv_sem).wait()
        own[j] = own[j - 1] + got[j - 1]
    if j < 5:
        norm_copy(j, at, own, got, send_sem, recv_sem).start()


LANES = 128


def normed(v):
    center = jnp.mean(v, axis=-1, keepdims=True)
    centered = v - center
    spread = jnp.mean(centered * centered, axis=-1, keepdims=True)
    scale = lax.rsqrt(spread + 1e-05)
    return centered * scale, scale


def row_blocks(step, body):
    for b in range(256 // step):
        body(slice(b * step, b * step + step))


def norm_forward(load, out, norm_gain, norm_bias, k):
    def body(rows):
        hat, _ = normed(load(rows))
        out[rows, :] = (hat * norm_gain[k : k + 1, :] + norm_bias[k : k + 1, :]).astype(BF16)

    row_blocks(64, body)


def norm_backward(load, load_grad, store, norm_gain, sums, k):
    def body(rows):
        hat, scale = normed(load(rows))
        dy = load_grad(rows)
        sums[k : k + 1, :] += jnp.sum(dy * hat, axis=0, keepdims=True)
        sums[k + 3 : k + 4, :] += jnp.sum(dy, axis=0, keepdims=True)
        dhat = dy * norm_gain[k : k + 1, :]
        mean = jnp.mean(dhat, axis=-1, keepdims=True)
        along = jnp.mean(dhat * hat, axis=-1, keepdims=True)
        store(rows, scale * (dhat - mean - hat * along))

    row_blocks(64, body)


def two_heads(tile):
    first = lax.broadcasted_iota(jnp.int32, tile.shape, 1) < HEAD_DIM
    zero = jnp.zeros_like(tile)
    return jnp.concatenate([jnp.where(first, tile, zero), jnp.where(first, zero, tile)], axis=0)


def upright(sideways):
    rows = sideways.shape[1] // 2
    own = jnp.concatenate([sideways[:HEAD_DIM, :rows], sideways[HEAD_DIM:, rows:]], axis=0)
    return own.T


def dot(a, b, over):
    return lax.dot_general(a, b, (over, ((), ())), preferred_element_type=F32)


LAST = ((1,), (1,))
PLAIN = ((1,), (0,))
ROWS = ((0,), (0,))


def attend(items):
    scores = [jnp.where(allowed, dot(k, two_heads(q), LAST), -1e30) for q, k, _, allowed in items]
    raised = [jnp.exp(s - jnp.max(s, axis=0, keepdims=True)) for s in scores]
    weights = [(r * (1.0 / jnp.sum(r, axis=0, keepdims=True))).astype(BF16) for r in raised]
    contexts = [upright(dot(item[2], w, ROWS).astype(BF16)) for w, item in zip(weights, items)]
    return list(zip(weights, contexts))


def attend_back(items):
    stacked = [two_heads(item[4]) for item in items]
    dweights = [dot(item[2], s, LAST) for item, s in zip(items, stacked)]
    dvs = [dot(item[3], s, PLAIN).astype(BF16) for item, s in zip(items, stacked)]
    dscores = []
    for item, d in zip(items, dweights):
        probs = item[3].astype(F32)
        terms = probs * d
        dscores.append((terms - probs * jnp.sum(terms, axis=0, keepdims=True)).astype(BF16))
    dqs = [upright((dot(item[1], d, ROWS) * (1.0 / math.sqrt(HEAD_DIM))).astype(BF16)) for item, d in zip(items, dscores)]
    dks = [dot(d, two_heads(item[0]), PLAIN).astype(BF16) for item, d in zip(items, dscores)]
    return list(zip(dqs, dks, dvs))


def in_groups(pairs, size, body):
    for n in range(0, len(pairs), size):
        body(pairs[n : n + size])


def column(slot, h, g):
    return (slot, slice(None), pl.ds(pl.multiple_of(256 * g + LANES * h, LANES), LANES))


def back(rg, slots, weight, rows=None):
    half = weight.shape[1] // 2
    total = None
    for j, slot in enumerate(slots):
        for g in range(3):
            at = j * 384 + g * LANES
            w = jnp.concatenate([weight[:, at : at + LANES], weight[:, half + at : half + at + LANES]], axis=1)
            term = dot(rg[slot, :, 256 * g : 256 * g + 256], w, LAST)
            total = term if total is None else total + term
    return total


CHUNKS = (0, 3, 1, 4, 2, 5)


def layer_kernel(
    dec_input, memory, src_len, out_grad, self_qkv, self_out, cross_query, cross_kv, cross_out, ffn_in, ffn_out,
    norm_gain, norm_bias,
    o_layer, o_input, o_memory, units, norm_out,
    x_in, mem, og, w_qkv, w_self, w_query, w_kv, w_cross, w_in, w_out,
    normal, qkv, p_self, context, hidden1, qx, kv, p_cross, hidden2,
    active, acc, dthird,
    lt, rg, n_own, n_got, n_send, n_recv, load_sem, swap_send, swap_recv, out_sem, out_send, out_recv, *rest
):
    at = place()
    y = at["y"]
    red = Reducer(at, lt, rg, units, *rest)
    across = partner("y", at)

    loads = [
        pltpu.make_async_copy(src, dst, load_sem.at[n])
        for n, (src, dst) in enumerate(
            ((self_qkv, w_qkv), (self_out, w_self), (cross_kv, w_kv), (cross_query, w_query), (cross_out, w_cross))
        )
    ]
    for load in loads:
        load.start()

    def ffn_load(n):
        cols = slice(CHUNKS[n] * 512, CHUNKS[n] * 512 + 512)
        slot = n % 3
        return (
            pltpu.make_async_copy(ffn_in.at[:, cols], w_in.at[slot], load_sem.at[5 + slot]),
            pltpu.make_async_copy(ffn_out.at[cols, :], w_out.at[slot], load_sem.at[8 + slot]),
        )

    for n in range(3):
        for load in ffn_load(n):
            load.start()

    def own_rows(n, src, dst, rows):
        return [
            pltpu.make_async_copy(
                src.at[2 * y + e], dst.at[pl.ds(pl.multiple_of(2 * e * rows + y * rows, rows), rows), :], load_sem.at[11 + 2 * n + e]
            )
            for e in range(2)
        ]

    def swap(n, src, dst, rows):
        return [
            pltpu.make_async_remote_copy(
                src_ref=src.at[2 * (1 - y) + e],
                dst_ref=dst.at[pl.ds(pl.multiple_of(2 * e * rows + y * rows, rows), rows), :],
                send_sem=swap_send.at[n, e], recv_sem=swap_recv.at[n, e], device_id=across, device_id_type=MESH,
            )
            for e in range(2)
        ]

    moved = ((dec_input, x_in, 64), (memory, mem, 128), (out_grad, og, 64))
    owns = [own_rows(n, *m) for n, m in enumerate(moved)]
    swaps = [swap(n, *m) for n, m in enumerate(moved)]
    for own in owns:
        for copy in own:
            copy.start()
    greet(at)
    for copy in swaps[0]:
        copy.start()
    for copy in swaps[1]:
        copy.start()
    for copy in swaps[2]:
        copy.start()

    def own_here(n):
        for copy in owns[n]:
            copy.wait()

    def other_here(n, e):
        swaps[n][e].wait()

    scale = 1.0 / math.sqrt(HEAD_DIM)

    own_here(0)
    for e in range(2):
        other_here(0, e)
    norm_forward(lambda rows: x_in[rows, :].astype(F32), normal, norm_gain, norm_bias, 0)
    loads[0].wait()

    for n in range(9):
        out = jnp.dot(normal[...], w_qkv[:, 256 * n : 256 * n + 256], preferred_element_type=F32)
        out = (out * scale if n < 3 else out).astype(BF16)
        qkv[2 * n] = out[:, 0:LANES]
        qkv[2 * n + 1] = out[:, LANES:256]

    store_left(lt, 10, normal[...].T)

    def pair(e, p):
        return slice(e * 128, e * 128 + 128), slice(p * LANES, p * LANES + LANES)

    pairs = [(e, p) for p in range(6) for e in range(2)]

    def self_operands(e, p):
        rows, _ = pair(e, p)
        return qkv[p, rows, :], qkv[6 + p, rows, :], qkv[12 + p, rows, :]

    def self_forward(group):
        k_at = lax.broadcasted_iota(jnp.int32, (128, 256), 0)
        q_at = lax.broadcasted_iota(jnp.int32, (128, 256), 1) % 128
        results = attend([(*self_operands(e, p), q_at >= k_at) for e, p in group])
        for (e, p), (weights, values) in zip(group, results):
            p_self[6 * e + p] = weights
            context[pair(e, p)] = values

    in_groups(pairs, 4, self_forward)

    loads[1].wait()
    for n in range(3):
        cols = slice(256 * n, 256 * n + 256)
        hidden1[:, cols] = x_in[:, cols].astype(F32) + jnp.dot(context[...], w_self[:, cols], preferred_element_type=F32)
    store_left(lt, 9, context[...].T)
    norm_forward(lambda rows: hidden1[rows, :], normal, norm_gain, norm_bias, 1)

    loads[3].wait()
    for n in range(3):
        out = jnp.dot(normal[...], w_query[:, 256 * n : 256 * n + 256], preferred_element_type=F32)
        out = (out * scale).astype(BF16)
        qx[2 * n] = out[:, 0:LANES]
        qx[2 * n + 1] = out[:, LANES:256]
    store_left(lt, 8, normal[...].T)
    loads[2].wait()
    own_here(1)

    def project_kv(blocks):
        rows = [pl.ds(pl.multiple_of(at_, 128), 128) for at_ in blocks]
        source = jnp.concatenate([mem[r, :] for r in rows], axis=0)
        for n in range(6):
            out = jnp.dot(source, w_kv[:, 256 * n : 256 * n + 256], preferred_element_type=F32).astype(BF16)
            for k, r in enumerate(rows):
                kv[2 * n, r, :] = out[128 * k : 128 * k + 128, 0:LANES]
                kv[2 * n + 1, r, :] = out[128 * k : 128 * k + 128, LANES:256]

    project_kv([128 * y, 256 + 128 * y])

    def cross_operands(e, p):
        rows, keys = pair(e, p)[0], slice(e * 256, e * 256 + 256)
        return qx[p, rows, :], kv[p, keys, :], kv[6 + p, keys, :]

    def cross_forward(group):
        k_at = lax.broadcasted_iota(jnp.int32, (256, 256), 0)
        results = attend([(*cross_operands(e, p), k_at < src_len[2 * y + e]) for e, p in group])
        for (e, p), (weights, values) in zip(group, results):
            p_cross[6 * e + p] = weights
            context[pair(e, p)] = values

    for e in range(2):
        other_here(1, e)
        project_kv([256 * e + 128 * (1 - y)])
        cross_forward([(e, p) for p in range(6)])

    loads[4].wait()
    for n in range(3):
        cols = slice(256 * n, 256 * n + 256)
        hidden2[:, cols] = hidden1[:, cols] + jnp.dot(context[...], w_cross[:, cols], preferred_element_type=F32)
    norm_forward(lambda rows: hidden2[rows, :], normal, norm_gain, norm_bias, 2)

    own_here(2)
    for e in range(2):
        other_here(2, e)

    def spread(slot, rows_of):
        for g in range(3):
            for h in range(2):
                lane = h * 384 + g * LANES
                rg[slot, :, 256 * g + LANES * h : 256 * g + LANES * h + LANES] = rows_of[:, lane : lane + LANES].astype(BF16)

    acc[...] = jnp.zeros_like(acc)
    dthird[...] = jnp.zeros_like(dthird)
    root = math.sqrt(2.0 / math.pi)

    def up_tile(tile):
        lane = 256 * (tile % 3) + LANES * (tile // 12)
        return (1 + (tile % 12) // 3, slice(None), slice(lane, lane + LANES))

    def feed_in(n, s):
        slot, cols = n % 3, slice(256 * s, 256 * s + 256)
        up = jnp.dot(normal[...], w_in[slot, :, cols], preferred_element_type=F32)
        return up, dot(og[...], w_out[slot, cols, :], LAST)

    def feed_bend(n, s, up, dact):
        square = up * up
        bend = jnp.tanh(up * (root + (root * 0.044715) * square))
        lift = 0.5 + 0.5 * bend
        active[n % 2, :, 256 * s : 256 * s + 256] = (up * lift).astype(BF16)
        slope = lift + (0.5 * up) * (1.0 - bend * bend) * (root + (3.0 * 0.044715 * root) * square)
        grad = (dact * slope).astype(BF16)
        for t in range(2):
            rg[up_tile(4 * CHUNKS[n] + 2 * s + t)] = grad[:, LANES * t : LANES * t + LANES]

    def feed_out(n, k):
        slot, cols = n % 3, slice(256 * k, 256 * k + 256)
        acc[:, cols] += jnp.dot(active[n % 2], w_out[slot, :, cols], preferred_element_type=F32)
        dup = jnp.concatenate([rg[up_tile(4 * CHUNKS[n] + t)] for t in range(4)], axis=1)
        dthird[:, cols] += dot(dup, w_in[slot, cols, :], LAST)

    def feed_left(n):
        flipped = active[n % 2].T
        at_ = 0
        while at_ < 512:
            feature = CHUNKS[n] * 512 + at_
            i, k, r = feature // 192, (feature % 192) // 48, feature % 48
            size = min(48 - r, 512 - at_)
            to = 48 * (i // 2) + r
            lt[k, i % 2, to : to + size, :] = flipped[at_ : at_ + size, :]
            at_ += size

    def feed(n):
        for load in ffn_load(n):
            load.wait()
        for s in range(2):
            up, dact = feed_in(n, s)
            if n:
                for k in ((0, 1), (2,))[s]:
                    feed_out(n - 1, k)
            feed_bend(n, s, up, dact)
        if n:
            feed_left(n - 1)
            if n < 4:
                for load in ffn_load(n + 2):
                    load.start()

    PIECES = (
        [(normal, o_layer, 64, e, r) for e in range(2) for r in (0, 32)]
        + [(mem, o_memory, 128, e, r) for e in range(2) for r in (0, 32, 64, 96)]
        + [(x_in, o_input, 64, e, r) for e in range(2) for r in (0, 32)]
    )

    def piece(n, leaving):
        buf, out, rows, e, r = PIECES[n]
        which = 1 - y if leaving else y
        src = buf.at[pl.ds(pl.multiple_of(2 * e * rows + which * rows + r, 32), 32), :]
        dst = out.at[2 * y + e, r : r + 32, :]
        if not leaving:
            return pltpu.make_async_copy(src, dst, out_sem.at[n])
        return pltpu.make_async_remote_copy(
            src_ref=src, dst_ref=dst, send_sem=out_send.at[n], recv_sem=out_recv.at[n], device_id=across, device_id_type=MESH
        )

    def send(n):
        piece(n, True).start()
        piece(n, False).start()

    def tick(n):
        red.tick(n)
        if n >= 3:
            send(n - 3)

    feed(0)
    feed(1)
    store_left(lt, 4, normal[...].T)
    red.first(0)
    feed(2)
    red.second(0)
    feed(3)
    red.first(1)
    feed(4)
    red.second(1)
    feed(5)
    for k in range(3):
        feed_out(5, k)
    feed_left(5)
    spread(0, og)
    red.tick(2, but=(1,))

    normal[...] = (hidden2[...] + acc[...]).astype(BF16)

    sums = n_own.at[0]
    sums[...] = jnp.zeros(sums.shape, F32)

    def store_grad(rows, value):
        acc[rows, :] = value

    norm_backward(
        lambda rows: hidden2[rows, :], lambda rows: dthird[rows, :],
        lambda rows, v: store_grad(rows, og[rows, :].astype(F32) + v), norm_gain, sums, 2,
    )
    spread(5, acc)
    tick(3)
    store_left(lt, 5, context[...].T)
    dc = context

    def context_grad(slot, weight):
        for n in range(3):
            rows = slice(256 * n, 256 * n + 256)
            dc[:, rows] = back(rg, (slot,), weight.at[rows, :]).astype(BF16)

    context_grad(5, w_cross)

    def cross_backward(group):
        results = attend_back([(*cross_operands(e, p), p_cross[6 * e + p], dc[pair(e, p)]) for e, p in group])
        for (e, p), (dq, dk, dv) in zip(group, results):
            j, g = p // 3, p % 3
            rg[8, pair(e, p)[0], 256 * g + LANES * j : 256 * g + LANES * j + LANES] = dq
            rg[6 + 7 * e + j, :, 256 * g : 256 * g + LANES] = dk
            rg[6 + 7 * e + j, :, 256 * g + LANES : 256 * g + 256] = dv

    tick(4)
    in_groups(pairs[:6], 3, cross_backward)
    tick(5)
    in_groups(pairs[6:], 3, cross_backward)

    store_left(lt, 6, mem[0:256, :].T)
    store_left(lt, 7, mem[256:512, :].T)

    def memory_rows(e):
        for n in range(3):
            rows = slice(256 * n, 256 * n + 256)
            mem[256 * e : 256 * e + 256, rows] = back(rg, (6 + 7 * e, 7 + 7 * e), w_kv.at[rows, :]).astype(BF16)

    memory_rows(0)
    tick(6)
    memory_rows(1)
    for n in range(3):
        rows = slice(256 * n, 256 * n + 256)
        dthird[:, rows] = back(rg, (8,), w_query.at[rows, :])
    tick(7)
    norm_backward(
        lambda rows: hidden1[rows, :], lambda rows: dthird[rows, :],
        lambda rows, v: store_grad(rows, acc[rows, :] + v), norm_gain, sums, 1,
    )
    spread(9, acc)
    context_grad(9, w_self)
    tick(8)

    def self_backward(group):
        results = attend_back([(*self_operands(e, p), p_self[6 * e + p], dc[pair(e, p)]) for e, p in group])
        for (e, p), values in zip(group, results):
            for n, value in enumerate(values):
                tile = 6 * n + p
                lane = 256 * (tile % 3) + LANES * (tile // 9)
                rg[10 + (tile % 9) // 3, pair(e, p)[0], lane : lane + LANES] = value

    in_groups(pairs[:6], 3, self_backward)
    tick(9)
    in_groups(pairs[6:], 3, self_backward)
    tick(10)
    for n in range(3):
        rows = slice(256 * n, 256 * n + 256)
        dthird[:, rows] = back(rg, (10, 11, 12), w_qkv.at[rows, :])
    tick(11)

    def store_input(rows, v):
        x_in[rows, :] = (acc[rows, :] + v).astype(BF16)

    norm_backward(
        lambda rows: x_in[rows, :].astype(F32), lambda rows: dthird[rows, :], store_input, norm_gain, sums, 0
    )

    def body(n, carry):
        red.tick(n)
        for j in range(6):
            @pl.when(n == 12 + j)
            def _():
                norm_step(j, at, n_own, n_got, n_send, n_recv)

        for k in range(9, 16):
            @pl.when(n == k + 3)
            def _():
                send(k)

        return carry

    lax.fori_loop(12, red.TICKS, body, 0)
    norm_out[...] = n_own[5]
    red.drain()
    for n in range(16):
        piece(n, True).wait()
        piece(n, False).wait()


def layer_call(args):
    anywhere = pl.BlockSpec(memory_space=pl.ANY)
    vmem = pl.BlockSpec(memory_space=pltpu.VMEM)
    rows = lambda width, kind=BF16: pltpu.VMEM((256, width), kind)
    return pl.pallas_call(
        layer_kernel,
        out_shape=(
            jax.ShapeDtypeStruct((4, 64, 768), BF16),
            jax.ShapeDtypeStruct((4, 64, 768), BF16),
            jax.ShapeDtypeStruct((4, 128, 768), BF16),
            jax.ShapeDtypeStruct((TRIPLES, 3, 48, 128), F32),
            jax.ShapeDtypeStruct((8, 768), F32),
        ),
        in_specs=[anywhere, anywhere, pl.BlockSpec(memory_space=pltpu.SMEM)] + [anywhere] * 8 + [vmem] * 2,
        out_specs=(anywhere, anywhere, anywhere, anywhere, vmem),
        scratch_shapes=[
            rows(768), pltpu.VMEM((512, 768), BF16), rows(768),
            pltpu.VMEM((768, 2304), BF16), pltpu.VMEM((768, 768), BF16), pltpu.VMEM((768, 768), BF16),
            pltpu.VMEM((768, 1536), BF16), pltpu.VMEM((768, 768), BF16),
            pltpu.VMEM((3, 768, 512), BF16), pltpu.VMEM((3, 512, 768), BF16),
            rows(768), pltpu.VMEM((18, 256, 128), BF16), pltpu.VMEM((12, 128, 256), BF16), rows(768),
            rows(768, F32), pltpu.VMEM((6, 256, 128), BF16), pltpu.VMEM((12, 512, 128), BF16),
            pltpu.VMEM((12, 256, 256), BF16), rows(768, F32),
            pltpu.VMEM((2, 256, 512), BF16), rows(768, F32), rows(768, F32),
            pltpu.VMEM((11, 2, 384, 256), BF16),
            pltpu.VMEM((15, 256, 768), BF16),
            pltpu.VMEM((6, 8, 768), F32),
            pltpu.VMEM((5, 8, 768), F32),
            pltpu.SemaphoreType.DMA((5,)),
            pltpu.SemaphoreType.DMA((5,)),
            pltpu.SemaphoreType.DMA((17,)),
            pltpu.SemaphoreType.DMA((3, 2)),
            pltpu.SemaphoreType.DMA((3, 2)),
            pltpu.SemaphoreType.DMA((16,)),
            pltpu.SemaphoreType.DMA((16,)),
            pltpu.SemaphoreType.DMA((16,)),
        ] + Reducer.SCRATCH,
        compiler_params=pltpu.CompilerParams(collective_id=0, has_side_effects=True, vmem_limit_bytes=61 << 20),
    )(*args)


WEIGHTS = ((13, 3), (12, 1), (11, 1), (9, 2), (8, 1), (0, 4))


def finish_kernel(layer, inputs, memories, units, norms, *refs):
    o_layer, o_input, o_memory = refs[0:3]
    o_weights, o_ffn_out, o_gain, o_bias = refs[3:9], refs[9], refs[10], refs[11]
    low_input, low_memory, high_input, high_memory, blocks = refs[12:17]
    w_bufs, ffn_buf, sem, out_sem, low_layer = refs[17:23], refs[23], refs[24], refs[25], refs[26]
    loads = [
        pltpu.make_async_copy(units, blocks, sem.at[0]),
        pltpu.make_async_copy(memories, low_memory, sem.at[1]),
        pltpu.make_async_copy(inputs, low_input, sem.at[2]),
        pltpu.make_async_copy(layer, low_layer, sem.at[3]),
    ]
    for load in loads:
        load.start()
    stores = []

    def store(src, dst):
        copy = pltpu.make_async_copy(src, dst, out_sem.at[len(stores)])
        copy.start()
        stores.append(copy)

    o_gain[...] = norms[0:3, :]
    o_bias[...] = norms[3:6, :]
    loads[0].wait()
    for (t, count), buf, out in zip(WEIGHTS, w_bufs, o_weights):
        for j in range(count):
            for g in range(3):
                buf[:, j * 384 + g * LANES : j * 384 + g * LANES + LANES] = blocks[t + j, g]
        store(buf, out)
    for k in range(4):
        for g in range(3):
            ffn_buf[48 * k : 48 * k + 48, g * LANES : g * LANES + LANES] = blocks[4 + k, g]
    store(ffn_buf, o_ffn_out)
    loads[1].wait()
    for e in range(4):
        high_memory[e] = low_memory[e].astype(F32)
        store(high_memory.at[e], o_memory.at[e])
    loads[2].wait()
    high_input[...] = low_input[...].astype(F32)
    store(high_input, o_input)
    loads[3].wait()
    store(low_layer, o_layer)
    for copy in stores:
        copy.wait()


def finish_call(layer, inputs, memories, units, norms):
    anywhere = pl.BlockSpec(memory_space=pl.ANY)
    vmem = pl.BlockSpec(memory_space=pltpu.VMEM)
    widths = [count * 384 for _, count in WEIGHTS]
    return pl.pallas_call(
        finish_kernel,
        out_shape=(
            jax.ShapeDtypeStruct(layer.shape, BF16),
            jax.ShapeDtypeStruct(inputs.shape, F32),
            jax.ShapeDtypeStruct(memories.shape, F32),
            *[jax.ShapeDtypeStruct((48, w), F32) for w in widths],
            jax.ShapeDtypeStruct((192, 384), F32),
            jax.ShapeDtypeStruct((3, 768), F32),
            jax.ShapeDtypeStruct((3, 768), F32),
        ),
        in_specs=[anywhere] * 4 + [vmem],
        out_specs=(anywhere,) * 10 + (vmem, vmem),
        scratch_shapes=[
            pltpu.VMEM(inputs.shape, BF16), pltpu.VMEM(memories.shape, BF16),
            pltpu.VMEM(inputs.shape, F32), pltpu.VMEM(memories.shape, F32), pltpu.VMEM(units.shape, F32),
            *[pltpu.VMEM((48, w), F32) for w in widths], pltpu.VMEM((192, 384), F32),
            pltpu.SemaphoreType.DMA((4,)), pltpu.SemaphoreType.DMA((13,)), pltpu.VMEM(layer.shape, BF16),
        ],
        compiler_params=pltpu.CompilerParams(vmem_limit_bytes=60 << 20),
    )(layer, inputs, memories, units, norms)


def per_device_paired(*args):
    return finish_call(*layer_call(args))

def layer_norm(x, gain, shift):
    center = jnp.mean(x, axis=-1, keepdims=True)
    centered = x - center
    spread = jnp.mean(centered * centered, axis=-1, keepdims=True)
    return centered * lax.rsqrt(spread + 1e-05) * gain + shift


def smooth(v):
    return jax.nn.gelu(v, approximate=True)


def project(rows, weight):
    return jnp.einsum("etd,df->etf", rows, weight, preferred_element_type=jnp.float32)


def project_back(grads, weight):
    return jnp.einsum("etf,df->etd", grads, weight, preferred_element_type=jnp.float32)


def outer(rows, grads):
    return jnp.einsum("etd,etf->df", rows, grads, preferred_element_type=jnp.float32)


def outer_full(rows, grads):
    return jnp.einsum(
        "etd,etf->df", rows.astype(jnp.float32), grads, precision=lax.Precision.HIGHEST
    )


def back_full(grads, weight):
    return jnp.einsum(
        "etf,df->etd", grads, weight.astype(jnp.float32), precision=lax.Precision.HIGHEST
    )


def split_heads(queries, key_values):
    examples, rows, width = queries.shape
    count = key_values.shape[1]
    heads_q = queries.reshape(examples, rows, HEADS, HEAD_DIM)
    heads_k = key_values[:, :, :width].reshape(examples, count, HEADS, HEAD_DIM)
    heads_v = key_values[:, :, width:].reshape(examples, count, HEADS, HEAD_DIM)
    return (heads_q, heads_k, heads_v)


def masked_logits(heads_q, heads_k, allowed):
    scores = jnp.einsum("eqhd,ekhd->ehqk", heads_q, heads_k, preferred_element_type=jnp.float32)
    return jnp.where(allowed, scores * (1.0 / math.sqrt(HEAD_DIM)), -1e30)


def attend_forward(queries, key_values, allowed):
    examples, rows, width = queries.shape
    heads_q, heads_k, heads_v = split_heads(queries, key_values)
    logits = masked_logits(heads_q, heads_k, allowed)
    row_top = jnp.max(logits, axis=-1, keepdims=True)
    raised = jnp.where(allowed, jnp.exp(logits - row_top), 0.0)
    row_total = jnp.sum(raised, axis=-1, keepdims=True)
    weights = (raised / row_total).astype(jnp.bfloat16)
    context = jnp.einsum("ehqk,ekhd->eqhd", weights, heads_v, preferred_element_type=jnp.float32)
    return (
        context.reshape(examples, rows, width).astype(jnp.bfloat16),
        row_top + jnp.log(row_total),
    )


def attend_backward(queries, key_values, allowed, log_total, grad_context):
    examples, rows, width = queries.shape
    count = key_values.shape[1]
    heads_q, heads_k, heads_v = split_heads(queries, key_values)
    logits = masked_logits(heads_q, heads_k, allowed)
    soft = jnp.where(allowed, jnp.exp(logits - log_total), 0.0)
    grad_heads = grad_context.reshape(examples, rows, HEADS, HEAD_DIM)
    grad_soft = jnp.einsum(
        "eqhd,ekhd->ehqk", grad_heads, heads_v, preferred_element_type=jnp.float32
    )
    grad_values = jnp.einsum(
        "ehqk,eqhd->ekhd", soft.astype(jnp.bfloat16), grad_heads, preferred_element_type=jnp.float32
    )
    inner = jnp.sum(soft * grad_soft, axis=-1, keepdims=True)
    grad_scores = (soft * (grad_soft - inner) * (1.0 / math.sqrt(HEAD_DIM))).astype(jnp.bfloat16)
    grad_queries = jnp.einsum(
        "ehqk,ekhd->eqhd", grad_scores, heads_k, preferred_element_type=jnp.float32
    )
    grad_keys = jnp.einsum(
        "ehqk,eqhd->ekhd", grad_scores, heads_q, preferred_element_type=jnp.float32
    )
    joined = jnp.concatenate(
        [grad_keys.reshape(examples, count, width), grad_values.reshape(examples, count, width)],
        axis=2,
    )
    return (grad_queries.reshape(examples, rows, width), joined)


def per_device_wide(
    dec_input,
    memory,
    src_len,
    out_grad,
    self_qkv,
    self_out,
    cross_query,
    cross_kv,
    cross_out,
    ffn_in,
    ffn_out,
    norm_gain,
    norm_bias,
):
    examples, local_rows, width = dec_input.shape
    local_sources = memory.shape[1]
    seq_count = lax.axis_size("seq")
    all_targets = local_rows * seq_count
    all_sources = local_sources * seq_count
    rank = lax.axis_index("seq")
    x = dec_input.astype(jnp.float32)
    first_f, pull_first = jax.vjp(layer_norm, x, norm_gain[0], norm_bias[0])
    first = first_f.astype(jnp.bfloat16)
    projected = project(first, self_qkv).astype(jnp.bfloat16)
    self_queries = projected[:, :, :width]
    self_kv = lax.all_gather(projected[:, :, width:], "seq", axis=1, tiled=True)
    query_place = rank * local_rows + jnp.arange(local_rows, dtype=jnp.int32)
    key_place = jnp.arange(all_targets, dtype=jnp.int32)
    causal = (query_place[:, None] >= key_place[None, :])[None, None]
    self_context, self_total = attend_forward(self_queries, self_kv, causal)
    hidden1 = x + project(self_context, self_out)
    second_f, pull_second = jax.vjp(layer_norm, hidden1, norm_gain[1], norm_bias[1])
    second = second_f.astype(jnp.bfloat16)
    cross_queries = project(second, cross_query).astype(jnp.bfloat16)
    gathered = lax.all_gather(memory, "seq", axis=1, tiled=True)
    memory_kv = project(gathered, cross_kv).astype(jnp.bfloat16)
    source_place = jnp.arange(all_sources, dtype=jnp.int32)
    visible = (source_place[None, :] < src_len[:, None])[:, None, None, :]
    cross_context, cross_total = attend_forward(cross_queries, memory_kv, visible)
    hidden2 = hidden1 + project(cross_context, cross_out)
    third_f, pull_third = jax.vjp(layer_norm, hidden2, norm_gain[2], norm_bias[2])
    third = third_f.astype(jnp.bfloat16)
    raised_up = project(third, ffn_in)
    active_f, pull_smooth = jax.vjp(smooth, raised_up)
    activated = active_f.astype(jnp.bfloat16)
    layer_out = (hidden2 + project(activated, ffn_out)).astype(jnp.bfloat16)
    grad_out = out_grad.astype(jnp.float32)
    ffn_out_grad = outer(activated, out_grad)
    (grad_up,) = pull_smooth(project_back(out_grad, ffn_out))
    grad_up_low = grad_up.astype(jnp.bfloat16)
    ffn_in_grad = outer(third, grad_up_low)
    back_third, gain_third, bias_third = pull_third(project_back(grad_up_low, ffn_in))
    grad_hidden2 = grad_out + back_third
    cross_branch = grad_hidden2.astype(jnp.bfloat16)
    cross_out_grad = outer(cross_context, cross_branch)
    grad_cross_context = project_back(cross_branch, cross_out).astype(jnp.bfloat16)
    grad_cross_q, grad_memory_kv = attend_backward(
        cross_queries, memory_kv, visible, cross_total, grad_cross_context
    )
    local_kv_grad = lax.psum_scatter(
        grad_memory_kv.astype(jnp.bfloat16), "seq", scatter_dimension=1, tiled=True
    ).astype(jnp.float32)
    cross_kv_grad = outer_full(memory, local_kv_grad)
    memory_grad = back_full(local_kv_grad, cross_kv)
    grad_cross_low = grad_cross_q.astype(jnp.bfloat16)
    cross_query_grad = outer(second, grad_cross_low)
    back_second, gain_second, bias_second = pull_second(project_back(grad_cross_low, cross_query))
    grad_hidden1 = grad_hidden2 + back_second
    self_branch = grad_hidden1.astype(jnp.bfloat16)
    self_out_grad = outer(self_context, self_branch)
    grad_self_context = project_back(self_branch, self_out).astype(jnp.bfloat16)
    grad_self_q, grad_self_kv = attend_backward(
        self_queries, self_kv, causal, self_total, grad_self_context
    )
    local_self_kv = lax.psum_scatter(grad_self_kv, "seq", scatter_dimension=1, tiled=True)
    grad_projected = jnp.concatenate([grad_self_q, local_self_kv], axis=2).astype(jnp.bfloat16)
    self_qkv_grad = outer(first, grad_projected)
    back_first, gain_first, bias_first = pull_first(project_back(grad_projected, self_qkv))
    input_grad = grad_hidden1 + back_first
    gain_terms = jnp.stack([gain_first, gain_second, gain_third])
    bias_terms = jnp.stack([bias_first, bias_second, bias_third])
    gain_total, bias_total = lax.psum((gain_terms, bias_terms), ("dp", "seq"))
    partial_value = (
        lax.psum_scatter(
            self_qkv_grad.astype(jnp.bfloat16), "dp", scatter_dimension=0, tiled=True
        ).astype(jnp.float32),
        lax.psum_scatter(
            self_out_grad.astype(jnp.bfloat16), "dp", scatter_dimension=0, tiled=True
        ).astype(jnp.float32),
        lax.psum_scatter(
            cross_query_grad.astype(jnp.bfloat16), "dp", scatter_dimension=0, tiled=True
        ).astype(jnp.float32),
        lax.psum_scatter(
            cross_kv_grad.astype(jnp.bfloat16), "dp", scatter_dimension=0, tiled=True
        ).astype(jnp.float32),
        lax.psum_scatter(
            cross_out_grad.astype(jnp.bfloat16), "dp", scatter_dimension=0, tiled=True
        ).astype(jnp.float32),
        lax.psum_scatter(
            ffn_in_grad.astype(jnp.bfloat16), "dp", scatter_dimension=0, tiled=True
        ).astype(jnp.float32),
        lax.psum_scatter(
            ffn_out_grad.astype(jnp.bfloat16), "dp", scatter_dimension=0, tiled=True
        ).astype(jnp.float32),
    )
    finished = (
        lax.psum_scatter(
            partial_value[0].astype(jnp.bfloat16), "seq", scatter_dimension=1, tiled=True
        ).astype(jnp.float32),
        lax.psum_scatter(
            partial_value[1].astype(jnp.bfloat16), "seq", scatter_dimension=1, tiled=True
        ).astype(jnp.float32),
        lax.psum_scatter(
            partial_value[2].astype(jnp.bfloat16), "seq", scatter_dimension=1, tiled=True
        ).astype(jnp.float32),
        lax.psum_scatter(
            partial_value[3].astype(jnp.bfloat16), "seq", scatter_dimension=1, tiled=True
        ).astype(jnp.float32),
        lax.psum_scatter(
            partial_value[4].astype(jnp.bfloat16), "seq", scatter_dimension=1, tiled=True
        ).astype(jnp.float32),
        lax.psum_scatter(
            partial_value[5].astype(jnp.bfloat16), "seq", scatter_dimension=1, tiled=True
        ).astype(jnp.float32),
        lax.psum_scatter(
            partial_value[6].astype(jnp.bfloat16), "seq", scatter_dimension=1, tiled=True
        ).astype(jnp.float32),
    )
    return (
        layer_out,
        input_grad,
        memory_grad,
        finished[0],
        finished[1],
        finished[2],
        finished[3],
        finished[4],
        finished[5],
        finished[6],
        gain_total,
        bias_total,
    )


def solution(mesh):
    paired = mesh.shape["dp"] == 16 and mesh.shape["seq"] == 2
    per_device = per_device_paired if paired else per_device_wide
    in_specs = (
        P("dp", "seq", None),
        P("dp", "seq", None),
        P("dp"),
        P("dp", "seq", None),
        P(),
        P(),
        P(),
        P(),
        P(),
        P(),
        P(),
        P(),
        P(),
    )
    out_specs = (
        P("dp", "seq", None),
        P("dp", "seq", None),
        P("dp", "seq", None),
        P("dp", "seq"),
        P("dp", "seq"),
        P("dp", "seq"),
        P("dp", "seq"),
        P("dp", "seq"),
        P("dp", "seq"),
        P("dp", "seq"),
        P(),
        P(),
    )
    return jax.shard_map(
        per_device, mesh=mesh, in_specs=in_specs, out_specs=out_specs, check_vma=False
    )
```

```python
import functools
import math

import jax
import jax.numpy as jnp
from jax import lax
from jax.experimental import pallas as pl
from jax.experimental.pallas import tpu as pltpu
from jax.sharding import PartitionSpec as P

HEADS = 12
HEAD_DIM = 64
MESH = pl.DeviceIdType.MESH
F32 = jnp.float32
BF16 = jnp.bfloat16
TRIPLES = 16
ORDERS = (("x", "l", "y", "h"), ("y", "x", "l", "h"), ("l", "x", "y", "h"))


def place():
    i = lax.axis_index("dp")
    return {"c": i % 2, "x": (i // 2) % 2, "l": (i // 4) % 2, "h": i // 8, "y": lax.axis_index("seq")}


def partner(axis, at):
    i = lax.axis_index("dp")
    y = at["y"]
    if axis == "y":
        return (i, 1 - y)
    step = {"c": 1, "x": 2, "l": 4, "h": 8}[axis]
    return (i + step - 2 * step * at[axis], y)


def greet(at):
    barrier = pltpu.get_barrier_semaphore()
    for axis in ("c", "x", "l", "h", "y"):
        pl.semaphore_signal(barrier, inc=1, device_id=partner(axis, at), device_id_type=MESH)
    pl.semaphore_wait(barrier, 5)


LEFT = (4, 4, 4, 4, 0, 1, 2, 3, 5, 6, 6, 8, 9, 10, 10, 10)
RIGHT = (1, 2, 3, 4, 0, 0, 0, 0, 5, 6, 7, 8, 9, 10, 11, 12)


def look_up(table, t):
    if isinstance(t, int):
        return table[t]
    value = table[-1]
    for n in range(TRIPLES - 2, -1, -1):
        if table[n] != table[n + 1]:
            value = jnp.where(t <= n, table[n], value)
    return value


def when(condition):
    if isinstance(condition, bool):
        return (lambda body: body()) if condition else (lambda body: None)
    return pl.when(condition)


def negate(condition):
    return not condition if isinstance(condition, bool) else jnp.logical_not(condition)


def store_left(lt, slot, rows_by_feature):
    for i in range(16):
        lt[slot, i % 2, 48 * (i // 2) : 48 * (i // 2) + 48, :] = rows_by_feature[48 * i : 48 * i + 48, :]


class Reducer:
    LAGS = (0, 1, 3, 5, 7, 8)
    SLOTS = (2, 3, 3, 3, 3)
    TICKS = TRIPLES + 8
    SCRATCH = [
        pltpu.VMEM((2, 3, 384, 256), BF16),
        pltpu.VMEM((TRIPLES, 3, 384, 256), BF16),
        pltpu.VMEM((3, 3, 2, 2, 2, 2, 48, 128), BF16),
        pltpu.VMEM((TRIPLES, 3, 2, 2, 2, 48, 128), BF16),
        pltpu.VMEM((3, 3, 2, 2, 2, 48, 128), BF16),
        pltpu.VMEM((TRIPLES, 3, 2, 2, 48, 128), BF16),
        pltpu.VMEM((3, 3, 2, 2, 48, 128), BF16),
        pltpu.VMEM((TRIPLES, 3, 2, 48, 128), BF16),
        pltpu.VMEM((3, 3, 2, 48, 128), BF16),
        pltpu.VMEM((TRIPLES, 3, 48, 128), BF16),
        pltpu.VMEM((3, 3, 48, 128), F32),
        pltpu.SemaphoreType.DMA((3,)),
        pltpu.SemaphoreType.DMA((5, 3, 3)),
        pltpu.SemaphoreType.DMA((5, TRIPLES, 3)),
    ]

    def __init__(self, at, lt, rg, out, s0, r0, s1, r1, s2, r2, s3, r3, s4, r4, done, done_sem, send_sem, recv_sem):
        self.at, self.lt, self.rg, self.out = at, lt, rg, out
        self.sent, self.got = (s0, s1, s2, s3, s4), (r0, r1, r2, r3, r4)
        self.done, self.done_sem = done, done_sem
        self.send_sem, self.recv_sem = send_sem, recv_sem

    def axis(self, stage, g):
        return "c" if stage == 0 else ORDERS[g][stage - 1]

    def copy(self, stage, t, g):
        axis = self.axis(stage, g)
        slot = t % self.SLOTS[stage]
        src = self.sent[stage].at[slot, g]
        if stage:
            src = src.at[1 - self.at[axis]]
        return pltpu.make_async_remote_copy(
            src_ref=src,
            dst_ref=self.got[stage].at[t, g],
            send_sem=self.send_sem.at[stage, slot, g],
            recv_sem=self.recv_sem.at[stage, t, g],
            device_id=partner(axis, self.at),
            device_id_type=MESH,
        )

    def free(self, stage, t):
        slots = self.SLOTS[stage]

        @when(t >= slots)
        def _():
            for g in range(3):
                self.copy(stage, t - slots, g).wait_send()

    def product(self, t, half, g):
        cols = slice(256 * g, 256 * g + 256)
        return jnp.dot(self.lt[look_up(LEFT, t), half], self.rg[look_up(RIGHT, t), :, cols], preferred_element_type=F32)

    def first(self, t):
        self.free(0, t)
        half = 1 - self.at["c"]
        memory = (t == 9) | (t == 10)
        for g in range(3):
            cols = slice(256 * g, 256 * g + 256)

            @when(negate(memory))
            def _():
                self.sent[0][t % 2, g] = self.product(t, half, g).astype(BF16)

            @when(memory)
            def _():
                more = jnp.dot(self.lt[7, half], self.rg[t + 4, :, cols], preferred_element_type=F32)
                self.sent[0][t % 2, g] = (self.product(t, half, g) + more).astype(BF16)

            self.copy(0, t, g).start()

    def second(self, t):
        self.free(1, t)
        half = self.at["c"]
        memory = (t == 9) | (t == 10)
        for g in range(3):
            cols = slice(256 * g, 256 * g + 256)
            self.copy(0, t, g).wait_recv()

            def spread(total):
                order = ORDERS[g]
                for b in range(8):
                    bits = {"h": b // 4, "l": (b // 2) % 2, "x": b % 2}
                    for y in range(2):
                        bits["y"] = y
                        where = tuple(bits[a] for a in order)
                        self.sent[1][(t % self.SLOTS[1], g) + where] = total[48 * b : 48 * b + 48, 128 * y : 128 * y + 128].astype(BF16)

            @when(negate(memory))
            def _():
                spread(self.product(t, half, g) + self.got[0][t, g].astype(F32))

            @when(memory)
            def _():
                more = jnp.dot(self.lt[7, half], self.rg[t + 4, :, cols], preferred_element_type=F32)
                spread(self.product(t, half, g) + more + self.got[0][t, g].astype(F32))

            self.copy(1, t, g).start()

    def write(self, t):
        return pltpu.make_async_copy(self.done.at[t % 3], self.out.at[t], self.done_sem.at[t % 3])

    def onward(self, stage, t):
        if stage < 5:
            self.free(stage, t)
        else:

            @when(t >= 3)
            def _():
                self.write(t - 3).wait()

        for g in range(3):
            self.copy(stage - 1, t, g).wait_recv()
            own = self.sent[stage - 1][t % self.SLOTS[stage - 1], g, self.at[self.axis(stage - 1, g)]]
            total = own.astype(F32) + self.got[stage - 1][t, g].astype(F32)
            if stage < 5:
                self.sent[stage][t % self.SLOTS[stage], g] = total.astype(BF16)
                self.copy(stage, t, g).start()
            else:
                self.done[t % 3, g] = total
        if stage == 5:
            self.write(t).start()

    def tick(self, n):
        for stage in range(6):
            t = n - self.LAGS[stage]

            @when((t >= (2 if stage < 2 else 0)) & (t < TRIPLES))
            def _():
                if stage == 0:
                    self.first(t)
                elif stage == 1:
                    self.second(t)
                else:
                    self.onward(stage, t)

    def drain(self):
        for t in range(TRIPLES - 3, TRIPLES):
            self.write(t).wait()
        for stage in range(5):
            for t in range(TRIPLES - self.SLOTS[stage], TRIPLES):
                for g in range(3):
                    self.copy(stage, t, g).wait_send()


NORM_ORDER = ("c", "x", "y", "l", "h")


def norm_copy(j, at, own, got, send_sem, recv_sem):
    return pltpu.make_async_remote_copy(
        src_ref=own.at[j], dst_ref=got.at[j], send_sem=send_sem.at[j], recv_sem=recv_sem.at[j],
        device_id=partner(NORM_ORDER[j], at), device_id_type=MESH,
    )


def norm_step(j, at, own, got, send_sem, recv_sem):
    if j:
        norm_copy(j - 1, at, own, got, send_sem, recv_sem).wait()
        own[j] = own[j - 1] + got[j - 1]
    if j < 5:
        norm_copy(j, at, own, got, send_sem, recv_sem).start()


LANES = 128


def normed(v):
    center = jnp.mean(v, axis=-1, keepdims=True)
    centered = v - center
    spread = jnp.mean(centered * centered, axis=-1, keepdims=True)
    scale = lax.rsqrt(spread + 1e-05)
    return centered * scale, scale


def row_blocks(step, body):
    for b in range(256 // step):
        body(slice(b * step, b * step + step))


def norm_forward(load, out, norm_gain, norm_bias, k):
    def body(rows):
        hat, _ = normed(load(rows))
        out[rows, :] = (hat * norm_gain[k : k + 1, :] + norm_bias[k : k + 1, :]).astype(BF16)

    row_blocks(64, body)


def norm_backward(load, load_grad, store, norm_gain, sums, k):
    def body(rows):
        hat, scale = normed(load(rows))
        dy = load_grad(rows)
        sums[k : k + 1, :] += jnp.sum(dy * hat, axis=0, keepdims=True)
        sums[k + 3 : k + 4, :] += jnp.sum(dy, axis=0, keepdims=True)
        dhat = dy * norm_gain[k : k + 1, :]
        mean = jnp.mean(dhat, axis=-1, keepdims=True)
        along = jnp.mean(dhat * hat, axis=-1, keepdims=True)
        store(rows, scale * (dhat - mean - hat * along))

    def run(b, carry):
        body(pl.ds(pl.multiple_of(b * 64, 64), 64))
        return carry

    lax.fori_loop(0, 4, run, 0)


def two_heads(tile):
    first = lax.broadcasted_iota(jnp.int32, tile.shape, 1) < HEAD_DIM
    zero = jnp.zeros_like(tile)
    return jnp.concatenate([jnp.where(first, tile, zero), jnp.where(first, zero, tile)], axis=0)


def upright(sideways):
    rows = sideways.shape[1] // 2
    own = jnp.concatenate([sideways[:HEAD_DIM, :rows], sideways[HEAD_DIM:, rows:]], axis=0)
    return own.T


def dot(a, b, over):
    return lax.dot_general(a, b, (over, ((), ())), preferred_element_type=F32)


LAST = ((1,), (1,))
PLAIN = ((1,), (0,))
ROWS = ((0,), (0,))


def attend(items):
    scores = [jnp.where(allowed, dot(k, two_heads(q), LAST), -1e30) for q, k, _, allowed in items]
    raised = [jnp.exp(s - jnp.max(s, axis=0, keepdims=True)) for s in scores]
    weights = [(r * (1.0 / jnp.sum(r, axis=0, keepdims=True))).astype(BF16) for r in raised]
    contexts = [upright(dot(item[2], w, ROWS).astype(BF16)) for w, item in zip(weights, items)]
    return list(zip(weights, contexts))


def attend_back(items):
    stacked = [two_heads(item[4]) for item in items]
    dweights = [dot(item[2], s, LAST) for item, s in zip(items, stacked)]
    dvs = [dot(item[3], s, PLAIN).astype(BF16) for item, s in zip(items, stacked)]
    dscores = []
    for item, d in zip(items, dweights):
        probs = item[3].astype(F32)
        terms = probs * d
        dscores.append((terms - probs * jnp.sum(terms, axis=0, keepdims=True)).astype(BF16))
    dqs = [upright((dot(item[1], d, ROWS) * (1.0 / math.sqrt(HEAD_DIM))).astype(BF16)) for item, d in zip(items, dscores)]
    dks = [dot(d, two_heads(item[0]), PLAIN).astype(BF16) for item, d in zip(items, dscores)]
    return list(zip(dqs, dks, dvs))


def in_groups(pairs, size, body):
    for n in range(0, len(pairs), size):
        body(pairs[n : n + size])


def column(slot, h, g):
    return (slot, slice(None), pl.ds(pl.multiple_of(256 * g + LANES * h, LANES), LANES))


def back(rg, slots, weight, rows=None):
    half = weight.shape[1] // 2
    total = None
    for j, slot in enumerate(slots):
        for g in range(3):
            at = j * 384 + g * LANES
            w = jnp.concatenate([weight[:, at : at + LANES], weight[:, half + at : half + at + LANES]], axis=1)
            term = dot(rg[slot, :, 256 * g : 256 * g + 256], w, LAST)
            total = term if total is None else total + term
    return total


CHUNKS = (0, 3, 1, 4, 2, 5)


def layer_kernel(
    dec_input, memory, src_len, out_grad, self_qkv, self_out, cross_query, cross_kv, cross_out, ffn_in, ffn_out,
    norm_gain, norm_bias,
    o_layer, o_input, o_memory, units, norm_out,
    x_in, mem, og, w_qkv, w_self, w_query, w_kv, w_cross, w_in, w_out,
    normal, qkv, p_self, context, hidden1, qx, kv, p_cross, hidden2,
    active, acc, dthird,
    lt, rg, n_own, n_got, n_send, n_recv, load_sem, swap_send, swap_recv, out_sem, out_send, out_recv, *rest
):
    at = place()
    y = at["y"]
    red = Reducer(at, lt, rg, units, *rest)
    across = partner("y", at)

    loads = [
        pltpu.make_async_copy(src, dst, load_sem.at[n])
        for n, (src, dst) in enumerate(
            ((self_qkv, w_qkv), (self_out, w_self), (cross_kv, w_kv), (cross_query, w_query), (cross_out, w_cross))
        )
    ]
    for load in loads:
        load.start()

    def ffn_load(n):
        cols = slice(CHUNKS[n] * 512, CHUNKS[n] * 512 + 512)
        slot = n % 3
        return (
            pltpu.make_async_copy(ffn_in.at[:, cols], w_in.at[slot], load_sem.at[5 + slot]),
            pltpu.make_async_copy(ffn_out.at[cols, :], w_out.at[slot], load_sem.at[8 + slot]),
        )

    for n in range(3):
        for load in ffn_load(n):
            load.start()

    def own_rows(n, src, dst, rows):
        return [
            pltpu.make_async_copy(
                src.at[2 * y + e], dst.at[pl.ds(pl.multiple_of(2 * e * rows + y * rows, rows), rows), :], load_sem.at[11 + 2 * n + e]
            )
            for e in range(2)
        ]

    def swap(n, src, dst, rows):
        return [
            pltpu.make_async_remote_copy(
                src_ref=src.at[2 * (1 - y) + e],
                dst_ref=dst.at[pl.ds(pl.multiple_of(2 * e * rows + y * rows, rows), rows), :],
                send_sem=swap_send.at[n, e], recv_sem=swap_recv.at[n, e], device_id=across, device_id_type=MESH,
            )
            for e in range(2)
        ]

    moved = ((dec_input, x_in, 64), (memory, mem, 128), (out_grad, og, 64))
    owns = [own_rows(n, *m) for n, m in enumerate(moved)]
    swaps = [swap(n, *m) for n, m in enumerate(moved)]
    for own in owns:
        for copy in own:
            copy.start()
    greet(at)
    for copy in swaps[0]:
        copy.start()
    for copy in swaps[1]:
        copy.start()
    for copy in swaps[2]:
        copy.start()

    def own_here(n):
        for copy in owns[n]:
            copy.wait()

    def other_here(n, e):
        swaps[n][e].wait()

    scale = 1.0 / math.sqrt(HEAD_DIM)

    own_here(0)
    for e in range(2):
        other_here(0, e)
    norm_forward(lambda rows: x_in[rows, :].astype(F32), normal, norm_gain, norm_bias, 0)
    loads[0].wait()

    for n in range(9):
        out = jnp.dot(normal[...], w_qkv[:, 256 * n : 256 * n + 256], preferred_element_type=F32)
        out = (out * scale if n < 3 else out).astype(BF16)
        qkv[2 * n] = out[:, 0:LANES]
        qkv[2 * n + 1] = out[:, LANES:256]

    store_left(lt, 10, normal[...].T)

    def pair(e, p):
        return slice(e * 128, e * 128 + 128), slice(p * LANES, p * LANES + LANES)

    pairs = [(e, p) for p in range(6) for e in range(2)]

    def self_operands(e, p):
        rows, _ = pair(e, p)
        return qkv[p, rows, :], qkv[6 + p, rows, :], qkv[12 + p, rows, :]

    def self_forward(group):
        k_at = lax.broadcasted_iota(jnp.int32, (128, 256), 0)
        q_at = lax.broadcasted_iota(jnp.int32, (128, 256), 1) % 128
        results = attend([(*self_operands(e, p), q_at >= k_at) for e, p in group])
        for (e, p), (weights, values) in zip(group, results):
            p_self[6 * e + p] = weights
            context[pair(e, p)] = values

    in_groups(pairs, 4, self_forward)

    loads[1].wait()
    for n in range(3):
        cols = slice(256 * n, 256 * n + 256)
        hidden1[:, cols] = x_in[:, cols].astype(F32) + jnp.dot(context[...], w_self[:, cols], preferred_element_type=F32)
    store_left(lt, 9, context[...].T)
    norm_forward(lambda rows: hidden1[rows, :], normal, norm_gain, norm_bias, 1)

    loads[3].wait()
    for n in range(3):
        out = jnp.dot(normal[...], w_query[:, 256 * n : 256 * n + 256], preferred_element_type=F32)
        out = (out * scale).astype(BF16)
        qx[2 * n] = out[:, 0:LANES]
        qx[2 * n + 1] = out[:, LANES:256]
    store_left(lt, 8, normal[...].T)
    loads[2].wait()
    own_here(1)

    def project_kv(blocks):
        rows = [pl.ds(pl.multiple_of(at_, 128), 128) for at_ in blocks]
        source = jnp.concatenate([mem[r, :] for r in rows], axis=0)
        for n in range(6):
            out = jnp.dot(source, w_kv[:, 256 * n : 256 * n + 256], preferred_element_type=F32).astype(BF16)
            for k, r in enumerate(rows):
                kv[2 * n, r, :] = out[128 * k : 128 * k + 128, 0:LANES]
                kv[2 * n + 1, r, :] = out[128 * k : 128 * k + 128, LANES:256]

    project_kv([128 * y, 256 + 128 * y])

    def cross_operands(e, p):
        rows, keys = pair(e, p)[0], slice(e * 256, e * 256 + 256)
        return qx[p, rows, :], kv[p, keys, :], kv[6 + p, keys, :]

    def cross_forward(group):
        k_at = lax.broadcasted_iota(jnp.int32, (256, 256), 0)
        results = attend([(*cross_operands(e, p), k_at < src_len[2 * y + e]) for e, p in group])
        for (e, p), (weights, values) in zip(group, results):
            p_cross[6 * e + p] = weights
            context[pair(e, p)] = values

    for e in range(2):
        other_here(1, e)
        project_kv([256 * e + 128 * (1 - y)])
        cross_forward([(e, p) for p in range(6)])

    loads[4].wait()
    for n in range(3):
        cols = slice(256 * n, 256 * n + 256)
        hidden2[:, cols] = hidden1[:, cols] + jnp.dot(context[...], w_cross[:, cols], preferred_element_type=F32)
    norm_forward(lambda rows: hidden2[rows, :], normal, norm_gain, norm_bias, 2)

    own_here(2)
    for e in range(2):
        other_here(2, e)

    def spread(slot, rows_of):
        for g in range(3):
            for h in range(2):
                lane = h * 384 + g * LANES
                rg[slot, :, 256 * g + LANES * h : 256 * g + LANES * h + LANES] = rows_of[:, lane : lane + LANES].astype(BF16)

    acc[...] = jnp.zeros_like(acc)
    dthird[...] = jnp.zeros_like(dthird)
    root = math.sqrt(2.0 / math.pi)

    def up_tile(tile):
        lane = 256 * (tile % 3) + LANES * (tile // 12)
        return (1 + (tile % 12) // 3, slice(None), slice(lane, lane + LANES))

    def feed_in(n, s):
        slot, cols = n % 3, slice(256 * s, 256 * s + 256)
        up = jnp.dot(normal[...], w_in[slot, :, cols], preferred_element_type=F32)
        return up, dot(og[...], w_out[slot, cols, :], LAST)

    def feed_bend(n, s, up, dact):
        square = up * up
        bend = jnp.tanh(up * (root + (root * 0.044715) * square))
        lift = 0.5 + 0.5 * bend
        active[n % 2, :, 256 * s : 256 * s + 256] = (up * lift).astype(BF16)
        slope = lift + (0.5 * up) * (1.0 - bend * bend) * (root + (3.0 * 0.044715 * root) * square)
        grad = (dact * slope).astype(BF16)
        for t in range(2):
            rg[up_tile(4 * CHUNKS[n] + 2 * s + t)] = grad[:, LANES * t : LANES * t + LANES]

    def feed_out(n, k):
        slot, cols = n % 3, slice(256 * k, 256 * k + 256)
        acc[:, cols] += jnp.dot(active[n % 2], w_out[slot, :, cols], preferred_element_type=F32)
        dup = jnp.concatenate([rg[up_tile(4 * CHUNKS[n] + t)] for t in range(4)], axis=1)
        dthird[:, cols] += dot(dup, w_in[slot, cols, :], LAST)

    def feed_left(n):
        flipped = active[n % 2].T
        at_ = 0
        while at_ < 512:
            feature = CHUNKS[n] * 512 + at_
            i, k, r = feature // 192, (feature % 192) // 48, feature % 48
            size = min(48 - r, 512 - at_)
            to = 48 * (i // 2) + r
            lt[k, i % 2, to : to + size, :] = flipped[at_ : at_ + size, :]
            at_ += size

    def feed(n):
        for load in ffn_load(n):
            load.wait()
        for s in range(2):
            up, dact = feed_in(n, s)
            if n:
                for k in ((0, 1), (2,))[s]:
                    feed_out(n - 1, k)
            feed_bend(n, s, up, dact)
        if n:
            feed_left(n - 1)
            if n < 4:
                for load in ffn_load(n + 2):
                    load.start()

    PIECES = (
        [(normal, o_layer, 64, e, r) for e in range(2) for r in (0, 32)]
        + [(mem, o_memory, 128, e, r) for e in range(2) for r in (0, 32, 64, 96)]
        + [(x_in, o_input, 64, e, r) for e in range(2) for r in (0, 32)]
    )

    def piece(n, leaving):
        buf, out, rows, e, r = PIECES[n]
        which = 1 - y if leaving else y
        src = buf.at[pl.ds(pl.multiple_of(2 * e * rows + which * rows + r, 32), 32), :]
        dst = out.at[2 * y + e, r : r + 32, :]
        if not leaving:
            return pltpu.make_async_copy(src, dst, out_sem.at[n])
        return pltpu.make_async_remote_copy(
            src_ref=src, dst_ref=dst, send_sem=out_send.at[n], recv_sem=out_recv.at[n], device_id=across, device_id_type=MESH
        )

    def send(n):
        piece(n, True).start()
        piece(n, False).start()

    feed(0)
    feed(1)
    store_left(lt, 4, normal[...].T)
    red.first(0)
    feed(2)
    red.second(0)
    feed(3)
    red.first(1)
    feed(4)
    red.second(1)
    feed(5)
    for k in range(3):
        feed_out(5, k)
    feed_left(5)
    spread(0, og)

    sums = n_own.at[0]
    sums[...] = jnp.zeros(sums.shape, F32)
    dc = context

    def store_grad(rows, value):
        acc[rows, :] = value

    def store_input(rows, v):
        x_in[rows, :] = (acc[rows, :] + v).astype(BF16)

    def context_grad(slot, weight):
        for n in range(3):
            rows = slice(256 * n, 256 * n + 256)
            dc[:, rows] = back(rg, (slot,), weight.at[rows, :]).astype(BF16)

    def cross_backward(group):
        results = attend_back([(*cross_operands(e, p), p_cross[6 * e + p], dc[pair(e, p)]) for e, p in group])
        for (e, p), (dq, dk, dv) in zip(group, results):
            j, g = p // 3, p % 3
            rg[8, pair(e, p)[0], 256 * g + LANES * j : 256 * g + LANES * j + LANES] = dq
            rg[6 + 7 * e + j, :, 256 * g : 256 * g + LANES] = dk
            rg[6 + 7 * e + j, :, 256 * g + LANES : 256 * g + 256] = dv

    def self_backward(group):
        results = attend_back([(*self_operands(e, p), p_self[6 * e + p], dc[pair(e, p)]) for e, p in group])
        for (e, p), values in zip(group, results):
            for n, value in enumerate(values):
                tile = 6 * n + p
                lane = 256 * (tile % 3) + LANES * (tile // 9)
                rg[10 + (tile % 9) // 3, pair(e, p)[0], lane : lane + LANES] = value

    def memory_rows(e):
        for n in range(3):
            rows = slice(256 * n, 256 * n + 256)
            mem[256 * e : 256 * e + 256, rows] = back(rg, (6 + 7 * e, 7 + 7 * e), w_kv.at[rows, :]).astype(BF16)

    def back_rows(slots, weight):
        for n in range(3):
            rows = slice(256 * n, 256 * n + 256)
            dthird[:, rows] = back(rg, slots, weight.at[rows, :])

    def piece_3():
        normal[...] = (hidden2[...] + acc[...]).astype(BF16)
        norm_backward(
            lambda rows: hidden2[rows, :], lambda rows: dthird[rows, :],
            lambda rows, v: store_grad(rows, og[rows, :].astype(F32) + v), norm_gain, sums, 2,
        )
        spread(5, acc)

    def piece_4():
        store_left(lt, 5, context[...].T)
        context_grad(5, w_cross)

    def piece_5():
        in_groups(pairs[:6], 3, cross_backward)

    def piece_6():
        in_groups(pairs[6:], 3, cross_backward)
        store_left(lt, 6, mem[0:256, :].T)
        store_left(lt, 7, mem[256:512, :].T)
        memory_rows(0)

    def piece_7():
        memory_rows(1)
        back_rows((8,), w_query)

    def piece_8():
        norm_backward(
            lambda rows: hidden1[rows, :], lambda rows: dthird[rows, :],
            lambda rows, v: store_grad(rows, acc[rows, :] + v), norm_gain, sums, 1,
        )
        spread(9, acc)
        context_grad(9, w_self)

    def piece_9():
        in_groups(pairs[:6], 3, self_backward)

    def piece_10():
        in_groups(pairs[6:], 3, self_backward)

    def piece_11():
        back_rows((10, 11, 12), w_qkv)

    def piece_12():
        norm_backward(
            lambda rows: x_in[rows, :].astype(F32), lambda rows: dthird[rows, :], store_input, norm_gain, sums, 0
        )

    pieces = (piece_3, piece_4, piece_5, piece_6, piece_7, piece_8, piece_9, piece_10, piece_11, piece_12)

    def body(n, carry):
        for k, run in enumerate(pieces):
            pl.when(n == 3 + k)(run)
        red.tick(n)
        for j in range(6):
            @pl.when(n == 12 + j)
            def _():
                norm_step(j, at, n_own, n_got, n_send, n_recv)

        for k in range(16):
            @pl.when(n == k + 3)
            def _():
                send(k)

        return carry

    lax.fori_loop(2, red.TICKS, body, 0)
    norm_out[...] = n_own[5]
    red.drain()
    for n in range(16):
        piece(n, True).wait()
        piece(n, False).wait()


def layer_call(args):
    anywhere = pl.BlockSpec(memory_space=pl.ANY)
    vmem = pl.BlockSpec(memory_space=pltpu.VMEM)
    rows = lambda width, kind=BF16: pltpu.VMEM((256, width), kind)
    return pl.pallas_call(
        layer_kernel,
        out_shape=(
            jax.ShapeDtypeStruct((4, 64, 768), BF16),
            jax.ShapeDtypeStruct((4, 64, 768), BF16),
            jax.ShapeDtypeStruct((4, 128, 768), BF16),
            jax.ShapeDtypeStruct((TRIPLES, 3, 48, 128), F32),
            jax.ShapeDtypeStruct((8, 768), F32),
        ),
        in_specs=[anywhere, anywhere, pl.BlockSpec(memory_space=pltpu.SMEM)] + [anywhere] * 8 + [vmem] * 2,
        out_specs=(anywhere, anywhere, anywhere, anywhere, vmem),
        scratch_shapes=[
            rows(768), pltpu.VMEM((512, 768), BF16), rows(768),
            pltpu.VMEM((768, 2304), BF16), pltpu.VMEM((768, 768), BF16), pltpu.VMEM((768, 768), BF16),
            pltpu.VMEM((768, 1536), BF16), pltpu.VMEM((768, 768), BF16),
            pltpu.VMEM((3, 768, 512), BF16), pltpu.VMEM((3, 512, 768), BF16),
            rows(768), pltpu.VMEM((18, 256, 128), BF16), pltpu.VMEM((12, 128, 256), BF16), rows(768),
            rows(768, F32), pltpu.VMEM((6, 256, 128), BF16), pltpu.VMEM((12, 512, 128), BF16),
            pltpu.VMEM((12, 256, 256), BF16), rows(768, F32),
            pltpu.VMEM((2, 256, 512), BF16), rows(768, F32), rows(768, F32),
            pltpu.VMEM((11, 2, 384, 256), BF16),
            pltpu.VMEM((15, 256, 768), BF16),
            pltpu.VMEM((6, 8, 768), F32),
            pltpu.VMEM((5, 8, 768), F32),
            pltpu.SemaphoreType.DMA((5,)),
            pltpu.SemaphoreType.DMA((5,)),
            pltpu.SemaphoreType.DMA((17,)),
            pltpu.SemaphoreType.DMA((3, 2)),
            pltpu.SemaphoreType.DMA((3, 2)),
            pltpu.SemaphoreType.DMA((16,)),
            pltpu.SemaphoreType.DMA((16,)),
            pltpu.SemaphoreType.DMA((16,)),
        ] + Reducer.SCRATCH,
        compiler_params=pltpu.CompilerParams(collective_id=0, has_side_effects=True, vmem_limit_bytes=61 << 20),
    )(*args)


WEIGHTS = ((13, 3), (12, 1), (11, 1), (9, 2), (8, 1), (0, 4))


def finish_kernel(layer, inputs, memories, units, norms, *refs):
    o_layer, o_input, o_memory = refs[0:3]
    o_weights, o_ffn_out, o_gain, o_bias = refs[3:9], refs[9], refs[10], refs[11]
    low_input, low_memory, high_input, high_memory, blocks = refs[12:17]
    w_bufs, ffn_buf, sem, out_sem, low_layer = refs[17:23], refs[23], refs[24], refs[25], refs[26]
    loads = [
        pltpu.make_async_copy(units, blocks, sem.at[0]),
        pltpu.make_async_copy(memories, low_memory, sem.at[1]),
        pltpu.make_async_copy(inputs, low_input, sem.at[2]),
        pltpu.make_async_copy(layer, low_layer, sem.at[3]),
    ]
    for load in loads:
        load.start()
    stores = []

    def store(src, dst):
        copy = pltpu.make_async_copy(src, dst, out_sem.at[len(stores)])
        copy.start()
        stores.append(copy)

    o_gain[...] = norms[0:3, :]
    o_bias[...] = norms[3:6, :]
    loads[0].wait()
    for (t, count), buf, out in zip(WEIGHTS, w_bufs, o_weights):
        for j in range(count):
            for g in range(3):
                buf[:, j * 384 + g * LANES : j * 384 + g * LANES + LANES] = blocks[t + j, g]
        store(buf, out)
    for k in range(4):
        for g in range(3):
            ffn_buf[48 * k : 48 * k + 48, g * LANES : g * LANES + LANES] = blocks[4 + k, g]
    store(ffn_buf, o_ffn_out)
    loads[1].wait()
    for e in range(4):
        high_memory[e] = low_memory[e].astype(F32)
        store(high_memory.at[e], o_memory.at[e])
    loads[2].wait()
    high_input[...] = low_input[...].astype(F32)
    store(high_input, o_input)
    loads[3].wait()
    store(low_layer, o_layer)
    for copy in stores:
        copy.wait()


def finish_call(layer, inputs, memories, units, norms):
    anywhere = pl.BlockSpec(memory_space=pl.ANY)
    vmem = pl.BlockSpec(memory_space=pltpu.VMEM)
    widths = [count * 384 for _, count in WEIGHTS]
    return pl.pallas_call(
        finish_kernel,
        out_shape=(
            jax.ShapeDtypeStruct(layer.shape, BF16),
            jax.ShapeDtypeStruct(inputs.shape, F32),
            jax.ShapeDtypeStruct(memories.shape, F32),
            *[jax.ShapeDtypeStruct((48, w), F32) for w in widths],
            jax.ShapeDtypeStruct((192, 384), F32),
            jax.ShapeDtypeStruct((3, 768), F32),
            jax.ShapeDtypeStruct((3, 768), F32),
        ),
        in_specs=[anywhere] * 4 + [vmem],
        out_specs=(anywhere,) * 10 + (vmem, vmem),
        scratch_shapes=[
            pltpu.VMEM(inputs.shape, BF16), pltpu.VMEM(memories.shape, BF16),
            pltpu.VMEM(inputs.shape, F32), pltpu.VMEM(memories.shape, F32), pltpu.VMEM(units.shape, F32),
            *[pltpu.VMEM((48, w), F32) for w in widths], pltpu.VMEM((192, 384), F32),
            pltpu.SemaphoreType.DMA((4,)), pltpu.SemaphoreType.DMA((13,)), pltpu.VMEM(layer.shape, BF16),
        ],
        compiler_params=pltpu.CompilerParams(vmem_limit_bytes=60 << 20),
    )(layer, inputs, memories, units, norms)


def per_device_paired(*args):
    return finish_call(*layer_call(args))

def layer_norm(x, gain, shift):
    center = jnp.mean(x, axis=-1, keepdims=True)
    centered = x - center
    spread = jnp.mean(centered * centered, axis=-1, keepdims=True)
    return centered * lax.rsqrt(spread + 1e-05) * gain + shift


def smooth(v):
    return jax.nn.gelu(v, approximate=True)


def project(rows, weight):
    return jnp.einsum("etd,df->etf", rows, weight, preferred_element_type=jnp.float32)


def project_back(grads, weight):
    return jnp.einsum("etf,df->etd", grads, weight, preferred_element_type=jnp.float32)


def outer(rows, grads):
    return jnp.einsum("etd,etf->df", rows, grads, preferred_element_type=jnp.float32)


def outer_full(rows, grads):
    return jnp.einsum(
        "etd,etf->df", rows.astype(jnp.float32), grads, precision=lax.Precision.HIGHEST
    )


def back_full(grads, weight):
    return jnp.einsum(
        "etf,df->etd", grads, weight.astype(jnp.float32), precision=lax.Precision.HIGHEST
    )


def split_heads(queries, key_values):
    examples, rows, width = queries.shape
    count = key_values.shape[1]
    heads_q = queries.reshape(examples, rows, HEADS, HEAD_DIM)
    heads_k = key_values[:, :, :width].reshape(examples, count, HEADS, HEAD_DIM)
    heads_v = key_values[:, :, width:].reshape(examples, count, HEADS, HEAD_DIM)
    return (heads_q, heads_k, heads_v)


def masked_logits(heads_q, heads_k, allowed):
    scores = jnp.einsum("eqhd,ekhd->ehqk", heads_q, heads_k, preferred_element_type=jnp.float32)
    return jnp.where(allowed, scores * (1.0 / math.sqrt(HEAD_DIM)), -1e30)


def attend_forward(queries, key_values, allowed):
    examples, rows, width = queries.shape
    heads_q, heads_k, heads_v = split_heads(queries, key_values)
    logits = masked_logits(heads_q, heads_k, allowed)
    row_top = jnp.max(logits, axis=-1, keepdims=True)
    raised = jnp.where(allowed, jnp.exp(logits - row_top), 0.0)
    row_total = jnp.sum(raised, axis=-1, keepdims=True)
    weights = (raised / row_total).astype(jnp.bfloat16)
    context = jnp.einsum("ehqk,ekhd->eqhd", weights, heads_v, preferred_element_type=jnp.float32)
    return (
        context.reshape(examples, rows, width).astype(jnp.bfloat16),
        row_top + jnp.log(row_total),
    )


def attend_backward(queries, key_values, allowed, log_total, grad_context):
    examples, rows, width = queries.shape
    count = key_values.shape[1]
    heads_q, heads_k, heads_v = split_heads(queries, key_values)
    logits = masked_logits(heads_q, heads_k, allowed)
    soft = jnp.where(allowed, jnp.exp(logits - log_total), 0.0)
    grad_heads = grad_context.reshape(examples, rows, HEADS, HEAD_DIM)
    grad_soft = jnp.einsum(
        "eqhd,ekhd->ehqk", grad_heads, heads_v, preferred_element_type=jnp.float32
    )
    grad_values = jnp.einsum(
        "ehqk,eqhd->ekhd", soft.astype(jnp.bfloat16), grad_heads, preferred_element_type=jnp.float32
    )
    inner = jnp.sum(soft * grad_soft, axis=-1, keepdims=True)
    grad_scores = (soft * (grad_soft - inner) * (1.0 / math.sqrt(HEAD_DIM))).astype(jnp.bfloat16)
    grad_queries = jnp.einsum(
        "ehqk,ekhd->eqhd", grad_scores, heads_k, preferred_element_type=jnp.float32
    )
    grad_keys = jnp.einsum(
        "ehqk,eqhd->ekhd", grad_scores, heads_q, preferred_element_type=jnp.float32
    )
    joined = jnp.concatenate(
        [grad_keys.reshape(examples, count, width), grad_values.reshape(examples, count, width)],
        axis=2,
    )
    return (grad_queries.reshape(examples, rows, width), joined)


def per_device_wide(
    dec_input,
    memory,
    src_len,
    out_grad,
    self_qkv,
    self_out,
    cross_query,
    cross_kv,
    cross_out,
    ffn_in,
    ffn_out,
    norm_gain,
    norm_bias,
):
    examples, local_rows, width = dec_input.shape
    local_sources = memory.shape[1]
    seq_count = lax.axis_size("seq")
    all_targets = local_rows * seq_count
    all_sources = local_sources * seq_count
    rank = lax.axis_index("seq")
    x = dec_input.astype(jnp.float32)
    first_f, pull_first = jax.vjp(layer_norm, x, norm_gain[0], norm_bias[0])
    first = first_f.astype(jnp.bfloat16)
    projected = project(first, self_qkv).astype(jnp.bfloat16)
    self_queries = projected[:, :, :width]
    self_kv = lax.all_gather(projected[:, :, width:], "seq", axis=1, tiled=True)
    query_place = rank * local_rows + jnp.arange(local_rows, dtype=jnp.int32)
    key_place = jnp.arange(all_targets, dtype=jnp.int32)
    causal = (query_place[:, None] >= key_place[None, :])[None, None]
    self_context, self_total = attend_forward(self_queries, self_kv, causal)
    hidden1 = x + project(self_context, self_out)
    second_f, pull_second = jax.vjp(layer_norm, hidden1, norm_gain[1], norm_bias[1])
    second = second_f.astype(jnp.bfloat16)
    cross_queries = project(second, cross_query).astype(jnp.bfloat16)
    gathered = lax.all_gather(memory, "seq", axis=1, tiled=True)
    memory_kv = project(gathered, cross_kv).astype(jnp.bfloat16)
    source_place = jnp.arange(all_sources, dtype=jnp.int32)
    visible = (source_place[None, :] < src_len[:, None])[:, None, None, :]
    cross_context, cross_total = attend_forward(cross_queries, memory_kv, visible)
    hidden2 = hidden1 + project(cross_context, cross_out)
    third_f, pull_third = jax.vjp(layer_norm, hidden2, norm_gain[2], norm_bias[2])
    third = third_f.astype(jnp.bfloat16)
    raised_up = project(third, ffn_in)
    active_f, pull_smooth = jax.vjp(smooth, raised_up)
    activated = active_f.astype(jnp.bfloat16)
    layer_out = (hidden2 + project(activated, ffn_out)).astype(jnp.bfloat16)
    grad_out = out_grad.astype(jnp.float32)
    ffn_out_grad = outer(activated, out_grad)
    (grad_up,) = pull_smooth(project_back(out_grad, ffn_out))
    grad_up_low = grad_up.astype(jnp.bfloat16)
    ffn_in_grad = outer(third, grad_up_low)
    back_third, gain_third, bias_third = pull_third(project_back(grad_up_low, ffn_in))
    grad_hidden2 = grad_out + back_third
    cross_branch = grad_hidden2.astype(jnp.bfloat16)
    cross_out_grad = outer(cross_context, cross_branch)
    grad_cross_context = project_back(cross_branch, cross_out).astype(jnp.bfloat16)
    grad_cross_q, grad_memory_kv = attend_backward(
        cross_queries, memory_kv, visible, cross_total, grad_cross_context
    )
    local_kv_grad = lax.psum_scatter(
        grad_memory_kv.astype(jnp.bfloat16), "seq", scatter_dimension=1, tiled=True
    ).astype(jnp.float32)
    cross_kv_grad = outer_full(memory, local_kv_grad)
    memory_grad = back_full(local_kv_grad, cross_kv)
    grad_cross_low = grad_cross_q.astype(jnp.bfloat16)
    cross_query_grad = outer(second, grad_cross_low)
    back_second, gain_second, bias_second = pull_second(project_back(grad_cross_low, cross_query))
    grad_hidden1 = grad_hidden2 + back_second
    self_branch = grad_hidden1.astype(jnp.bfloat16)
    self_out_grad = outer(self_context, self_branch)
    grad_self_context = project_back(self_branch, self_out).astype(jnp.bfloat16)
    grad_self_q, grad_self_kv = attend_backward(
        self_queries, self_kv, causal, self_total, grad_self_context
    )
    local_self_kv = lax.psum_scatter(grad_self_kv, "seq", scatter_dimension=1, tiled=True)
    grad_projected = jnp.concatenate([grad_self_q, local_self_kv], axis=2).astype(jnp.bfloat16)
    self_qkv_grad = outer(first, grad_projected)
    back_first, gain_first, bias_first = pull_first(project_back(grad_projected, self_qkv))
    input_grad = grad_hidden1 + back_first
    gain_terms = jnp.stack([gain_first, gain_second, gain_third])
    bias_terms = jnp.stack([bias_first, bias_second, bias_third])
    gain_total, bias_total = lax.psum((gain_terms, bias_terms), ("dp", "seq"))
    partial_value = (
        lax.psum_scatter(
            self_qkv_grad.astype(jnp.bfloat16), "dp", scatter_dimension=0, tiled=True
        ).astype(jnp.float32),
        lax.psum_scatter(
            self_out_grad.astype(jnp.bfloat16), "dp", scatter_dimension=0, tiled=True
        ).astype(jnp.float32),
        lax.psum_scatter(
            cross_query_grad.astype(jnp.bfloat16), "dp", scatter_dimension=0, tiled=True
        ).astype(jnp.float32),
        lax.psum_scatter(
            cross_kv_grad.astype(jnp.bfloat16), "dp", scatter_dimension=0, tiled=True
        ).astype(jnp.float32),
        lax.psum_scatter(
            cross_out_grad.astype(jnp.bfloat16), "dp", scatter_dimension=0, tiled=True
        ).astype(jnp.float32),
        lax.psum_scatter(
            ffn_in_grad.astype(jnp.bfloat16), "dp", scatter_dimension=0, tiled=True
        ).astype(jnp.float32),
        lax.psum_scatter(
            ffn_out_grad.astype(jnp.bfloat16), "dp", scatter_dimension=0, tiled=True
        ).astype(jnp.float32),
    )
    finished = (
        lax.psum_scatter(
            partial_value[0].astype(jnp.bfloat16), "seq", scatter_dimension=1, tiled=True
        ).astype(jnp.float32),
        lax.psum_scatter(
            partial_value[1].astype(jnp.bfloat16), "seq", scatter_dimension=1, tiled=True
        ).astype(jnp.float32),
        lax.psum_scatter(
            partial_value[2].astype(jnp.bfloat16), "seq", scatter_dimension=1, tiled=True
        ).astype(jnp.float32),
        lax.psum_scatter(
            partial_value[3].astype(jnp.bfloat16), "seq", scatter_dimension=1, tiled=True
        ).astype(jnp.float32),
        lax.psum_scatter(
            partial_value[4].astype(jnp.bfloat16), "seq", scatter_dimension=1, tiled=True
        ).astype(jnp.float32),
        lax.psum_scatter(
            partial_value[5].astype(jnp.bfloat16), "seq", scatter_dimension=1, tiled=True
        ).astype(jnp.float32),
        lax.psum_scatter(
            partial_value[6].astype(jnp.bfloat16), "seq", scatter_dimension=1, tiled=True
        ).astype(jnp.float32),
    )
    return (
        layer_out,
        input_grad,
        memory_grad,
        finished[0],
        finished[1],
        finished[2],
        finished[3],
        finished[4],
        finished[5],
        finished[6],
        gain_total,
        bias_total,
    )


def solution(mesh):
    paired = mesh.shape["dp"] == 16 and mesh.shape["seq"] == 2
    per_device = per_device_paired if paired else per_device_wide
    in_specs = (
        P("dp", "seq", None),
        P("dp", "seq", None),
        P("dp"),
        P("dp", "seq", None),
        P(),
        P(),
        P(),
        P(),
        P(),
        P(),
        P(),
        P(),
        P(),
    )
    out_specs = (
        P("dp", "seq", None),
        P("dp", "seq", None),
        P("dp", "seq", None),
        P("dp", "seq"),
        P("dp", "seq"),
        P("dp", "seq"),
        P("dp", "seq"),
        P("dp", "seq"),
        P("dp", "seq"),
        P("dp", "seq"),
        P(),
        P(),
    )
    return jax.shard_map(
        per_device, mesh=mesh, in_specs=in_specs, out_specs=out_specs, check_vma=False
    )
```

```python
import functools
import math

import jax
import jax.numpy as jnp
from jax import lax
from jax.experimental import pallas as pl
from jax.experimental.pallas import tpu as pltpu
from jax.sharding import PartitionSpec as P

HEADS = 12
HEAD_DIM = 64
MESH = pl.DeviceIdType.MESH
F32 = jnp.float32
BF16 = jnp.bfloat16
TRIPLES = 16
ORDERS = (("x", "l", "y", "h"), ("y", "x", "l", "h"), ("l", "x", "y", "h"))


def place():
    i = lax.axis_index("dp")
    return {"c": i % 2, "x": (i // 2) % 2, "l": (i // 4) % 2, "h": i // 8, "y": lax.axis_index("seq")}


def partner(axis, at):
    i = lax.axis_index("dp")
    y = at["y"]
    if axis == "y":
        return (i, 1 - y)
    step = {"c": 1, "x": 2, "l": 4, "h": 8}[axis]
    return (i + step - 2 * step * at[axis], y)


def greet(at):
    barrier = pltpu.get_barrier_semaphore()
    for axis in ("c", "x", "l", "h", "y"):
        pl.semaphore_signal(barrier, inc=1, device_id=partner(axis, at), device_id_type=MESH)
    pl.semaphore_wait(barrier, 5)


LEFT = (4, 4, 4, 4, 0, 1, 2, 3, 5, 6, 6, 8, 9, 10, 10, 10)
RIGHT = (1, 2, 3, 4, 0, 0, 0, 0, 5, 6, 7, 8, 9, 10, 11, 12)


def look_up(table, t):
    if isinstance(t, int):
        return table[t]
    value = table[-1]
    for n in range(TRIPLES - 2, -1, -1):
        if table[n] != table[n + 1]:
            value = jnp.where(t <= n, table[n], value)
    return value


def when(condition):
    if isinstance(condition, bool):
        return (lambda body: body()) if condition else (lambda body: None)
    return pl.when(condition)


def negate(condition):
    return not condition if isinstance(condition, bool) else jnp.logical_not(condition)


def store_left(lt, slot, rows_by_feature):
    for i in range(16):
        lt[slot, i % 2, 48 * (i // 2) : 48 * (i // 2) + 48, :] = rows_by_feature[48 * i : 48 * i + 48, :]


class Reducer:
    LAGS = (0, 1, 3, 5, 7, 8)
    SLOTS = (2, 3, 3, 3, 3)
    TICKS = TRIPLES + 8
    SCRATCH = [
        pltpu.VMEM((2, 3, 384, 256), BF16),
        pltpu.VMEM((TRIPLES, 3, 384, 256), BF16),
        pltpu.VMEM((3, 3, 2, 2, 2, 2, 48, 128), BF16),
        pltpu.VMEM((TRIPLES, 3, 2, 2, 2, 48, 128), BF16),
        pltpu.VMEM((3, 3, 2, 2, 2, 48, 128), BF16),
        pltpu.VMEM((TRIPLES, 3, 2, 2, 48, 128), BF16),
        pltpu.VMEM((3, 3, 2, 2, 48, 128), BF16),
        pltpu.VMEM((TRIPLES, 3, 2, 48, 128), BF16),
        pltpu.VMEM((3, 3, 2, 48, 128), BF16),
        pltpu.VMEM((TRIPLES, 3, 48, 128), BF16),
        pltpu.VMEM((3, 3, 48, 128), F32),
        pltpu.SemaphoreType.DMA((3,)),
        pltpu.SemaphoreType.DMA((5, 3, 3)),
        pltpu.SemaphoreType.DMA((5, TRIPLES, 3)),
    ]

    def __init__(self, at, lt, rg, out, s0, r0, s1, r1, s2, r2, s3, r3, s4, r4, done, done_sem, send_sem, recv_sem):
        self.at, self.lt, self.rg, self.out = at, lt, rg, out
        self.sent, self.got = (s0, s1, s2, s3, s4), (r0, r1, r2, r3, r4)
        self.done, self.done_sem = done, done_sem
        self.send_sem, self.recv_sem = send_sem, recv_sem

    def axis(self, stage, g):
        return "c" if stage == 0 else ORDERS[g][stage - 1]

    def copy(self, stage, t, g):
        axis = self.axis(stage, g)
        slot = t % self.SLOTS[stage]
        src = self.sent[stage].at[slot, g]
        if stage:
            src = src.at[1 - self.at[axis]]
        return pltpu.make_async_remote_copy(
            src_ref=src,
            dst_ref=self.got[stage].at[t, g],
            send_sem=self.send_sem.at[stage, slot, g],
            recv_sem=self.recv_sem.at[stage, t, g],
            device_id=partner(axis, self.at),
            device_id_type=MESH,
        )

    def free(self, stage, t):
        slots = self.SLOTS[stage]

        @when(t >= slots)
        def _():
            for g in range(3):
                self.copy(stage, t - slots, g).wait_send()

    def product(self, t, half, g):
        cols = slice(256 * g, 256 * g + 256)
        return jnp.dot(self.lt[look_up(LEFT, t), half], self.rg[look_up(RIGHT, t), :, cols], preferred_element_type=F32)

    def first(self, t):
        self.free(0, t)
        half = 1 - self.at["c"]
        memory = (t == 9) | (t == 10)
        for g in range(3):
            cols = slice(256 * g, 256 * g + 256)

            @when(negate(memory))
            def _():
                self.sent[0][t % 2, g] = self.product(t, half, g).astype(BF16)

            @when(memory)
            def _():
                more = jnp.dot(self.lt[7, half], self.rg[t + 4, :, cols], preferred_element_type=F32)
                self.sent[0][t % 2, g] = (self.product(t, half, g) + more).astype(BF16)

            self.copy(0, t, g).start()

    def second(self, t):
        self.free(1, t)
        half = self.at["c"]
        memory = (t == 9) | (t == 10)
        for g in range(3):
            cols = slice(256 * g, 256 * g + 256)
            self.copy(0, t, g).wait_recv()

            def spread(total):
                order = ORDERS[g]
                for b in range(8):
                    bits = {"h": b // 4, "l": (b // 2) % 2, "x": b % 2}
                    for y in range(2):
                        bits["y"] = y
                        where = tuple(bits[a] for a in order)
                        self.sent[1][(t % self.SLOTS[1], g) + where] = total[48 * b : 48 * b + 48, 128 * y : 128 * y + 128].astype(BF16)

            @when(negate(memory))
            def _():
                spread(self.product(t, half, g) + self.got[0][t, g].astype(F32))

            @when(memory)
            def _():
                more = jnp.dot(self.lt[7, half], self.rg[t + 4, :, cols], preferred_element_type=F32)
                spread(self.product(t, half, g) + more + self.got[0][t, g].astype(F32))

            self.copy(1, t, g).start()

    def write(self, t):
        return pltpu.make_async_copy(self.done.at[t % 3], self.out.at[t], self.done_sem.at[t % 3])

    def onward(self, stage, t):
        if stage < 5:
            self.free(stage, t)
        else:

            @when(t >= 3)
            def _():
                self.write(t - 3).wait()

        for g in range(3):
            self.copy(stage - 1, t, g).wait_recv()
            own = self.sent[stage - 1][t % self.SLOTS[stage - 1], g, self.at[self.axis(stage - 1, g)]]
            total = own.astype(F32) + self.got[stage - 1][t, g].astype(F32)
            if stage < 5:
                self.sent[stage][t % self.SLOTS[stage], g] = total.astype(BF16)
                self.copy(stage, t, g).start()
            else:
                self.done[t % 3, g] = total
        if stage == 5:
            self.write(t).start()

    def tick(self, n, stages):
        for stage in stages:
            t = n - self.LAGS[stage]

            @when((t >= (2 if stage < 2 else 0)) & (t < TRIPLES))
            def _():
                if stage == 0:
                    self.first(t)
                elif stage == 1:
                    self.second(t)
                else:
                    self.onward(stage, t)

    def drain(self):
        for t in range(TRIPLES - 3, TRIPLES):
            self.write(t).wait()
        for stage in range(5):
            for t in range(TRIPLES - self.SLOTS[stage], TRIPLES):
                for g in range(3):
                    self.copy(stage, t, g).wait_send()


NORM_ORDER = ("c", "x", "y", "l", "h")


def norm_copy(j, at, own, got, send_sem, recv_sem):
    return pltpu.make_async_remote_copy(
        src_ref=own.at[j], dst_ref=got.at[j], send_sem=send_sem.at[j], recv_sem=recv_sem.at[j],
        device_id=partner(NORM_ORDER[j], at), device_id_type=MESH,
    )


def norm_step(j, at, own, got, send_sem, recv_sem):
    if j:
        norm_copy(j - 1, at, own, got, send_sem, recv_sem).wait()
        own[j] = own[j - 1] + got[j - 1]
    if j < 5:
        norm_copy(j, at, own, got, send_sem, recv_sem).start()


LANES = 128


def normed(v):
    center = jnp.mean(v, axis=-1, keepdims=True)
    centered = v - center
    spread = jnp.mean(centered * centered, axis=-1, keepdims=True)
    scale = lax.rsqrt(spread + 1e-05)
    return centered * scale, scale


def row_blocks(step, body):
    for b in range(256 // step):
        body(slice(b * step, b * step + step))


def norm_forward(load, out, norm_gain, norm_bias, k):
    def body(rows):
        hat, _ = normed(load(rows))
        out[rows, :] = (hat * norm_gain[k : k + 1, :] + norm_bias[k : k + 1, :]).astype(BF16)

    row_blocks(64, body)


def norm_backward(load, load_grad, store, norm_gain, sums, k):
    def body(rows):
        hat, scale = normed(load(rows))
        dy = load_grad(rows)
        sums[k : k + 1, :] += jnp.sum(dy * hat, axis=0, keepdims=True)
        sums[k + 3 : k + 4, :] += jnp.sum(dy, axis=0, keepdims=True)
        dhat = dy * norm_gain[k : k + 1, :]
        mean = jnp.mean(dhat, axis=-1, keepdims=True)
        along = jnp.mean(dhat * hat, axis=-1, keepdims=True)
        store(rows, scale * (dhat - mean - hat * along))

    def run(b, carry):
        body(pl.ds(pl.multiple_of(b * 64, 64), 64))
        return carry

    lax.fori_loop(0, 4, run, 0)


def two_heads(tile):
    first = lax.broadcasted_iota(jnp.int32, tile.shape, 1) < HEAD_DIM
    zero = jnp.zeros_like(tile)
    return jnp.concatenate([jnp.where(first, tile, zero), jnp.where(first, zero, tile)], axis=0)


def upright(sideways):
    rows = sideways.shape[1] // 2
    own = jnp.concatenate([sideways[:HEAD_DIM, :rows], sideways[HEAD_DIM:, rows:]], axis=0)
    return own.T


def dot(a, b, over):
    return lax.dot_general(a, b, (over, ((), ())), preferred_element_type=F32)


LAST = ((1,), (1,))
PLAIN = ((1,), (0,))
ROWS = ((0,), (0,))


def attend(items):
    scores = [jnp.where(allowed, dot(k, two_heads(q), LAST), -1e30) for q, k, _, allowed in items]
    raised = [jnp.exp(s - jnp.max(s, axis=0, keepdims=True)) for s in scores]
    weights = [(r * (1.0 / jnp.sum(r, axis=0, keepdims=True))).astype(BF16) for r in raised]
    contexts = [upright(dot(item[2], w, ROWS).astype(BF16)) for w, item in zip(weights, items)]
    return list(zip(weights, contexts))


def attend_back(items):
    stacked = [two_heads(item[4]) for item in items]
    dweights = [dot(item[2], s, LAST) for item, s in zip(items, stacked)]
    dvs = [dot(item[3], s, PLAIN).astype(BF16) for item, s in zip(items, stacked)]
    dscores = []
    for item, d in zip(items, dweights):
        probs = item[3].astype(F32)
        terms = probs * d
        dscores.append((terms - probs * jnp.sum(terms, axis=0, keepdims=True)).astype(BF16))
    dqs = [upright((dot(item[1], d, ROWS) * (1.0 / math.sqrt(HEAD_DIM))).astype(BF16)) for item, d in zip(items, dscores)]
    dks = [dot(d, two_heads(item[0]), PLAIN).astype(BF16) for item, d in zip(items, dscores)]
    return list(zip(dqs, dks, dvs))


def in_groups(pairs, size, body):
    for n in range(0, len(pairs), size):
        body(pairs[n : n + size])


def column(slot, h, g):
    return (slot, slice(None), pl.ds(pl.multiple_of(256 * g + LANES * h, LANES), LANES))


def back(rg, slots, weight, rows=None):
    half = weight.shape[1] // 2
    total = None
    for j, slot in enumerate(slots):
        for g in range(3):
            at = j * 384 + g * LANES
            w = jnp.concatenate([weight[:, at : at + LANES], weight[:, half + at : half + at + LANES]], axis=1)
            term = dot(rg[slot, :, 256 * g : 256 * g + 256], w, LAST)
            total = term if total is None else total + term
    return total


CHUNKS = (0, 3, 1, 4, 2, 5)


def layer_kernel(
    dec_input, memory, src_len, out_grad, self_qkv, self_out, cross_query, cross_kv, cross_out, ffn_in, ffn_out,
    norm_gain, norm_bias,
    o_layer, o_input, o_memory, units, norm_out,
    x_in, mem, og, w_qkv, w_self, w_query, w_kv, w_cross, w_in, w_out,
    normal, qkv, p_self, context, hidden1, qx, kv, p_cross, hidden2,
    active, acc, dthird,
    lt, rg, n_own, n_got, n_send, n_recv, load_sem, swap_send, swap_recv, out_sem, out_send, out_recv, *rest
):
    at = place()
    y = at["y"]
    red = Reducer(at, lt, rg, units, *rest)
    across = partner("y", at)

    loads = [
        pltpu.make_async_copy(src, dst, load_sem.at[n])
        for n, (src, dst) in enumerate(
            ((self_qkv, w_qkv), (self_out, w_self), (cross_kv, w_kv), (cross_query, w_query), (cross_out, w_cross))
        )
    ]
    for load in loads:
        load.start()

    def ffn_load(n):
        cols = slice(CHUNKS[n] * 512, CHUNKS[n] * 512 + 512)
        slot = n % 3
        return (
            pltpu.make_async_copy(ffn_in.at[:, cols], w_in.at[slot], load_sem.at[5 + slot]),
            pltpu.make_async_copy(ffn_out.at[cols, :], w_out.at[slot], load_sem.at[8 + slot]),
        )

    for n in range(3):
        for load in ffn_load(n):
            load.start()

    def own_rows(n, src, dst, rows):
        return [
            pltpu.make_async_copy(
                src.at[2 * y + e], dst.at[pl.ds(pl.multiple_of(2 * e * rows + y * rows, rows), rows), :], load_sem.at[11 + 2 * n + e]
            )
            for e in range(2)
        ]

    def swap(n, src, dst, rows):
        return [
            pltpu.make_async_remote_copy(
                src_ref=src.at[2 * (1 - y) + e],
                dst_ref=dst.at[pl.ds(pl.multiple_of(2 * e * rows + y * rows, rows), rows), :],
                send_sem=swap_send.at[n, e], recv_sem=swap_recv.at[n, e], device_id=across, device_id_type=MESH,
            )
            for e in range(2)
        ]

    moved = ((dec_input, x_in, 64), (memory, mem, 128), (out_grad, og, 64))
    owns = [own_rows(n, *m) for n, m in enumerate(moved)]
    swaps = [swap(n, *m) for n, m in enumerate(moved)]
    for own in owns:
        for copy in own:
            copy.start()
    greet(at)
    for copy in swaps[0]:
        copy.start()
    for copy in swaps[1]:
        copy.start()
    for copy in swaps[2]:
        copy.start()

    def own_here(n):
        for copy in owns[n]:
            copy.wait()

    def other_here(n, e):
        swaps[n][e].wait()

    scale = 1.0 / math.sqrt(HEAD_DIM)

    own_here(0)
    for e in range(2):
        other_here(0, e)
    norm_forward(lambda rows: x_in[rows, :].astype(F32), normal, norm_gain, norm_bias, 0)
    loads[0].wait()

    for n in range(9):
        out = jnp.dot(normal[...], w_qkv[:, 256 * n : 256 * n + 256], preferred_element_type=F32)
        out = (out * scale if n < 3 else out).astype(BF16)
        qkv[2 * n] = out[:, 0:LANES]
        qkv[2 * n + 1] = out[:, LANES:256]

    store_left(lt, 10, normal[...].T)

    def pair(e, p):
        return slice(e * 128, e * 128 + 128), slice(p * LANES, p * LANES + LANES)

    pairs = [(e, p) for p in range(6) for e in range(2)]

    def self_operands(e, p):
        rows, _ = pair(e, p)
        return qkv[p, rows, :], qkv[6 + p, rows, :], qkv[12 + p, rows, :]

    def self_forward(group):
        k_at = lax.broadcasted_iota(jnp.int32, (128, 256), 0)
        q_at = lax.broadcasted_iota(jnp.int32, (128, 256), 1) % 128
        results = attend([(*self_operands(e, p), q_at >= k_at) for e, p in group])
        for (e, p), (weights, values) in zip(group, results):
            p_self[6 * e + p] = weights
            context[pair(e, p)] = values

    in_groups(pairs, 4, self_forward)

    loads[1].wait()
    for n in range(3):
        cols = slice(256 * n, 256 * n + 256)
        hidden1[:, cols] = x_in[:, cols].astype(F32) + jnp.dot(context[...], w_self[:, cols], preferred_element_type=F32)
    store_left(lt, 9, context[...].T)
    norm_forward(lambda rows: hidden1[rows, :], normal, norm_gain, norm_bias, 1)

    loads[3].wait()
    for n in range(3):
        out = jnp.dot(normal[...], w_query[:, 256 * n : 256 * n + 256], preferred_element_type=F32)
        out = (out * scale).astype(BF16)
        qx[2 * n] = out[:, 0:LANES]
        qx[2 * n + 1] = out[:, LANES:256]
    store_left(lt, 8, normal[...].T)
    loads[2].wait()
    own_here(1)

    def project_kv(blocks):
        rows = [pl.ds(pl.multiple_of(at_, 128), 128) for at_ in blocks]
        source = jnp.concatenate([mem[r, :] for r in rows], axis=0)
        for n in range(6):
            out = jnp.dot(source, w_kv[:, 256 * n : 256 * n + 256], preferred_element_type=F32).astype(BF16)
            for k, r in enumerate(rows):
                kv[2 * n, r, :] = out[128 * k : 128 * k + 128, 0:LANES]
                kv[2 * n + 1, r, :] = out[128 * k : 128 * k + 128, LANES:256]

    project_kv([128 * y, 256 + 128 * y])

    def cross_operands(e, p):
        rows, keys = pair(e, p)[0], slice(e * 256, e * 256 + 256)
        return qx[p, rows, :], kv[p, keys, :], kv[6 + p, keys, :]

    def cross_forward(group):
        k_at = lax.broadcasted_iota(jnp.int32, (256, 256), 0)
        results = attend([(*cross_operands(e, p), k_at < src_len[2 * y + e]) for e, p in group])
        for (e, p), (weights, values) in zip(group, results):
            p_cross[6 * e + p] = weights
            context[pair(e, p)] = values

    for e in range(2):
        other_here(1, e)
        project_kv([256 * e + 128 * (1 - y)])
        cross_forward([(e, p) for p in range(6)])

    loads[4].wait()
    for n in range(3):
        cols = slice(256 * n, 256 * n + 256)
        hidden2[:, cols] = hidden1[:, cols] + jnp.dot(context[...], w_cross[:, cols], preferred_element_type=F32)
    norm_forward(lambda rows: hidden2[rows, :], normal, norm_gain, norm_bias, 2)

    own_here(2)
    for e in range(2):
        other_here(2, e)

    def spread(slot, rows_of):
        for g in range(3):
            for h in range(2):
                lane = h * 384 + g * LANES
                rg[slot, :, 256 * g + LANES * h : 256 * g + LANES * h + LANES] = rows_of[:, lane : lane + LANES].astype(BF16)

    acc[...] = jnp.zeros_like(acc)
    dthird[...] = jnp.zeros_like(dthird)
    root = math.sqrt(2.0 / math.pi)

    def up_tile(tile):
        lane = 256 * (tile % 3) + LANES * (tile // 12)
        return (1 + (tile % 12) // 3, slice(None), slice(lane, lane + LANES))

    def feed_in(n, s):
        slot, cols = n % 3, slice(256 * s, 256 * s + 256)
        up = jnp.dot(normal[...], w_in[slot, :, cols], preferred_element_type=F32)
        return up, dot(og[...], w_out[slot, cols, :], LAST)

    def feed_bend(n, s, up, dact):
        square = up * up
        bend = jnp.tanh(up * (root + (root * 0.044715) * square))
        lift = 0.5 + 0.5 * bend
        active[n % 2, :, 256 * s : 256 * s + 256] = (up * lift).astype(BF16)
        slope = lift + (0.5 * up) * (1.0 - bend * bend) * (root + (3.0 * 0.044715 * root) * square)
        grad = (dact * slope).astype(BF16)
        for t in range(2):
            rg[up_tile(4 * CHUNKS[n] + 2 * s + t)] = grad[:, LANES * t : LANES * t + LANES]

    def feed_out(n, k):
        slot, cols = n % 3, slice(256 * k, 256 * k + 256)
        acc[:, cols] += jnp.dot(active[n % 2], w_out[slot, :, cols], preferred_element_type=F32)
        dup = jnp.concatenate([rg[up_tile(4 * CHUNKS[n] + t)] for t in range(4)], axis=1)
        dthird[:, cols] += dot(dup, w_in[slot, cols, :], LAST)

    def feed_left(n):
        flipped = active[n % 2].T
        at_ = 0
        while at_ < 512:
            feature = CHUNKS[n] * 512 + at_
            i, k, r = feature // 192, (feature % 192) // 48, feature % 48
            size = min(48 - r, 512 - at_)
            to = 48 * (i // 2) + r
            lt[k, i % 2, to : to + size, :] = flipped[at_ : at_ + size, :]
            at_ += size

    def feed(n):
        for load in ffn_load(n):
            load.wait()
        for s in range(2):
            up, dact = feed_in(n, s)
            if n:
                for k in ((0, 1), (2,))[s]:
                    feed_out(n - 1, k)
            feed_bend(n, s, up, dact)
        if n:
            feed_left(n - 1)
            if n < 4:
                for load in ffn_load(n + 2):
                    load.start()

    PIECES = (
        [(normal, o_layer, 64, e, r) for e in range(2) for r in (0, 32)]
        + [(mem, o_memory, 128, e, r) for e in range(2) for r in (0, 32, 64, 96)]
        + [(x_in, o_input, 64, e, r) for e in range(2) for r in (0, 32)]
    )

    def piece(n, leaving):
        buf, out, rows, e, r = PIECES[n]
        which = 1 - y if leaving else y
        src = buf.at[pl.ds(pl.multiple_of(2 * e * rows + which * rows + r, 32), 32), :]
        dst = out.at[2 * y + e, r : r + 32, :]
        if not leaving:
            return pltpu.make_async_copy(src, dst, out_sem.at[n])
        return pltpu.make_async_remote_copy(
            src_ref=src, dst_ref=dst, send_sem=out_send.at[n], recv_sem=out_recv.at[n], device_id=across, device_id_type=MESH
        )

    def send(n):
        piece(n, True).start()
        piece(n, False).start()

    feed(0)
    feed(1)
    store_left(lt, 4, normal[...].T)
    red.first(0)
    feed(2)
    red.second(0)
    feed(3)
    red.first(1)
    feed(4)
    red.second(1)
    feed(5)
    for k in range(3):
        feed_out(5, k)
    feed_left(5)
    spread(0, og)

    sums = n_own.at[0]
    sums[...] = jnp.zeros(sums.shape, F32)
    dc = context

    def store_grad(rows, value):
        acc[rows, :] = value

    def store_input(rows, v):
        x_in[rows, :] = (acc[rows, :] + v).astype(BF16)

    def context_grad(slot, weight):
        for n in range(3):
            rows = slice(256 * n, 256 * n + 256)
            dc[:, rows] = back(rg, (slot,), weight.at[rows, :]).astype(BF16)

    def cross_backward(group):
        results = attend_back([(*cross_operands(e, p), p_cross[6 * e + p], dc[pair(e, p)]) for e, p in group])
        for (e, p), (dq, dk, dv) in zip(group, results):
            j, g = p // 3, p % 3
            rg[8, pair(e, p)[0], 256 * g + LANES * j : 256 * g + LANES * j + LANES] = dq
            rg[6 + 7 * e + j, :, 256 * g : 256 * g + LANES] = dk
            rg[6 + 7 * e + j, :, 256 * g + LANES : 256 * g + 256] = dv

    def self_backward(group):
        results = attend_back([(*self_operands(e, p), p_self[6 * e + p], dc[pair(e, p)]) for e, p in group])
        for (e, p), values in zip(group, results):
            for n, value in enumerate(values):
                tile = 6 * n + p
                lane = 256 * (tile % 3) + LANES * (tile // 9)
                rg[10 + (tile % 9) // 3, pair(e, p)[0], lane : lane + LANES] = value

    def memory_rows(e):
        for n in range(3):
            rows = slice(256 * n, 256 * n + 256)
            mem[256 * e : 256 * e + 256, rows] = back(rg, (6 + 7 * e, 7 + 7 * e), w_kv.at[rows, :]).astype(BF16)

    def back_rows(slots, weight):
        for n in range(3):
            rows = slice(256 * n, 256 * n + 256)
            dthird[:, rows] = back(rg, slots, weight.at[rows, :])

    def piece_3():
        normal[...] = (hidden2[...] + acc[...]).astype(BF16)
        norm_backward(
            lambda rows: hidden2[rows, :], lambda rows: dthird[rows, :],
            lambda rows, v: store_grad(rows, og[rows, :].astype(F32) + v), norm_gain, sums, 2,
        )
        spread(5, acc)

    def piece_4():
        store_left(lt, 5, context[...].T)
        context_grad(5, w_cross)

    def piece_5():
        in_groups(pairs[:6], 3, cross_backward)

    def piece_6():
        in_groups(pairs[6:], 3, cross_backward)
        store_left(lt, 6, mem[0:256, :].T)
        store_left(lt, 7, mem[256:512, :].T)
        memory_rows(0)

    def piece_7():
        memory_rows(1)
        back_rows((8,), w_query)

    def piece_8():
        norm_backward(
            lambda rows: hidden1[rows, :], lambda rows: dthird[rows, :],
            lambda rows, v: store_grad(rows, acc[rows, :] + v), norm_gain, sums, 1,
        )
        spread(9, acc)
        context_grad(9, w_self)

    def piece_9():
        in_groups(pairs[:6], 3, self_backward)

    def piece_10():
        in_groups(pairs[6:], 3, self_backward)

    def piece_11():
        back_rows((10, 11, 12), w_qkv)

    def piece_12():
        norm_backward(
            lambda rows: x_in[rows, :].astype(F32), lambda rows: dthird[rows, :], store_input, norm_gain, sums, 0
        )

    pieces = (piece_3, piece_4, piece_5, piece_6, piece_7, piece_8, piece_9, piece_10, piece_11, piece_12)

    def body(n, carry):
        red.tick(n, (1, 0, 2))
        for k, run in enumerate(pieces):
            pl.when(n == 3 + k)(run)
        red.tick(n, (3, 4, 5))
        for j in range(6):
            @pl.when(n == 12 + j)
            def _():
                norm_step(j, at, n_own, n_got, n_send, n_recv)

        for k in range(16):
            @pl.when(n == k + 3)
            def _():
                send(k)

        return carry

    lax.fori_loop(2, red.TICKS, body, 0)
    norm_out[...] = n_own[5]
    red.drain()
    for n in range(16):
        piece(n, True).wait()
        piece(n, False).wait()


def layer_call(args):
    anywhere = pl.BlockSpec(memory_space=pl.ANY)
    vmem = pl.BlockSpec(memory_space=pltpu.VMEM)
    rows = lambda width, kind=BF16: pltpu.VMEM((256, width), kind)
    return pl.pallas_call(
        layer_kernel,
        out_shape=(
            jax.ShapeDtypeStruct((4, 64, 768), BF16),
            jax.ShapeDtypeStruct((4, 64, 768), BF16),
            jax.ShapeDtypeStruct((4, 128, 768), BF16),
            jax.ShapeDtypeStruct((TRIPLES, 3, 48, 128), F32),
            jax.ShapeDtypeStruct((8, 768), F32),
        ),
        in_specs=[anywhere, anywhere, pl.BlockSpec(memory_space=pltpu.SMEM)] + [anywhere] * 8 + [vmem] * 2,
        out_specs=(anywhere, anywhere, anywhere, anywhere, vmem),
        scratch_shapes=[
            rows(768), pltpu.VMEM((512, 768), BF16), rows(768),
            pltpu.VMEM((768, 2304), BF16), pltpu.VMEM((768, 768), BF16), pltpu.VMEM((768, 768), BF16),
            pltpu.VMEM((768, 1536), BF16), pltpu.VMEM((768, 768), BF16),
            pltpu.VMEM((3, 768, 512), BF16), pltpu.VMEM((3, 512, 768), BF16),
            rows(768), pltpu.VMEM((18, 256, 128), BF16), pltpu.VMEM((12, 128, 256), BF16), rows(768),
            rows(768, F32), pltpu.VMEM((6, 256, 128), BF16), pltpu.VMEM((12, 512, 128), BF16),
            pltpu.VMEM((12, 256, 256), BF16), rows(768, F32),
            pltpu.VMEM((2, 256, 512), BF16), rows(768, F32), rows(768, F32),
            pltpu.VMEM((11, 2, 384, 256), BF16),
            pltpu.VMEM((15, 256, 768), BF16),
            pltpu.VMEM((6, 8, 768), F32),
            pltpu.VMEM((5, 8, 768), F32),
            pltpu.SemaphoreType.DMA((5,)),
            pltpu.SemaphoreType.DMA((5,)),
            pltpu.SemaphoreType.DMA((17,)),
            pltpu.SemaphoreType.DMA((3, 2)),
            pltpu.SemaphoreType.DMA((3, 2)),
            pltpu.SemaphoreType.DMA((16,)),
            pltpu.SemaphoreType.DMA((16,)),
            pltpu.SemaphoreType.DMA((16,)),
        ] + Reducer.SCRATCH,
        compiler_params=pltpu.CompilerParams(collective_id=0, has_side_effects=True, vmem_limit_bytes=61 << 20),
    )(*args)


WEIGHTS = ((13, 3), (12, 1), (11, 1), (9, 2), (8, 1), (0, 4))


def finish_kernel(layer, inputs, memories, units, norms, *refs):
    o_layer, o_input, o_memory = refs[0:3]
    o_weights, o_ffn_out, o_gain, o_bias = refs[3:9], refs[9], refs[10], refs[11]
    low_input, low_memory, high_input, high_memory, blocks = refs[12:17]
    w_bufs, ffn_buf, sem, out_sem, low_layer = refs[17:23], refs[23], refs[24], refs[25], refs[26]
    loads = [
        pltpu.make_async_copy(units, blocks, sem.at[0]),
        pltpu.make_async_copy(memories, low_memory, sem.at[1]),
        pltpu.make_async_copy(inputs, low_input, sem.at[2]),
        pltpu.make_async_copy(layer, low_layer, sem.at[3]),
    ]
    for load in loads:
        load.start()
    stores = []

    def store(src, dst):
        copy = pltpu.make_async_copy(src, dst, out_sem.at[len(stores)])
        copy.start()
        stores.append(copy)

    o_gain[...] = norms[0:3, :]
    o_bias[...] = norms[3:6, :]
    loads[0].wait()
    for (t, count), buf, out in zip(WEIGHTS, w_bufs, o_weights):
        for j in range(count):
            for g in range(3):
                buf[:, j * 384 + g * LANES : j * 384 + g * LANES + LANES] = blocks[t + j, g]
        store(buf, out)
    for k in range(4):
        for g in range(3):
            ffn_buf[48 * k : 48 * k + 48, g * LANES : g * LANES + LANES] = blocks[4 + k, g]
    store(ffn_buf, o_ffn_out)
    loads[1].wait()
    for e in range(4):
        high_memory[e] = low_memory[e].astype(F32)
        store(high_memory.at[e], o_memory.at[e])
    loads[2].wait()
    high_input[...] = low_input[...].astype(F32)
    store(high_input, o_input)
    loads[3].wait()
    store(low_layer, o_layer)
    for copy in stores:
        copy.wait()


def finish_call(layer, inputs, memories, units, norms):
    anywhere = pl.BlockSpec(memory_space=pl.ANY)
    vmem = pl.BlockSpec(memory_space=pltpu.VMEM)
    widths = [count * 384 for _, count in WEIGHTS]
    return pl.pallas_call(
        finish_kernel,
        out_shape=(
            jax.ShapeDtypeStruct(layer.shape, BF16),
            jax.ShapeDtypeStruct(inputs.shape, F32),
            jax.ShapeDtypeStruct(memories.shape, F32),
            *[jax.ShapeDtypeStruct((48, w), F32) for w in widths],
            jax.ShapeDtypeStruct((192, 384), F32),
            jax.ShapeDtypeStruct((3, 768), F32),
            jax.ShapeDtypeStruct((3, 768), F32),
        ),
        in_specs=[anywhere] * 4 + [vmem],
        out_specs=(anywhere,) * 10 + (vmem, vmem),
        scratch_shapes=[
            pltpu.VMEM(inputs.shape, BF16), pltpu.VMEM(memories.shape, BF16),
            pltpu.VMEM(inputs.shape, F32), pltpu.VMEM(memories.shape, F32), pltpu.VMEM(units.shape, F32),
            *[pltpu.VMEM((48, w), F32) for w in widths], pltpu.VMEM((192, 384), F32),
            pltpu.SemaphoreType.DMA((4,)), pltpu.SemaphoreType.DMA((13,)), pltpu.VMEM(layer.shape, BF16),
        ],
        compiler_params=pltpu.CompilerParams(vmem_limit_bytes=60 << 20),
    )(layer, inputs, memories, units, norms)


def per_device_paired(*args):
    return finish_call(*layer_call(args))

def layer_norm(x, gain, shift):
    center = jnp.mean(x, axis=-1, keepdims=True)
    centered = x - center
    spread = jnp.mean(centered * centered, axis=-1, keepdims=True)
    return centered * lax.rsqrt(spread + 1e-05) * gain + shift


def smooth(v):
    return jax.nn.gelu(v, approximate=True)


def project(rows, weight):
    return jnp.einsum("etd,df->etf", rows, weight, preferred_element_type=jnp.float32)


def project_back(grads, weight):
    return jnp.einsum("etf,df->etd", grads, weight, preferred_element_type=jnp.float32)


def outer(rows, grads):
    return jnp.einsum("etd,etf->df", rows, grads, preferred_element_type=jnp.float32)


def outer_full(rows, grads):
    return jnp.einsum(
        "etd,etf->df", rows.astype(jnp.float32), grads, precision=lax.Precision.HIGHEST
    )


def back_full(grads, weight):
    return jnp.einsum(
        "etf,df->etd", grads, weight.astype(jnp.float32), precision=lax.Precision.HIGHEST
    )


def split_heads(queries, key_values):
    examples, rows, width = queries.shape
    count = key_values.shape[1]
    heads_q = queries.reshape(examples, rows, HEADS, HEAD_DIM)
    heads_k = key_values[:, :, :width].reshape(examples, count, HEADS, HEAD_DIM)
    heads_v = key_values[:, :, width:].reshape(examples, count, HEADS, HEAD_DIM)
    return (heads_q, heads_k, heads_v)


def masked_logits(heads_q, heads_k, allowed):
    scores = jnp.einsum("eqhd,ekhd->ehqk", heads_q, heads_k, preferred_element_type=jnp.float32)
    return jnp.where(allowed, scores * (1.0 / math.sqrt(HEAD_DIM)), -1e30)


def attend_forward(queries, key_values, allowed):
    examples, rows, width = queries.shape
    heads_q, heads_k, heads_v = split_heads(queries, key_values)
    logits = masked_logits(heads_q, heads_k, allowed)
    row_top = jnp.max(logits, axis=-1, keepdims=True)
    raised = jnp.where(allowed, jnp.exp(logits - row_top), 0.0)
    row_total = jnp.sum(raised, axis=-1, keepdims=True)
    weights = (raised / row_total).astype(jnp.bfloat16)
    context = jnp.einsum("ehqk,ekhd->eqhd", weights, heads_v, preferred_element_type=jnp.float32)
    return (
        context.reshape(examples, rows, width).astype(jnp.bfloat16),
        row_top + jnp.log(row_total),
    )


def attend_backward(queries, key_values, allowed, log_total, grad_context):
    examples, rows, width = queries.shape
    count = key_values.shape[1]
    heads_q, heads_k, heads_v = split_heads(queries, key_values)
    logits = masked_logits(heads_q, heads_k, allowed)
    soft = jnp.where(allowed, jnp.exp(logits - log_total), 0.0)
    grad_heads = grad_context.reshape(examples, rows, HEADS, HEAD_DIM)
    grad_soft = jnp.einsum(
        "eqhd,ekhd->ehqk", grad_heads, heads_v, preferred_element_type=jnp.float32
    )
    grad_values = jnp.einsum(
        "ehqk,eqhd->ekhd", soft.astype(jnp.bfloat16), grad_heads, preferred_element_type=jnp.float32
    )
    inner = jnp.sum(soft * grad_soft, axis=-1, keepdims=True)
    grad_scores = (soft * (grad_soft - inner) * (1.0 / math.sqrt(HEAD_DIM))).astype(jnp.bfloat16)
    grad_queries = jnp.einsum(
        "ehqk,ekhd->eqhd", grad_scores, heads_k, preferred_element_type=jnp.float32
    )
    grad_keys = jnp.einsum(
        "ehqk,eqhd->ekhd", grad_scores, heads_q, preferred_element_type=jnp.float32
    )
    joined = jnp.concatenate(
        [grad_keys.reshape(examples, count, width), grad_values.reshape(examples, count, width)],
        axis=2,
    )
    return (grad_queries.reshape(examples, rows, width), joined)


def per_device_wide(
    dec_input,
    memory,
    src_len,
    out_grad,
    self_qkv,
    self_out,
    cross_query,
    cross_kv,
    cross_out,
    ffn_in,
    ffn_out,
    norm_gain,
    norm_bias,
):
    examples, local_rows, width = dec_input.shape
    local_sources = memory.shape[1]
    seq_count = lax.axis_size("seq")
    all_targets = local_rows * seq_count
    all_sources = local_sources * seq_count
    rank = lax.axis_index("seq")
    x = dec_input.astype(jnp.float32)
    first_f, pull_first = jax.vjp(layer_norm, x, norm_gain[0], norm_bias[0])
    first = first_f.astype(jnp.bfloat16)
    projected = project(first, self_qkv).astype(jnp.bfloat16)
    self_queries = projected[:, :, :width]
    self_kv = lax.all_gather(projected[:, :, width:], "seq", axis=1, tiled=True)
    query_place = rank * local_rows + jnp.arange(local_rows, dtype=jnp.int32)
    key_place = jnp.arange(all_targets, dtype=jnp.int32)
    causal = (query_place[:, None] >= key_place[None, :])[None, None]
    self_context, self_total = attend_forward(self_queries, self_kv, causal)
    hidden1 = x + project(self_context, self_out)
    second_f, pull_second = jax.vjp(layer_norm, hidden1, norm_gain[1], norm_bias[1])
    second = second_f.astype(jnp.bfloat16)
    cross_queries = project(second, cross_query).astype(jnp.bfloat16)
    gathered = lax.all_gather(memory, "seq", axis=1, tiled=True)
    memory_kv = project(gathered, cross_kv).astype(jnp.bfloat16)
    source_place = jnp.arange(all_sources, dtype=jnp.int32)
    visible = (source_place[None, :] < src_len[:, None])[:, None, None, :]
    cross_context, cross_total = attend_forward(cross_queries, memory_kv, visible)
    hidden2 = hidden1 + project(cross_context, cross_out)
    third_f, pull_third = jax.vjp(layer_norm, hidden2, norm_gain[2], norm_bias[2])
    third = third_f.astype(jnp.bfloat16)
    raised_up = project(third, ffn_in)
    active_f, pull_smooth = jax.vjp(smooth, raised_up)
    activated = active_f.astype(jnp.bfloat16)
    layer_out = (hidden2 + project(activated, ffn_out)).astype(jnp.bfloat16)
    grad_out = out_grad.astype(jnp.float32)
    ffn_out_grad = outer(activated, out_grad)
    (grad_up,) = pull_smooth(project_back(out_grad, ffn_out))
    grad_up_low = grad_up.astype(jnp.bfloat16)
    ffn_in_grad = outer(third, grad_up_low)
    back_third, gain_third, bias_third = pull_third(project_back(grad_up_low, ffn_in))
    grad_hidden2 = grad_out + back_third
    cross_branch = grad_hidden2.astype(jnp.bfloat16)
    cross_out_grad = outer(cross_context, cross_branch)
    grad_cross_context = project_back(cross_branch, cross_out).astype(jnp.bfloat16)
    grad_cross_q, grad_memory_kv = attend_backward(
        cross_queries, memory_kv, visible, cross_total, grad_cross_context
    )
    local_kv_grad = lax.psum_scatter(
        grad_memory_kv.astype(jnp.bfloat16), "seq", scatter_dimension=1, tiled=True
    ).astype(jnp.float32)
    cross_kv_grad = outer_full(memory, local_kv_grad)
    memory_grad = back_full(local_kv_grad, cross_kv)
    grad_cross_low = grad_cross_q.astype(jnp.bfloat16)
    cross_query_grad = outer(second, grad_cross_low)
    back_second, gain_second, bias_second = pull_second(project_back(grad_cross_low, cross_query))
    grad_hidden1 = grad_hidden2 + back_second
    self_branch = grad_hidden1.astype(jnp.bfloat16)
    self_out_grad = outer(self_context, self_branch)
    grad_self_context = project_back(self_branch, self_out).astype(jnp.bfloat16)
    grad_self_q, grad_self_kv = attend_backward(
        self_queries, self_kv, causal, self_total, grad_self_context
    )
    local_self_kv = lax.psum_scatter(grad_self_kv, "seq", scatter_dimension=1, tiled=True)
    grad_projected = jnp.concatenate([grad_self_q, local_self_kv], axis=2).astype(jnp.bfloat16)
    self_qkv_grad = outer(first, grad_projected)
    back_first, gain_first, bias_first = pull_first(project_back(grad_projected, self_qkv))
    input_grad = grad_hidden1 + back_first
    gain_terms = jnp.stack([gain_first, gain_second, gain_third])
    bias_terms = jnp.stack([bias_first, bias_second, bias_third])
    gain_total, bias_total = lax.psum((gain_terms, bias_terms), ("dp", "seq"))
    partial_value = (
        lax.psum_scatter(
            self_qkv_grad.astype(jnp.bfloat16), "dp", scatter_dimension=0, tiled=True
        ).astype(jnp.float32),
        lax.psum_scatter(
            self_out_grad.astype(jnp.bfloat16), "dp", scatter_dimension=0, tiled=True
        ).astype(jnp.float32),
        lax.psum_scatter(
            cross_query_grad.astype(jnp.bfloat16), "dp", scatter_dimension=0, tiled=True
        ).astype(jnp.float32),
        lax.psum_scatter(
            cross_kv_grad.astype(jnp.bfloat16), "dp", scatter_dimension=0, tiled=True
        ).astype(jnp.float32),
        lax.psum_scatter(
            cross_out_grad.astype(jnp.bfloat16), "dp", scatter_dimension=0, tiled=True
        ).astype(jnp.float32),
        lax.psum_scatter(
            ffn_in_grad.astype(jnp.bfloat16), "dp", scatter_dimension=0, tiled=True
        ).astype(jnp.float32),
        lax.psum_scatter(
            ffn_out_grad.astype(jnp.bfloat16), "dp", scatter_dimension=0, tiled=True
        ).astype(jnp.float32),
    )
    finished = (
        lax.psum_scatter(
            partial_value[0].astype(jnp.bfloat16), "seq", scatter_dimension=1, tiled=True
        ).astype(jnp.float32),
        lax.psum_scatter(
            partial_value[1].astype(jnp.bfloat16), "seq", scatter_dimension=1, tiled=True
        ).astype(jnp.float32),
        lax.psum_scatter(
            partial_value[2].astype(jnp.bfloat16), "seq", scatter_dimension=1, tiled=True
        ).astype(jnp.float32),
        lax.psum_scatter(
            partial_value[3].astype(jnp.bfloat16), "seq", scatter_dimension=1, tiled=True
        ).astype(jnp.float32),
        lax.psum_scatter(
            partial_value[4].astype(jnp.bfloat16), "seq", scatter_dimension=1, tiled=True
        ).astype(jnp.float32),
        lax.psum_scatter(
            partial_value[5].astype(jnp.bfloat16), "seq", scatter_dimension=1, tiled=True
        ).astype(jnp.float32),
        lax.psum_scatter(
            partial_value[6].astype(jnp.bfloat16), "seq", scatter_dimension=1, tiled=True
        ).astype(jnp.float32),
    )
    return (
        layer_out,
        input_grad,
        memory_grad,
        finished[0],
        finished[1],
        finished[2],
        finished[3],
        finished[4],
        finished[5],
        finished[6],
        gain_total,
        bias_total,
    )


def solution(mesh):
    paired = mesh.shape["dp"] == 16 and mesh.shape["seq"] == 2
    per_device = per_device_paired if paired else per_device_wide
    in_specs = (
        P("dp", "seq", None),
        P("dp", "seq", None),
        P("dp"),
        P("dp", "seq", None),
        P(),
        P(),
        P(),
        P(),
        P(),
        P(),
        P(),
        P(),
        P(),
    )
    out_specs = (
        P("dp", "seq", None),
        P("dp", "seq", None),
        P("dp", "seq", None),
        P("dp", "seq"),
        P("dp", "seq"),
        P("dp", "seq"),
        P("dp", "seq"),
        P("dp", "seq"),
        P("dp", "seq"),
        P("dp", "seq"),
        P(),
        P(),
    )
    return jax.shard_map(
        per_device, mesh=mesh, in_specs=in_specs, out_specs=out_specs, check_vma=False
    )
```

```python
import functools
import math

import jax
import jax.numpy as jnp
from jax import lax
from jax.experimental import pallas as pl
from jax.experimental.pallas import tpu as pltpu
from jax.sharding import PartitionSpec as P

HEADS = 12
HEAD_DIM = 64
MESH = pl.DeviceIdType.MESH
F32 = jnp.float32
BF16 = jnp.bfloat16
TRIPLES = 16
ORDERS = (("x", "l", "y", "h"), ("y", "x", "l", "h"), ("l", "x", "y", "h"))


def place():
    i = lax.axis_index("dp")
    return {"c": i % 2, "x": (i // 2) % 2, "l": (i // 4) % 2, "h": i // 8, "y": lax.axis_index("seq")}


def partner(axis, at):
    i = lax.axis_index("dp")
    y = at["y"]
    if axis == "y":
        return (i, 1 - y)
    step = {"c": 1, "x": 2, "l": 4, "h": 8}[axis]
    return (i + step - 2 * step * at[axis], y)


def greet(at):
    barrier = pltpu.get_barrier_semaphore()
    for axis in ("c", "x", "l", "h", "y"):
        pl.semaphore_signal(barrier, inc=1, device_id=partner(axis, at), device_id_type=MESH)
    pl.semaphore_wait(barrier, 5)


LEFT = (4, 4, 4, 4, 0, 1, 2, 3, 5, 6, 6, 8, 9, 10, 10, 10)
RIGHT = (1, 2, 3, 4, 0, 0, 0, 0, 5, 6, 7, 8, 9, 10, 11, 12)


def look_up(table, t):
    if isinstance(t, int):
        return table[t]
    value = table[-1]
    for n in range(TRIPLES - 2, -1, -1):
        if table[n] != table[n + 1]:
            value = jnp.where(t <= n, table[n], value)
    return value


def when(condition):
    if isinstance(condition, bool):
        return (lambda body: body()) if condition else (lambda body: None)
    return pl.when(condition)


def negate(condition):
    return not condition if isinstance(condition, bool) else jnp.logical_not(condition)


def store_left(lt, slot, rows_by_feature):
    for i in range(16):
        lt[slot, i % 2, 48 * (i // 2) : 48 * (i // 2) + 48, :] = rows_by_feature[48 * i : 48 * i + 48, :]


class Reducer:
    LAGS = (0, 1, 3, 5, 7, 8)
    SLOTS = (2, 3, 3, 3, 3)
    TICKS = TRIPLES + 8
    SCRATCH = [
        pltpu.VMEM((2, 3, 384, 256), BF16),
        pltpu.VMEM((TRIPLES, 3, 384, 256), BF16),
        pltpu.VMEM((3, 3, 2, 2, 2, 2, 48, 128), BF16),
        pltpu.VMEM((TRIPLES, 3, 2, 2, 2, 48, 128), BF16),
        pltpu.VMEM((3, 3, 2, 2, 2, 48, 128), BF16),
        pltpu.VMEM((TRIPLES, 3, 2, 2, 48, 128), BF16),
        pltpu.VMEM((3, 3, 2, 2, 48, 128), BF16),
        pltpu.VMEM((TRIPLES, 3, 2, 48, 128), BF16),
        pltpu.VMEM((3, 3, 2, 48, 128), BF16),
        pltpu.VMEM((TRIPLES, 3, 48, 128), BF16),
        pltpu.VMEM((3, 3, 48, 128), F32),
        pltpu.SemaphoreType.DMA((3,)),
        pltpu.SemaphoreType.DMA((5, 3, 3)),
        pltpu.SemaphoreType.DMA((5, TRIPLES, 3)),
    ]

    def __init__(self, at, lt, rg, out, s0, r0, s1, r1, s2, r2, s3, r3, s4, r4, done, done_sem, send_sem, recv_sem):
        self.at, self.lt, self.rg, self.out = at, lt, rg, out
        self.sent, self.got = (s0, s1, s2, s3, s4), (r0, r1, r2, r3, r4)
        self.done, self.done_sem = done, done_sem
        self.send_sem, self.recv_sem = send_sem, recv_sem

    def axis(self, stage, g):
        return "c" if stage == 0 else ORDERS[g][stage - 1]

    def copy(self, stage, t, g):
        axis = self.axis(stage, g)
        slot = t % self.SLOTS[stage]
        src = self.sent[stage].at[slot, g]
        if stage:
            src = src.at[1 - self.at[axis]]
        return pltpu.make_async_remote_copy(
            src_ref=src,
            dst_ref=self.got[stage].at[t, g],
            send_sem=self.send_sem.at[stage, slot, g],
            recv_sem=self.recv_sem.at[stage, t, g],
            device_id=partner(axis, self.at),
            device_id_type=MESH,
        )

    def free(self, stage, t):
        slots = self.SLOTS[stage]

        @when(t >= slots)
        def _():
            for g in range(3):
                self.copy(stage, t - slots, g).wait_send()

    def product(self, t, half, g):
        cols = slice(256 * g, 256 * g + 256)
        return jnp.dot(self.lt[look_up(LEFT, t), half], self.rg[look_up(RIGHT, t), :, cols], preferred_element_type=F32)

    def first(self, t):
        self.free(0, t)
        half = 1 - self.at["c"]
        memory = (t == 9) | (t == 10)
        for g in range(3):
            cols = slice(256 * g, 256 * g + 256)

            @when(negate(memory))
            def _():
                self.sent[0][t % 2, g] = self.product(t, half, g).astype(BF16)

            @when(memory)
            def _():
                more = jnp.dot(self.lt[7, half], self.rg[t + 4, :, cols], preferred_element_type=F32)
                self.sent[0][t % 2, g] = (self.product(t, half, g) + more).astype(BF16)

            self.copy(0, t, g).start()

    def second(self, t):
        self.free(1, t)
        half = self.at["c"]
        memory = (t == 9) | (t == 10)
        for g in range(3):
            cols = slice(256 * g, 256 * g + 256)
            self.copy(0, t, g).wait_recv()

            def spread(total):
                order = ORDERS[g]
                for b in range(8):
                    bits = {"h": b // 4, "l": (b // 2) % 2, "x": b % 2}
                    for y in range(2):
                        bits["y"] = y
                        where = tuple(bits[a] for a in order)
                        self.sent[1][(t % self.SLOTS[1], g) + where] = total[48 * b : 48 * b + 48, 128 * y : 128 * y + 128].astype(BF16)

            @when(negate(memory))
            def _():
                spread(self.product(t, half, g) + self.got[0][t, g].astype(F32))

            @when(memory)
            def _():
                more = jnp.dot(self.lt[7, half], self.rg[t + 4, :, cols], preferred_element_type=F32)
                spread(self.product(t, half, g) + more + self.got[0][t, g].astype(F32))

            self.copy(1, t, g).start()

    def write(self, t):
        return pltpu.make_async_copy(self.done.at[t % 3], self.out.at[t], self.done_sem.at[t % 3])

    def onward(self, stage, t):
        if stage < 5:
            self.free(stage, t)
        else:

            @when(t >= 3)
            def _():
                self.write(t - 3).wait()

        for g in range(3):
            self.copy(stage - 1, t, g).wait_recv()
            own = self.sent[stage - 1][t % self.SLOTS[stage - 1], g, self.at[self.axis(stage - 1, g)]]
            total = own.astype(F32) + self.got[stage - 1][t, g].astype(F32)
            if stage < 5:
                self.sent[stage][t % self.SLOTS[stage], g] = total.astype(BF16)
                self.copy(stage, t, g).start()
            else:
                self.done[t % 3, g] = total
        if stage == 5:
            self.write(t).start()

    def tick(self, n, stages):
        for stage in stages:
            t = n - self.LAGS[stage]

            @when((t >= (2 if stage < 2 else 0)) & (t < TRIPLES))
            def _():
                if stage == 0:
                    self.first(t)
                elif stage == 1:
                    self.second(t)
                else:
                    self.onward(stage, t)

    def drain(self):
        for t in range(TRIPLES - 3, TRIPLES):
            self.write(t).wait()
        for stage in range(5):
            for t in range(TRIPLES - self.SLOTS[stage], TRIPLES):
                for g in range(3):
                    self.copy(stage, t, g).wait_send()


NORM_ORDER = ("c", "x", "y", "l", "h")


def norm_copy(j, at, own, got, send_sem, recv_sem):
    return pltpu.make_async_remote_copy(
        src_ref=own.at[j], dst_ref=got.at[j], send_sem=send_sem.at[j], recv_sem=recv_sem.at[j],
        device_id=partner(NORM_ORDER[j], at), device_id_type=MESH,
    )


def norm_step(j, at, own, got, send_sem, recv_sem):
    if j:
        norm_copy(j - 1, at, own, got, send_sem, recv_sem).wait()
        own[j] = own[j - 1] + got[j - 1]
    if j < 5:
        norm_copy(j, at, own, got, send_sem, recv_sem).start()


LANES = 128


def normed(v):
    center = jnp.mean(v, axis=-1, keepdims=True)
    centered = v - center
    spread = jnp.mean(centered * centered, axis=-1, keepdims=True)
    scale = lax.rsqrt(spread + 1e-05)
    return centered * scale, scale


def row_blocks(step, body):
    for b in range(256 // step):
        body(slice(b * step, b * step + step))


def norm_forward(load, out, norm_gain, norm_bias, k):
    def body(rows):
        hat, _ = normed(load(rows))
        out[rows, :] = (hat * norm_gain[k : k + 1, :] + norm_bias[k : k + 1, :]).astype(BF16)

    row_blocks(64, body)


def norm_backward(load, load_grad, store, norm_gain, sums, k):
    def body(rows):
        hat, scale = normed(load(rows))
        dy = load_grad(rows)
        sums[k : k + 1, :] += jnp.sum(dy * hat, axis=0, keepdims=True)
        sums[k + 3 : k + 4, :] += jnp.sum(dy, axis=0, keepdims=True)
        dhat = dy * norm_gain[k : k + 1, :]
        mean = jnp.mean(dhat, axis=-1, keepdims=True)
        along = jnp.mean(dhat * hat, axis=-1, keepdims=True)
        store(rows, scale * (dhat - mean - hat * along))

    def run(b, carry):
        body(pl.ds(pl.multiple_of(b * 64, 64), 64))
        return carry

    lax.fori_loop(0, 4, run, 0)


def two_heads(tile):
    first = lax.broadcasted_iota(jnp.int32, tile.shape, 1) < HEAD_DIM
    zero = jnp.zeros_like(tile)
    return jnp.concatenate([jnp.where(first, tile, zero), jnp.where(first, zero, tile)], axis=0)


def upright(sideways):
    rows = sideways.shape[1] // 2
    own = jnp.concatenate([sideways[:HEAD_DIM, :rows], sideways[HEAD_DIM:, rows:]], axis=0)
    return own.T


def dot(a, b, over):
    return lax.dot_general(a, b, (over, ((), ())), preferred_element_type=F32)


LAST = ((1,), (1,))
PLAIN = ((1,), (0,))
ROWS = ((0,), (0,))


def attend(items):
    scores = [jnp.where(allowed, dot(k, two_heads(q), LAST), -1e30) for q, k, _, allowed in items]
    raised = [jnp.exp(s - jnp.max(s, axis=0, keepdims=True)) for s in scores]
    weights = [(r * (1.0 / jnp.sum(r, axis=0, keepdims=True))).astype(BF16) for r in raised]
    contexts = [upright(dot(item[2], w, ROWS).astype(BF16)) for w, item in zip(weights, items)]
    return list(zip(weights, contexts))


def attend_back(items):
    stacked = [two_heads(item[4]) for item in items]
    dweights = [dot(item[2], s, LAST) for item, s in zip(items, stacked)]
    dvs = [dot(item[3], s, PLAIN).astype(BF16) for item, s in zip(items, stacked)]
    dscores = []
    for item, d in zip(items, dweights):
        probs = item[3].astype(F32)
        terms = probs * d
        dscores.append((terms - probs * jnp.sum(terms, axis=0, keepdims=True)).astype(BF16))
    dqs = [upright((dot(item[1], d, ROWS) * (1.0 / math.sqrt(HEAD_DIM))).astype(BF16)) for item, d in zip(items, dscores)]
    dks = [dot(d, two_heads(item[0]), PLAIN).astype(BF16) for item, d in zip(items, dscores)]
    return list(zip(dqs, dks, dvs))


def in_groups(pairs, size, body):
    for n in range(0, len(pairs), size):
        body(pairs[n : n + size])


def column(slot, h, g):
    return (slot, slice(None), pl.ds(pl.multiple_of(256 * g + LANES * h, LANES), LANES))


def back(rg, slots, weight, rows=None):
    half = weight.shape[1] // 2
    total = None
    for j, slot in enumerate(slots):
        for g in range(3):
            at = j * 384 + g * LANES
            w = jnp.concatenate([weight[:, at : at + LANES], weight[:, half + at : half + at + LANES]], axis=1)
            term = dot(rg[slot, :, 256 * g : 256 * g + 256], w, LAST)
            total = term if total is None else total + term
    return total


CHUNKS = (0, 3, 1, 4, 2, 5)


def layer_kernel(
    dec_input, memory, src_len, out_grad, self_qkv, self_out, cross_query, cross_kv, cross_out, ffn_in, ffn_out,
    norm_gain, norm_bias,
    o_layer, o_input, o_memory, units, norm_out,
    x_in, mem, og, w_qkv, w_self, w_query, w_kv, w_cross, w_in, w_out,
    normal, qkv, p_self, context, hidden1, qx, kv, p_cross, hidden2,
    active, acc, dthird,
    lt, rg, n_own, n_got, n_send, n_recv, load_sem, swap_send, swap_recv, out_sem, out_send, out_recv, *rest
):
    at = place()
    y = at["y"]
    red = Reducer(at, lt, rg, units, *rest)
    across = partner("y", at)

    loads = [
        pltpu.make_async_copy(src, dst, load_sem.at[n])
        for n, (src, dst) in enumerate(
            ((self_qkv, w_qkv), (self_out, w_self), (cross_kv, w_kv), (cross_query, w_query), (cross_out, w_cross))
        )
    ]
    for load in loads:
        load.start()

    def ffn_load(n):
        cols = slice(CHUNKS[n] * 512, CHUNKS[n] * 512 + 512)
        slot = n % 3
        return (
            pltpu.make_async_copy(ffn_in.at[:, cols], w_in.at[slot], load_sem.at[5 + slot]),
            pltpu.make_async_copy(ffn_out.at[cols, :], w_out.at[slot], load_sem.at[8 + slot]),
        )

    for n in range(3):
        for load in ffn_load(n):
            load.start()

    def own_rows(n, src, dst, rows):
        return [
            pltpu.make_async_copy(
                src.at[2 * y + e], dst.at[pl.ds(pl.multiple_of(2 * e * rows + y * rows, rows), rows), :], load_sem.at[11 + 2 * n + e]
            )
            for e in range(2)
        ]

    def swap(n, src, dst, rows):
        return [
            pltpu.make_async_remote_copy(
                src_ref=src.at[2 * (1 - y) + e],
                dst_ref=dst.at[pl.ds(pl.multiple_of(2 * e * rows + y * rows, rows), rows), :],
                send_sem=swap_send.at[n, e], recv_sem=swap_recv.at[n, e], device_id=across, device_id_type=MESH,
            )
            for e in range(2)
        ]

    moved = ((dec_input, x_in, 64), (memory, mem, 128), (out_grad, og, 64))
    owns = [own_rows(n, *m) for n, m in enumerate(moved)]
    swaps = [swap(n, *m) for n, m in enumerate(moved)]
    for own in owns:
        for copy in own:
            copy.start()
    greet(at)
    for copy in swaps[0]:
        copy.start()
    for copy in swaps[1]:
        copy.start()
    for copy in swaps[2]:
        copy.start()

    def own_here(n):
        for copy in owns[n]:
            copy.wait()

    def other_here(n, e):
        swaps[n][e].wait()

    scale = 1.0 / math.sqrt(HEAD_DIM)

    own_here(0)
    for e in range(2):
        other_here(0, e)
    norm_forward(lambda rows: x_in[rows, :].astype(F32), normal, norm_gain, norm_bias, 0)
    loads[0].wait()

    for n in range(9):
        out = jnp.dot(normal[...], w_qkv[:, 256 * n : 256 * n + 256], preferred_element_type=F32)
        out = (out * scale if n < 3 else out).astype(BF16)
        qkv[2 * n] = out[:, 0:LANES]
        qkv[2 * n + 1] = out[:, LANES:256]

    store_left(lt, 10, normal[...].T)

    def pair(e, p):
        return slice(e * 128, e * 128 + 128), slice(p * LANES, p * LANES + LANES)

    pairs = [(e, p) for p in range(6) for e in range(2)]

    def self_operands(e, p):
        rows, _ = pair(e, p)
        return qkv[p, rows, :], qkv[6 + p, rows, :], qkv[12 + p, rows, :]

    def self_forward(group):
        k_at = lax.broadcasted_iota(jnp.int32, (128, 256), 0)
        q_at = lax.broadcasted_iota(jnp.int32, (128, 256), 1) % 128
        results = attend([(*self_operands(e, p), q_at >= k_at) for e, p in group])
        for (e, p), (weights, values) in zip(group, results):
            p_self[6 * e + p] = weights
            context[pair(e, p)] = values

    in_groups(pairs, 4, self_forward)

    loads[1].wait()
    for n in range(3):
        cols = slice(256 * n, 256 * n + 256)
        hidden1[:, cols] = x_in[:, cols].astype(F32) + jnp.dot(context[...], w_self[:, cols], preferred_element_type=F32)
    store_left(lt, 9, context[...].T)
    norm_forward(lambda rows: hidden1[rows, :], normal, norm_gain, norm_bias, 1)

    loads[3].wait()
    for n in range(3):
        out = jnp.dot(normal[...], w_query[:, 256 * n : 256 * n + 256], preferred_element_type=F32)
        out = (out * scale).astype(BF16)
        qx[2 * n] = out[:, 0:LANES]
        qx[2 * n + 1] = out[:, LANES:256]
    store_left(lt, 8, normal[...].T)
    loads[2].wait()
    own_here(1)

    def project_kv(blocks):
        rows = [pl.ds(pl.multiple_of(at_, 128), 128) for at_ in blocks]
        source = jnp.concatenate([mem[r, :] for r in rows], axis=0)
        for n in range(6):
            out = jnp.dot(source, w_kv[:, 256 * n : 256 * n + 256], preferred_element_type=F32).astype(BF16)
            for k, r in enumerate(rows):
                kv[2 * n, r, :] = out[128 * k : 128 * k + 128, 0:LANES]
                kv[2 * n + 1, r, :] = out[128 * k : 128 * k + 128, LANES:256]

    project_kv([128 * y, 256 + 128 * y])

    def cross_operands(e, p):
        rows, keys = pair(e, p)[0], slice(e * 256, e * 256 + 256)
        return qx[p, rows, :], kv[p, keys, :], kv[6 + p, keys, :]

    def cross_forward(group):
        k_at = lax.broadcasted_iota(jnp.int32, (256, 256), 0)
        results = attend([(*cross_operands(e, p), k_at < src_len[2 * y + e]) for e, p in group])
        for (e, p), (weights, values) in zip(group, results):
            p_cross[6 * e + p] = weights
            context[pair(e, p)] = values

    for e in range(2):
        other_here(1, e)
        project_kv([256 * e + 128 * (1 - y)])
        cross_forward([(e, p) for p in range(6)])

    loads[4].wait()
    for n in range(3):
        cols = slice(256 * n, 256 * n + 256)
        hidden2[:, cols] = hidden1[:, cols] + jnp.dot(context[...], w_cross[:, cols], preferred_element_type=F32)
    norm_forward(lambda rows: hidden2[rows, :], normal, norm_gain, norm_bias, 2)

    store_left(lt, 4, normal[...].T)
    acc[...] = jnp.zeros_like(acc)
    dthird[...] = jnp.zeros_like(dthird)
    own_here(2)
    for e in range(2):
        other_here(2, e)

    def spread(slot, rows_of):
        for g in range(3):
            for h in range(2):
                lane = h * 384 + g * LANES
                rg[slot, :, 256 * g + LANES * h : 256 * g + LANES * h + LANES] = rows_of[:, lane : lane + LANES].astype(BF16)

    root = math.sqrt(2.0 / math.pi)

    def up_tile(tile):
        lane = 256 * (tile % 3) + LANES * (tile // 12)
        return (1 + (tile % 12) // 3, slice(None), slice(lane, lane + LANES))

    def feed_in(n, s):
        slot, cols = n % 3, slice(256 * s, 256 * s + 256)
        up = jnp.dot(normal[...], w_in[slot, :, cols], preferred_element_type=F32)
        return up, dot(og[...], w_out[slot, cols, :], LAST)

    def feed_bend(n, s, up, dact):
        square = up * up
        bend = jnp.tanh(up * (root + (root * 0.044715) * square))
        lift = 0.5 + 0.5 * bend
        active[n % 2, :, 256 * s : 256 * s + 256] = (up * lift).astype(BF16)
        slope = lift + (0.5 * up) * (1.0 - bend * bend) * (root + (3.0 * 0.044715 * root) * square)
        grad = (dact * slope).astype(BF16)
        for t in range(2):
            rg[up_tile(4 * CHUNKS[n] + 2 * s + t)] = grad[:, LANES * t : LANES * t + LANES]

    def feed_out(n, k):
        slot, cols = n % 3, slice(256 * k, 256 * k + 256)
        acc[:, cols] += jnp.dot(active[n % 2], w_out[slot, :, cols], preferred_element_type=F32)
        dup = jnp.concatenate([rg[up_tile(4 * CHUNKS[n] + t)] for t in range(4)], axis=1)
        dthird[:, cols] += dot(dup, w_in[slot, cols, :], LAST)

    def feed_left(n):
        flipped = active[n % 2].T
        at_ = 0
        while at_ < 512:
            feature = CHUNKS[n] * 512 + at_
            i, k, r = feature // 192, (feature % 192) // 48, feature % 48
            size = min(48 - r, 512 - at_)
            to = 48 * (i // 2) + r
            lt[k, i % 2, to : to + size, :] = flipped[at_ : at_ + size, :]
            at_ += size

    def feed(n):
        for load in ffn_load(n):
            load.wait()
        for s in range(2):
            up, dact = feed_in(n, s)
            if n:
                for k in ((0, 1), (2,))[s]:
                    feed_out(n - 1, k)
            feed_bend(n, s, up, dact)
        if n:
            feed_left(n - 1)
            if n < 4:
                for load in ffn_load(n + 2):
                    load.start()

    PIECES = (
        [(normal, o_layer, 64, e, r) for e in range(2) for r in (0, 32)]
        + [(mem, o_memory, 128, e, r) for e in range(2) for r in (0, 32, 64, 96)]
        + [(x_in, o_input, 64, e, r) for e in range(2) for r in (0, 32)]
    )

    def piece(n, leaving):
        buf, out, rows, e, r = PIECES[n]
        which = 1 - y if leaving else y
        src = buf.at[pl.ds(pl.multiple_of(2 * e * rows + which * rows + r, 32), 32), :]
        dst = out.at[2 * y + e, r : r + 32, :]
        if not leaving:
            return pltpu.make_async_copy(src, dst, out_sem.at[n])
        return pltpu.make_async_remote_copy(
            src_ref=src, dst_ref=dst, send_sem=out_send.at[n], recv_sem=out_recv.at[n], device_id=across, device_id_type=MESH
        )

    def send(n):
        piece(n, True).start()
        piece(n, False).start()

    feed(0)
    feed(1)
    red.first(0)
    feed(2)
    red.second(0)
    feed(3)
    red.first(1)
    feed(4)
    red.second(1)
    feed(5)
    for k in range(3):
        feed_out(5, k)
    feed_left(5)
    spread(0, og)

    sums = n_own.at[0]
    sums[...] = jnp.zeros(sums.shape, F32)
    dc = context

    def store_grad(rows, value):
        acc[rows, :] = value

    def store_input(rows, v):
        x_in[rows, :] = (acc[rows, :] + v).astype(BF16)

    def context_grad(slot, weight):
        for n in range(3):
            rows = slice(256 * n, 256 * n + 256)
            dc[:, rows] = back(rg, (slot,), weight.at[rows, :]).astype(BF16)

    def cross_backward(group):
        results = attend_back([(*cross_operands(e, p), p_cross[6 * e + p], dc[pair(e, p)]) for e, p in group])
        for (e, p), (dq, dk, dv) in zip(group, results):
            j, g = p // 3, p % 3
            rg[8, pair(e, p)[0], 256 * g + LANES * j : 256 * g + LANES * j + LANES] = dq
            rg[6 + 7 * e + j, :, 256 * g : 256 * g + LANES] = dk
            rg[6 + 7 * e + j, :, 256 * g + LANES : 256 * g + 256] = dv

    def self_backward(group):
        results = attend_back([(*self_operands(e, p), p_self[6 * e + p], dc[pair(e, p)]) for e, p in group])
        for (e, p), values in zip(group, results):
            for n, value in enumerate(values):
                tile = 6 * n + p
                lane = 256 * (tile % 3) + LANES * (tile // 9)
                rg[10 + (tile % 9) // 3, pair(e, p)[0], lane : lane + LANES] = value

    def memory_rows(e):
        for n in range(3):
            rows = slice(256 * n, 256 * n + 256)
            mem[256 * e : 256 * e + 256, rows] = back(rg, (6 + 7 * e, 7 + 7 * e), w_kv.at[rows, :]).astype(BF16)

    def back_rows(slots, weight):
        for n in range(3):
            rows = slice(256 * n, 256 * n + 256)
            dthird[:, rows] = back(rg, slots, weight.at[rows, :])

    def piece_3():
        normal[...] = (hidden2[...] + acc[...]).astype(BF16)
        norm_backward(
            lambda rows: hidden2[rows, :], lambda rows: dthird[rows, :],
            lambda rows, v: store_grad(rows, og[rows, :].astype(F32) + v), norm_gain, sums, 2,
        )
        spread(5, acc)

    def piece_4():
        store_left(lt, 5, context[...].T)
        context_grad(5, w_cross)

    def piece_5():
        in_groups(pairs[:6], 3, cross_backward)

    def piece_6():
        in_groups(pairs[6:], 3, cross_backward)
        store_left(lt, 6, mem[0:256, :].T)
        store_left(lt, 7, mem[256:512, :].T)
        memory_rows(0)

    def piece_7():
        memory_rows(1)
        back_rows((8,), w_query)

    def piece_8():
        norm_backward(
            lambda rows: hidden1[rows, :], lambda rows: dthird[rows, :],
            lambda rows, v: store_grad(rows, acc[rows, :] + v), norm_gain, sums, 1,
        )
        spread(9, acc)
        context_grad(9, w_self)

    def piece_9():
        in_groups(pairs[:6], 3, self_backward)

    def piece_10():
        in_groups(pairs[6:], 3, self_backward)

    def piece_11():
        back_rows((10, 11, 12), w_qkv)

    def piece_12():
        norm_backward(
            lambda rows: x_in[rows, :].astype(F32), lambda rows: dthird[rows, :], store_input, norm_gain, sums, 0
        )

    pieces = (piece_3, piece_4, piece_5, piece_6, piece_7, piece_8, piece_9, piece_10, piece_11, piece_12)

    def body(n, carry):
        red.tick(n, (1, 0, 2, 3))
        for k, run in enumerate(pieces):
            pl.when(n == 3 + k)(run)
        red.tick(n, (4, 5))
        for j in range(6):
            @pl.when(n == 12 + j)
            def _():
                norm_step(j, at, n_own, n_got, n_send, n_recv)

        for k in range(16):
            @pl.when(n == k + 3)
            def _():
                send(k)

        return carry

    lax.fori_loop(2, red.TICKS, body, 0)
    norm_out[...] = n_own[5]
    red.drain()
    for n in range(16):
        piece(n, True).wait()
        piece(n, False).wait()


def layer_call(args):
    anywhere = pl.BlockSpec(memory_space=pl.ANY)
    vmem = pl.BlockSpec(memory_space=pltpu.VMEM)
    rows = lambda width, kind=BF16: pltpu.VMEM((256, width), kind)
    return pl.pallas_call(
        layer_kernel,
        out_shape=(
            jax.ShapeDtypeStruct((4, 64, 768), BF16),
            jax.ShapeDtypeStruct((4, 64, 768), BF16),
            jax.ShapeDtypeStruct((4, 128, 768), BF16),
            jax.ShapeDtypeStruct((TRIPLES, 3, 48, 128), F32),
            jax.ShapeDtypeStruct((8, 768), F32),
        ),
        in_specs=[anywhere, anywhere, pl.BlockSpec(memory_space=pltpu.SMEM)] + [anywhere] * 8 + [vmem] * 2,
        out_specs=(anywhere, anywhere, anywhere, anywhere, vmem),
        scratch_shapes=[
            rows(768), pltpu.VMEM((512, 768), BF16), rows(768),
            pltpu.VMEM((768, 2304), BF16), pltpu.VMEM((768, 768), BF16), pltpu.VMEM((768, 768), BF16),
            pltpu.VMEM((768, 1536), BF16), pltpu.VMEM((768, 768), BF16),
            pltpu.VMEM((3, 768, 512), BF16), pltpu.VMEM((3, 512, 768), BF16),
            rows(768), pltpu.VMEM((18, 256, 128), BF16), pltpu.VMEM((12, 128, 256), BF16), rows(768),
            rows(768, F32), pltpu.VMEM((6, 256, 128), BF16), pltpu.VMEM((12, 512, 128), BF16),
            pltpu.VMEM((12, 256, 256), BF16), rows(768, F32),
            pltpu.VMEM((2, 256, 512), BF16), rows(768, F32), rows(768, F32),
            pltpu.VMEM((11, 2, 384, 256), BF16),
            pltpu.VMEM((15, 256, 768), BF16),
            pltpu.VMEM((6, 8, 768), F32),
            pltpu.VMEM((5, 8, 768), F32),
            pltpu.SemaphoreType.DMA((5,)),
            pltpu.SemaphoreType.DMA((5,)),
            pltpu.SemaphoreType.DMA((17,)),
            pltpu.SemaphoreType.DMA((3, 2)),
            pltpu.SemaphoreType.DMA((3, 2)),
            pltpu.SemaphoreType.DMA((16,)),
            pltpu.SemaphoreType.DMA((16,)),
            pltpu.SemaphoreType.DMA((16,)),
        ] + Reducer.SCRATCH,
        compiler_params=pltpu.CompilerParams(collective_id=0, has_side_effects=True, vmem_limit_bytes=61 << 20),
    )(*args)


WEIGHTS = ((13, 3), (12, 1), (11, 1), (9, 2), (8, 1), (0, 4))


def finish_kernel(layer, inputs, memories, units, norms, *refs):
    o_layer, o_input, o_memory = refs[0:3]
    o_weights, o_ffn_out, o_gain, o_bias = refs[3:9], refs[9], refs[10], refs[11]
    low_input, low_memory, high_input, high_memory, blocks = refs[12:17]
    w_bufs, ffn_buf, sem, out_sem, low_layer = refs[17:23], refs[23], refs[24], refs[25], refs[26]
    loads = [
        pltpu.make_async_copy(units, blocks, sem.at[0]),
        pltpu.make_async_copy(memories, low_memory, sem.at[1]),
        pltpu.make_async_copy(inputs, low_input, sem.at[2]),
        pltpu.make_async_copy(layer, low_layer, sem.at[3]),
    ]
    for load in loads:
        load.start()
    stores = []

    def store(src, dst):
        copy = pltpu.make_async_copy(src, dst, out_sem.at[len(stores)])
        copy.start()
        stores.append(copy)

    o_gain[...] = norms[0:3, :]
    o_bias[...] = norms[3:6, :]
    loads[0].wait()
    for (t, count), buf, out in zip(WEIGHTS, w_bufs, o_weights):
        for j in range(count):
            for g in range(3):
                buf[:, j * 384 + g * LANES : j * 384 + g * LANES + LANES] = blocks[t + j, g]
        store(buf, out)
    for k in range(4):
        for g in range(3):
            ffn_buf[48 * k : 48 * k + 48, g * LANES : g * LANES + LANES] = blocks[4 + k, g]
    store(ffn_buf, o_ffn_out)
    loads[1].wait()
    for e in range(4):
        high_memory[e] = low_memory[e].astype(F32)
        store(high_memory.at[e], o_memory.at[e])
    loads[2].wait()
    high_input[...] = low_input[...].astype(F32)
    store(high_input, o_input)
    loads[3].wait()
    store(low_layer, o_layer)
    for copy in stores:
        copy.wait()


def finish_call(layer, inputs, memories, units, norms):
    anywhere = pl.BlockSpec(memory_space=pl.ANY)
    vmem = pl.BlockSpec(memory_space=pltpu.VMEM)
    widths = [count * 384 for _, count in WEIGHTS]
    return pl.pallas_call(
        finish_kernel,
        out_shape=(
            jax.ShapeDtypeStruct(layer.shape, BF16),
            jax.ShapeDtypeStruct(inputs.shape, F32),
            jax.ShapeDtypeStruct(memories.shape, F32),
            *[jax.ShapeDtypeStruct((48, w), F32) for w in widths],
            jax.ShapeDtypeStruct((192, 384), F32),
            jax.ShapeDtypeStruct((3, 768), F32),
            jax.ShapeDtypeStruct((3, 768), F32),
        ),
        in_specs=[anywhere] * 4 + [vmem],
        out_specs=(anywhere,) * 10 + (vmem, vmem),
        scratch_shapes=[
            pltpu.VMEM(inputs.shape, BF16), pltpu.VMEM(memories.shape, BF16),
            pltpu.VMEM(inputs.shape, F32), pltpu.VMEM(memories.shape, F32), pltpu.VMEM(units.shape, F32),
            *[pltpu.VMEM((48, w), F32) for w in widths], pltpu.VMEM((192, 384), F32),
            pltpu.SemaphoreType.DMA((4,)), pltpu.SemaphoreType.DMA((13,)), pltpu.VMEM(layer.shape, BF16),
        ],
        compiler_params=pltpu.CompilerParams(vmem_limit_bytes=60 << 20),
    )(layer, inputs, memories, units, norms)


def per_device_paired(*args):
    return finish_call(*layer_call(args))

def layer_norm(x, gain, shift):
    center = jnp.mean(x, axis=-1, keepdims=True)
    centered = x - center
    spread = jnp.mean(centered * centered, axis=-1, keepdims=True)
    return centered * lax.rsqrt(spread + 1e-05) * gain + shift


def smooth(v):
    return jax.nn.gelu(v, approximate=True)


def project(rows, weight):
    return jnp.einsum("etd,df->etf", rows, weight, preferred_element_type=jnp.float32)


def project_back(grads, weight):
    return jnp.einsum("etf,df->etd", grads, weight, preferred_element_type=jnp.float32)


def outer(rows, grads):
    return jnp.einsum("etd,etf->df", rows, grads, preferred_element_type=jnp.float32)


def outer_full(rows, grads):
    return jnp.einsum(
        "etd,etf->df", rows.astype(jnp.float32), grads, precision=lax.Precision.HIGHEST
    )


def back_full(grads, weight):
    return jnp.einsum(
        "etf,df->etd", grads, weight.astype(jnp.float32), precision=lax.Precision.HIGHEST
    )


def split_heads(queries, key_values):
    examples, rows, width = queries.shape
    count = key_values.shape[1]
    heads_q = queries.reshape(examples, rows, HEADS, HEAD_DIM)
    heads_k = key_values[:, :, :width].reshape(examples, count, HEADS, HEAD_DIM)
    heads_v = key_values[:, :, width:].reshape(examples, count, HEADS, HEAD_DIM)
    return (heads_q, heads_k, heads_v)


def masked_logits(heads_q, heads_k, allowed):
    scores = jnp.einsum("eqhd,ekhd->ehqk", heads_q, heads_k, preferred_element_type=jnp.float32)
    return jnp.where(allowed, scores * (1.0 / math.sqrt(HEAD_DIM)), -1e30)


def attend_forward(queries, key_values, allowed):
    examples, rows, width = queries.shape
    heads_q, heads_k, heads_v = split_heads(queries, key_values)
    logits = masked_logits(heads_q, heads_k, allowed)
    row_top = jnp.max(logits, axis=-1, keepdims=True)
    raised = jnp.where(allowed, jnp.exp(logits - row_top), 0.0)
    row_total = jnp.sum(raised, axis=-1, keepdims=True)
    weights = (raised / row_total).astype(jnp.bfloat16)
    context = jnp.einsum("ehqk,ekhd->eqhd", weights, heads_v, preferred_element_type=jnp.float32)
    return (
        context.reshape(examples, rows, width).astype(jnp.bfloat16),
        row_top + jnp.log(row_total),
    )


def attend_backward(queries, key_values, allowed, log_total, grad_context):
    examples, rows, width = queries.shape
    count = key_values.shape[1]
    heads_q, heads_k, heads_v = split_heads(queries, key_values)
    logits = masked_logits(heads_q, heads_k, allowed)
    soft = jnp.where(allowed, jnp.exp(logits - log_total), 0.0)
    grad_heads = grad_context.reshape(examples, rows, HEADS, HEAD_DIM)
    grad_soft = jnp.einsum(
        "eqhd,ekhd->ehqk", grad_heads, heads_v, preferred_element_type=jnp.float32
    )
    grad_values = jnp.einsum(
        "ehqk,eqhd->ekhd", soft.astype(jnp.bfloat16), grad_heads, preferred_element_type=jnp.float32
    )
    inner = jnp.sum(soft * grad_soft, axis=-1, keepdims=True)
    grad_scores = (soft * (grad_soft - inner) * (1.0 / math.sqrt(HEAD_DIM))).astype(jnp.bfloat16)
    grad_queries = jnp.einsum(
        "ehqk,ekhd->eqhd", grad_scores, heads_k, preferred_element_type=jnp.float32
    )
    grad_keys = jnp.einsum(
        "ehqk,eqhd->ekhd", grad_scores, heads_q, preferred_element_type=jnp.float32
    )
    joined = jnp.concatenate(
        [grad_keys.reshape(examples, count, width), grad_values.reshape(examples, count, width)],
        axis=2,
    )
    return (grad_queries.reshape(examples, rows, width), joined)


def per_device_wide(
    dec_input,
    memory,
    src_len,
    out_grad,
    self_qkv,
    self_out,
    cross_query,
    cross_kv,
    cross_out,
    ffn_in,
    ffn_out,
    norm_gain,
    norm_bias,
):
    examples, local_rows, width = dec_input.shape
    local_sources = memory.shape[1]
    seq_count = lax.axis_size("seq")
    all_targets = local_rows * seq_count
    all_sources = local_sources * seq_count
    rank = lax.axis_index("seq")
    x = dec_input.astype(jnp.float32)
    first_f, pull_first = jax.vjp(layer_norm, x, norm_gain[0], norm_bias[0])
    first = first_f.astype(jnp.bfloat16)
    projected = project(first, self_qkv).astype(jnp.bfloat16)
    self_queries = projected[:, :, :width]
    self_kv = lax.all_gather(projected[:, :, width:], "seq", axis=1, tiled=True)
    query_place = rank * local_rows + jnp.arange(local_rows, dtype=jnp.int32)
    key_place = jnp.arange(all_targets, dtype=jnp.int32)
    causal = (query_place[:, None] >= key_place[None, :])[None, None]
    self_context, self_total = attend_forward(self_queries, self_kv, causal)
    hidden1 = x + project(self_context, self_out)
    second_f, pull_second = jax.vjp(layer_norm, hidden1, norm_gain[1], norm_bias[1])
    second = second_f.astype(jnp.bfloat16)
    cross_queries = project(second, cross_query).astype(jnp.bfloat16)
    gathered = lax.all_gather(memory, "seq", axis=1, tiled=True)
    memory_kv = project(gathered, cross_kv).astype(jnp.bfloat16)
    source_place = jnp.arange(all_sources, dtype=jnp.int32)
    visible = (source_place[None, :] < src_len[:, None])[:, None, None, :]
    cross_context, cross_total = attend_forward(cross_queries, memory_kv, visible)
    hidden2 = hidden1 + project(cross_context, cross_out)
    third_f, pull_third = jax.vjp(layer_norm, hidden2, norm_gain[2], norm_bias[2])
    third = third_f.astype(jnp.bfloat16)
    raised_up = project(third, ffn_in)
    active_f, pull_smooth = jax.vjp(smooth, raised_up)
    activated = active_f.astype(jnp.bfloat16)
    layer_out = (hidden2 + project(activated, ffn_out)).astype(jnp.bfloat16)
    grad_out = out_grad.astype(jnp.float32)
    ffn_out_grad = outer(activated, out_grad)
    (grad_up,) = pull_smooth(project_back(out_grad, ffn_out))
    grad_up_low = grad_up.astype(jnp.bfloat16)
    ffn_in_grad = outer(third, grad_up_low)
    back_third, gain_third, bias_third = pull_third(project_back(grad_up_low, ffn_in))
    grad_hidden2 = grad_out + back_third
    cross_branch = grad_hidden2.astype(jnp.bfloat16)
    cross_out_grad = outer(cross_context, cross_branch)
    grad_cross_context = project_back(cross_branch, cross_out).astype(jnp.bfloat16)
    grad_cross_q, grad_memory_kv = attend_backward(
        cross_queries, memory_kv, visible, cross_total, grad_cross_context
    )
    local_kv_grad = lax.psum_scatter(
        grad_memory_kv.astype(jnp.bfloat16), "seq", scatter_dimension=1, tiled=True
    ).astype(jnp.float32)
    cross_kv_grad = outer_full(memory, local_kv_grad)
    memory_grad = back_full(local_kv_grad, cross_kv)
    grad_cross_low = grad_cross_q.astype(jnp.bfloat16)
    cross_query_grad = outer(second, grad_cross_low)
    back_second, gain_second, bias_second = pull_second(project_back(grad_cross_low, cross_query))
    grad_hidden1 = grad_hidden2 + back_second
    self_branch = grad_hidden1.astype(jnp.bfloat16)
    self_out_grad = outer(self_context, self_branch)
    grad_self_context = project_back(self_branch, self_out).astype(jnp.bfloat16)
    grad_self_q, grad_self_kv = attend_backward(
        self_queries, self_kv, causal, self_total, grad_self_context
    )
    local_self_kv = lax.psum_scatter(grad_self_kv, "seq", scatter_dimension=1, tiled=True)
    grad_projected = jnp.concatenate([grad_self_q, local_self_kv], axis=2).astype(jnp.bfloat16)
    self_qkv_grad = outer(first, grad_projected)
    back_first, gain_first, bias_first = pull_first(project_back(grad_projected, self_qkv))
    input_grad = grad_hidden1 + back_first
    gain_terms = jnp.stack([gain_first, gain_second, gain_third])
    bias_terms = jnp.stack([bias_first, bias_second, bias_third])
    gain_total, bias_total = lax.psum((gain_terms, bias_terms), ("dp", "seq"))
    partial_value = (
        lax.psum_scatter(
            self_qkv_grad.astype(jnp.bfloat16), "dp", scatter_dimension=0, tiled=True
        ).astype(jnp.float32),
        lax.psum_scatter(
            self_out_grad.astype(jnp.bfloat16), "dp", scatter_dimension=0, tiled=True
        ).astype(jnp.float32),
        lax.psum_scatter(
            cross_query_grad.astype(jnp.bfloat16), "dp", scatter_dimension=0, tiled=True
        ).astype(jnp.float32),
        lax.psum_scatter(
            cross_kv_grad.astype(jnp.bfloat16), "dp", scatter_dimension=0, tiled=True
        ).astype(jnp.float32),
        lax.psum_scatter(
            cross_out_grad.astype(jnp.bfloat16), "dp", scatter_dimension=0, tiled=True
        ).astype(jnp.float32),
        lax.psum_scatter(
            ffn_in_grad.astype(jnp.bfloat16), "dp", scatter_dimension=0, tiled=True
        ).astype(jnp.float32),
        lax.psum_scatter(
            ffn_out_grad.astype(jnp.bfloat16), "dp", scatter_dimension=0, tiled=True
        ).astype(jnp.float32),
    )
    finished = (
        lax.psum_scatter(
            partial_value[0].astype(jnp.bfloat16), "seq", scatter_dimension=1, tiled=True
        ).astype(jnp.float32),
        lax.psum_scatter(
            partial_value[1].astype(jnp.bfloat16), "seq", scatter_dimension=1, tiled=True
        ).astype(jnp.float32),
        lax.psum_scatter(
            partial_value[2].astype(jnp.bfloat16), "seq", scatter_dimension=1, tiled=True
        ).astype(jnp.float32),
        lax.psum_scatter(
            partial_value[3].astype(jnp.bfloat16), "seq", scatter_dimension=1, tiled=True
        ).astype(jnp.float32),
        lax.psum_scatter(
            partial_value[4].astype(jnp.bfloat16), "seq", scatter_dimension=1, tiled=True
        ).astype(jnp.float32),
        lax.psum_scatter(
            partial_value[5].astype(jnp.bfloat16), "seq", scatter_dimension=1, tiled=True
        ).astype(jnp.float32),
        lax.psum_scatter(
            partial_value[6].astype(jnp.bfloat16), "seq", scatter_dimension=1, tiled=True
        ).astype(jnp.float32),
    )
    return (
        layer_out,
        input_grad,
        memory_grad,
        finished[0],
        finished[1],
        finished[2],
        finished[3],
        finished[4],
        finished[5],
        finished[6],
        gain_total,
        bias_total,
    )


def solution(mesh):
    paired = mesh.shape["dp"] == 16 and mesh.shape["seq"] == 2
    per_device = per_device_paired if paired else per_device_wide
    in_specs = (
        P("dp", "seq", None),
        P("dp", "seq", None),
        P("dp"),
        P("dp", "seq", None),
        P(),
        P(),
        P(),
        P(),
        P(),
        P(),
        P(),
        P(),
        P(),
    )
    out_specs = (
        P("dp", "seq", None),
        P("dp", "seq", None),
        P("dp", "seq", None),
        P("dp", "seq"),
        P("dp", "seq"),
        P("dp", "seq"),
        P("dp", "seq"),
        P("dp", "seq"),
        P("dp", "seq"),
        P("dp", "seq"),
        P(),
        P(),
    )
    return jax.shard_map(
        per_device, mesh=mesh, in_specs=in_specs, out_specs=out_specs, check_vma=False
    )
```
